128 devices in a mesh: leaf: 128 (over z, x, y, core).
Axes of the slice: x: 4, y: 4, z: 4, core: 2. Of those that a mesh axis runs over, the one named last changes fastest.
Arguments:
- vectors: float32 [524288, 384], P('leaf'), may hold values from -6 to 6
- slot_frame: int32 [524288], P('leaf'), may hold values from 0 to 4095, as said below
- leaf_sizes: int32 [128, 8], P('leaf'), may hold values from 1 to 512, 3072 in all within a row
- near_field: float32 [1024, 512, 512], P('leaf'), may hold values from -0.25 to 0.25
- leaf_basis: float32 [1024, 512, 128], P('leaf'), may hold values from -0.25 to 0.25
- local_transfer: float32 [128, 15, 128, 128], P('leaf'), may hold values from -0.375 to 0.375
- local_coupling: float32 [128, 7, 128, 128], P('leaf'), may hold values from -1 to 1
- upper_transfer: float32 [128, 5, 128, 128], P('leaf'), as said below
- pair_coupling: float32 [128, 7, 128, 128], P('leaf'), as said below
Outputs:
- products: float32 [524288, 384], P('leaf')
- curvature: float32 [384], replicated
The draws below stay inside these ranges and needn't reach their ends.
Inputs may be any that keep to these rules, and one draw needn't show every extreme that they name: `slot_frame`: each device's block of 4096 entries is a permutation of 0 to 4095. `leaf_sizes`: each device's 8 sizes sum to 3072. `upper_transfer`: at group level j (entry j - 1) all devices under the same node of 2^j device subtrees hold the same matrix. `pair_coupling`: at group level j (entry j) all 2^(j + 1) devices under the same parent of the pair hold the same matrix.
All inputs are finite; a program needn't handle non-finite values.
Results may differ from the reference program's by a relative error of at most 0.0003.
Values sent between devices are 32-bit elements; how exact they have to be, the bound alone decides.
No kernel may reach another device: no remote copies, remote signals or barrier semaphores. Data moves between devices by JAX's collectives and lax.ppermute only.
A program may use at most 128 MiB of HBM per device.

```python
import math
import jax
import jax.numpy as jnp
import numpy as np
from jax import lax

LEAF = 512
R = 128
LEAVES_DEV = 8
SUBTREES = 128
XLEV = 7
NLEAVES = 1024
FRAMES = 524288
VECS = 384


def grouped_matrices(key, groups, copies, spread, flat_law):
    if flat_law:
        base = jax.random.uniform(key, (groups, R, R), jnp.float32, -1.0, 1.0) * (spread * math.sqrt(3.0))
    else:
        base = jax.random.normal(key, (groups, R, R), jnp.float32) * spread
    return jnp.repeat(base, copies, axis=0)


def draw_upper_transfer(key, part):
    flat_law = False
    blocks_list = []
    for height in range(1, XLEV - 1):
        blocks_list.append(grouped_matrices(jax.random.fold_in(key, height), SUBTREES // 2 ** height, 2 ** height, (2.0 * R) ** (-0.5), flat_law))
    return jnp.stack(blocks_list, axis=1)


def draw_pair_coupling(key, part):
    flat_law = False
    blocks_list = []
    for height in range(XLEV):
        blocks_list.append(grouped_matrices(jax.random.fold_in(key, 100 + height), SUBTREES // 2 ** (height + 1), 2 ** (height + 1), 2.0 * R ** (-0.5), flat_law))
    return jnp.stack(blocks_list, axis=1)


def draw_slot_frame(key, part):
    keys_all = jax.random.split(key, SUBTREES)

    def one_device(device_key):
        return jax.random.permutation(device_key, LEAVES_DEV * LEAF)
    orders = jax.vmap(one_device)(keys_all)
    return orders.reshape(-1).astype(jnp.int32)


def level_of(stream_key, shape, cuts, smallest, largest):
    level = 1.0
    for position, blocks in cuts:
        heights = jax.random.uniform(jax.random.fold_in(jax.random.fold_in(stream_key, 6), position), (blocks,), jnp.float32, smallest / len(cuts), largest / len(cuts))
        level = level * jnp.repeat(jnp.exp(heights), shape[position] // blocks).reshape((-1,) + (1,) * (len(shape) - 1 - position))
    return level


def profile(amount, total, reach, slope):
    portions = [(1 << 20) // math.isqrt(rank ** slope) + 1 for rank in range(2, amount + 1)]
    spare, holding = total - reach - (amount - 1), [1] * (amount - 1)
    while spare > 0:
        movable = [i for i in range(amount - 1) if holding[i] < reach]
        pool, remaining = sum([portions[i] for i in movable]), spare
        for i in movable:
            addition = min(reach - holding[i], max(1, remaining * portions[i] // pool), spare)
            holding[i] = holding[i] + addition
            spare = spare - addition
    return np.array([reach] + holding)


def uneven_parts(stream_key, amount, total, bound, lean):
    if amount == 2:
        one = jax.random.randint(stream_key, (), max(1, total - bound), min(bound, total - 1) + 1)
        return jnp.stack([one, total - one])
    lengths = jnp.asarray(profile(amount, total, bound, lean), jnp.int32)
    couples = (amount - 1) // 2
    giver, sink = lengths[1:1 + 2 * couples:2], lengths[2:2 + 2 * couples:2]
    room = jnp.minimum(giver - 1, bound - sink)
    passed = jax.random.randint(jax.random.fold_in(stream_key, 1), (couples,), 0, 1 << 20) % (room + 1)
    lengths = lengths.at[1:1 + 2 * couples:2].set(giver - passed).at[2:2 + 2 * couples:2].set(sink + passed)
    return lengths[jax.random.permutation(jax.random.fold_in(stream_key, 2), amount)]


def gaussian(key, shape, scale, reach, cuts=(), kind=jnp.bfloat16):
    level = level_of(key, shape, cuts, -0.22, 0.18) if cuts else 1.0
    drawn = jax.random.normal(key, shape, jnp.float32) * scale * level
    return jnp.minimum(jnp.maximum(drawn, -reach), reach).astype(kind)


def setup_inputs(seed: int = 0) -> dict:
    seeds = jax.random.split(jax.random.key(seed), 10)
    vectors = gaussian(seeds[0], (FRAMES, VECS), 1.0, 6.0, ((0, 128),), jnp.float32)
    slot_frame = draw_slot_frame(jax.random.fold_in(seeds[9], 71), 0)
    leaf_sizes = jax.vmap(lambda own: uneven_parts(own, LEAVES_DEV, 3 * LEAVES_DEV * LEAF // 4, LEAF, 2))(jax.random.split(seeds[2], SUBTREES)).reshape((SUBTREES, LEAVES_DEV)).astype(jnp.int32)
    near_field = gaussian(seeds[3], (NLEAVES, LEAF, LEAF), LEAF ** -0.5, 0.25, ((0, 128),), jnp.float32)
    leaf_basis = gaussian(seeds[4], (NLEAVES, LEAF, R), LEAF ** -0.5, 0.25, ((0, 128),), jnp.float32)
    local_transfer = gaussian(seeds[5], (SUBTREES, 2 * LEAVES_DEV - 1, R, R), (2 * R) ** -0.5, 0.375, ((0, 128),), jnp.float32)
    local_coupling = gaussian(seeds[6], (SUBTREES, LEAVES_DEV - 1, R, R), (R // 4) ** -0.5, 1.0, ((0, 128),), jnp.float32)
    upper_transfer = draw_upper_transfer(jax.random.fold_in(seeds[9], 71), 0)
    pair_coupling = draw_pair_coupling(jax.random.fold_in(seeds[9], 71), 0)
    return dict(vectors=vectors, slot_frame=slot_frame, leaf_sizes=leaf_sizes, near_field=near_field, leaf_basis=leaf_basis, local_transfer=local_transfer, local_coupling=local_coupling, upper_transfer=upper_transfer, pair_coupling=pair_coupling)


HIGH = lax.Precision.HIGHEST


def upward(leaf_basis, transfer, masked):
    coeffs = jnp.einsum("lir,liv->lrv", leaf_basis, masked, precision=HIGH)
    stacked = [coeffs]
    offset = 0
    number = leaf_basis.shape[0]
    while number > 1:
        matrices = transfer[offset:offset + number]
        lifted = jnp.einsum("nrs,nrv->nsv", matrices, stacked[-1], precision=HIGH)
        stacked.append(lifted[0::2] + lifted[1::2])
        offset = offset + number
        number = number // 2
    return stacked


def downward(stacked, top_incoming, transfer, coupling):
    fields_all = []
    starts = []
    offset_pairs = 0
    offset = 0
    for height in range(len(stacked) - 1):
        coeffs = stacked[height]
        number = coeffs.shape[0]
        starts.append(offset)
        offset = offset + number
        matrices = coupling[offset_pairs:offset_pairs + number // 2]
        from_right = jnp.einsum("prs,psv->prv", matrices, coeffs[1::2], precision=HIGH)
        from_left = jnp.einsum("psr,psv->prv", matrices, coeffs[0::2], precision=HIGH)
        fields_all.append(jnp.stack([from_right, from_left], axis=1).reshape(coeffs.shape))
        offset_pairs = offset_pairs + number // 2
    incoming = top_incoming[None]
    for height in reversed(range(len(stacked) - 1)):
        number = stacked[height].shape[0]
        matrices = transfer[starts[height]:starts[height] + number]
        incoming = fields_all[height] + jnp.einsum("nrs,nsv->nrv", matrices, jnp.repeat(incoming, 2, axis=0), precision=HIGH)
    return incoming


def prepare(vector_rows, slot_rows, sizes_row):
    tree_rows = jnp.take(vector_rows, slot_rows, axis=0).reshape(LEAVES_DEV, LEAF, VECS)
    is_valid = (jnp.arange(LEAF).astype(jnp.int32)[None, :] < sizes_row[:, None])[:, :, None]
    return jnp.where(is_valid, tree_rows, jnp.zeros_like(tree_rows)), is_valid


def reference(vectors, slot_frame, leaf_sizes, near_field, leaf_basis, local_transfer, local_coupling, upper_transfer, pair_coupling):
    frame_dev = LEAVES_DEV * LEAF
    vector_dev = vectors.reshape(SUBTREES, frame_dev, VECS)
    slot_dev = slot_frame.reshape(SUBTREES, frame_dev)
    near_dev = near_field.reshape(SUBTREES, LEAVES_DEV, LEAF, LEAF)
    basis_dev = leaf_basis.reshape(SUBTREES, LEAVES_DEV, LEAF, R)

    def root_of(pieces):
        vector_rows, slot_rows, sizes_row, basis_rows, transfer = pieces
        masked, is_valid = prepare(vector_rows, slot_rows, sizes_row)
        return upward(basis_rows, transfer, masked)[-1][0]

    current = lax.map(root_of, (vector_dev, slot_dev, leaf_sizes, basis_dev, local_transfer))
    fields_all = []
    lifts = []
    for height in range(XLEV):
        number = SUBTREES // (2 ** height)
        matrices = pair_coupling[::2 ** (height + 1), height]
        from_right = jnp.einsum("prs,psv->prv", matrices, current[1::2], precision=HIGH)
        from_left = jnp.einsum("psr,psv->prv", matrices, current[0::2], precision=HIGH)
        fields_all.append(jnp.stack([from_right, from_left], axis=1).reshape(number, R, VECS))
        if height < XLEV - 1:
            if height == 0:
                lift_mats = local_transfer[:, 2 * LEAVES_DEV - 2]
            else:
                lift_mats = upper_transfer[::2 ** height, height - 1]
            lifts.append(lift_mats)
            lifted = jnp.einsum("nrs,nrv->nsv", lift_mats, current, precision=HIGH)
            current = lifted[0::2] + lifted[1::2]
    incoming = fields_all[-1]
    for height in reversed(range(XLEV - 1)):
        incoming = fields_all[height] + jnp.einsum("nrs,nsv->nrv", lifts[height], jnp.repeat(incoming, 2, axis=0), precision=HIGH)

    def finish(pieces):
        vector_rows, slot_rows, sizes_row, near_rows, basis_rows, transfer, coupling, top_incoming = pieces
        masked, is_valid = prepare(vector_rows, slot_rows, sizes_row)
        stacked = upward(basis_rows, transfer, masked)
        leaf_incoming = downward(stacked, top_incoming, transfer, coupling)
        tree_out = jnp.einsum("lij,ljv->liv", near_rows, masked, precision=HIGH) + jnp.einsum("lir,lrv->liv", basis_rows, leaf_incoming, precision=HIGH)
        tree_out = jnp.where(is_valid, tree_out, jnp.zeros_like(tree_out)).reshape(frame_dev, VECS)
        return jnp.zeros_like(vector_rows).at[slot_rows].set(tree_out)

    products = lax.map(finish, (vector_dev, slot_dev, leaf_sizes, near_dev, basis_dev, local_transfer, local_coupling, incoming))
    products = products.reshape(FRAMES, VECS)
    curvature = jnp.sum(vectors * products, axis=0) / (2.0 * LEAF)
    return products, curvature
```

```python
import functools

import jax
import jax.numpy as jnp
from jax import lax
from jax.experimental import pallas as pl
from jax.experimental.pallas import tpu as pltpu
from jax.sharding import PartitionSpec as P

LEAF = 512
NL = 8
R = 128
V = 384
HALF = V // 2
QUART = HALF // 4
ROWS = NL * LEAF
S = 8
UN = 32
F32 = jnp.float32
BF16 = jnp.bfloat16
MIB = 1 << 20


def split(a):
    hi = a.astype(BF16)
    return hi, (a - hi.astype(F32)).astype(BF16)


def dot3s(terms, ca, cb):
    lhs, rhs = [], []
    for (ah, al), (bh, bl) in terms:
        lhs += [ah, ah, al]
        rhs += [bh, bl, bh]
    return lax.dot_general(
        jnp.concatenate(lhs, axis=ca),
        jnp.concatenate(rhs, axis=cb),
        (((ca,), (cb,)), ((), ())),
        preferred_element_type=F32,
    )


def dot3(a, b, ca=1, cb=0):
    return dot3s([(split(a), split(b))], ca, cb)


def tile_rows(start, count):
    return pl.ds(pl.multiple_of(start * S, S), count * S)


def rows_up_kernel(
    slot_hbm, sizes_hbm, v_hbm, basis_hbm, trans_hbm,
    xh_hbm, xl_hbm, call_ref, pay_ref,
    slot, sizes, vbuf, vt, xt, xh, xl, basis, trans, sem, vsem, osem,
):
    copies = [
        pltpu.make_async_copy(slot_hbm, slot, sem.at[0]),
        pltpu.make_async_copy(sizes_hbm, sizes, sem.at[1]),
        pltpu.make_async_copy(basis_hbm, basis, sem.at[2]),
        pltpu.make_async_copy(trans_hbm, trans, sem.at[3]),
    ]
    chunks = [
        pltpu.make_async_copy(
            v_hbm.at[pl.ds(c * LEAF, LEAF)], vbuf.at[pl.ds(c * LEAF, LEAF)], vsem.at[c]
        )
        for c in range(NL)
    ]
    copies[0].start()
    copies[1].start()
    for c in range(NL):
        chunks[c].start()
    copies[2].start()
    copies[3].start()
    for c in range(NL):
        chunks[c].wait()

        def spread(i, _, c=c):
            for u in range(4):
                base = pl.multiple_of(c * LEAF + i * 32 + u * 8, 8)
                for k in range(3):
                    vt[pl.ds(pl.multiple_of(base * S, 8) + k, 8, stride=S), :] = vbuf[
                        pl.ds(base, 8), 128 * k : 128 * k + 128
                    ]
            return 0

        lax.fori_loop(0, LEAF // 32, spread, 0)
    for c in copies:
        c.wait()
    outs = []
    coeffs = []
    for leaf in range(NL):
        size = sizes[0, leaf]

        def pick(i, _, leaf=leaf):
            base = pl.multiple_of(i * UN, UN)
            rows = [vt[tile_rows(slot[leaf * LEAF + base + r], 1), :] for r in range(UN)]
            for r in range(UN):
                xt[tile_rows(base + r, 1), :] = rows[r]
            return 0

        lax.fori_loop(0, (size + UN - 1) // UN, pick, 0)

        def pack(i, _, leaf=leaf, size=size):
            for u in range(2):
                base = pl.multiple_of(i * 32 + u * 16, 16)
                row = lax.broadcasted_iota(jnp.int32, (8, 128), 0) + base
                for k in range(3):
                    part = []
                    for half in range(2):
                        val = xt[pl.ds(pl.multiple_of((base + 8 * half) * S, 8) + k, 8, stride=S), :]
                        part.append(jnp.where(row + 8 * half < size, val, 0.0))
                    hi, lo = split(jnp.concatenate(part, axis=0))
                    xh[leaf, pl.ds(base, 16), 128 * k : 128 * k + 128] = hi
                    xl[leaf, pl.ds(base, 16), 128 * k : 128 * k + 128] = lo
            return 0

        lax.fori_loop(0, LEAF // 32, pack, 0)
        for n, (src, dst) in enumerate(((xh, xh_hbm), (xl, xl_hbm))):
            cp = pltpu.make_async_copy(src.at[leaf], dst.at[leaf], osem.at[2 * leaf + n])
            cp.start()
            outs.append(cp)
        c = dot3s([(split(basis[leaf]), (xh[leaf], xl[leaf]))], 0, 0)
        call_ref[leaf] = c
        coeffs.append(split(c))
    offset, at = 0, NL
    while len(coeffs) > 1:
        parents = []
        for m in range(len(coeffs) // 2):
            terms = [(split(trans[offset + 2 * m + t]), coeffs[2 * m + t]) for t in range(2)]
            c = dot3s(terms, 0, 0)
            parents.append(c)
            if len(coeffs) > 2:
                call_ref[at] = c
                at += 1
        offset += len(coeffs)
        coeffs = [split(c) for c in parents]
    pay_ref[0] = parents[0].T
    pay_ref[1] = dot3s([(coeffs[0], split(trans[2 * NL - 2]))], 0, 0)
    for cp in outs:
        cp.wait()


def rows_up(slot, sizes, vectors, basis, trans):
    hbm = pl.BlockSpec(memory_space=pl.ANY)
    vmem = pl.BlockSpec(memory_space=pltpu.VMEM)
    return pl.pallas_call(
        rows_up_kernel,
        out_shape=(
            jax.ShapeDtypeStruct((NL, LEAF, V), BF16),
            jax.ShapeDtypeStruct((NL, LEAF, V), BF16),
            jax.ShapeDtypeStruct((14, R, V), F32),
            jax.ShapeDtypeStruct((2, V, R), F32),
        ),
        in_specs=[hbm] * 5,
        out_specs=(hbm, hbm, vmem, vmem),
        scratch_shapes=[
            pltpu.SMEM((ROWS,), jnp.int32),
            pltpu.SMEM((1, NL), jnp.int32),
            pltpu.VMEM((ROWS, V), F32),
            pltpu.VMEM((ROWS * S, 128), F32),
            pltpu.VMEM((LEAF * S, 128), F32),
            pltpu.VMEM((NL, LEAF, V), BF16),
            pltpu.VMEM((NL, LEAF, V), BF16),
            pltpu.VMEM((NL, LEAF, R), F32),
            pltpu.VMEM((2 * NL - 1, R, R), F32),
            pltpu.SemaphoreType.DMA((4,)),
            pltpu.SemaphoreType.DMA((NL,)),
            pltpu.SemaphoreType.DMA((2 * NL,)),
        ],
        compiler_params=pltpu.CompilerParams(vmem_limit_bytes=48 * MIB),
        cost_estimate=pl.CostEstimate(flops=2 * 10**9, bytes_accessed=18 * 10**6, transcendentals=0),
        name="rows_up",
    )(slot, sizes, vectors, basis, trans)


def near_local_kernel(
    near_ref, xh_ref, xl_ref, basis_ref, call_ref, trans_ref, coup_ref,
    part_ref, eh_ref, el_ref, curv_ref, inc, tmat, near_h, near_l,
):
    leaf = pl.program_id(0)

    @pl.when(leaf == 0)
    def _():
        total = jnp.zeros((1, V), F32)
        starts = (0, 8, 12)
        fields = [None] * 14
        pair = 0
        for height in range(3):
            for m in range(4 >> height):
                a = starts[height] + 2 * m
                bm = split(coup_ref[pair])
                ca, cb = call_ref[a], call_ref[a + 1]
                fields[a] = dot3s([(bm, split(cb))], 1, 0)
                fields[a + 1] = dot3s([(bm, split(ca))], 0, 0)
                total += 2.0 * jnp.sum(ca * fields[a], axis=0, keepdims=True)
                pair += 1
        curv_ref[...] = jnp.broadcast_to(total, (8, V))
        top = [split(fields[12 + m]) for m in range(2)]
        tops = [split(trans_ref[12 + m]) for m in range(2)]
        for m in range(4):
            w = split(trans_ref[8 + m])
            mid = split(fields[8 + m] + dot3s([(w, top[m // 2])], 1, 0))
            tmid = split(dot3s([(w, tops[m // 2])], 1, 0))
            for n in (2 * m, 2 * m + 1):
                wl = split(trans_ref[n])
                inc[n] = fields[n] + dot3s([(wl, mid)], 1, 0)
                tmat[n] = dot3s([(wl, tmid)], 1, 0)

    nh, nlo = split(near_ref[0])
    near_h[...] = nh
    near_l[...] = nlo
    xh, xl = xh_ref[0], xl_ref[0]
    total = jnp.zeros((1, V), F32)
    base = split(basis_ref[0])
    g = split(inc[leaf])
    for blk in range(4):
        rows = slice(128 * blk, 128 * blk + 128)
        prod = dot3s([((near_h[rows, :], near_l[rows, :]), (xh, xl))], 1, 0)
        xb = xh[rows, :].astype(F32) + xl[rows, :].astype(F32)
        total += jnp.sum(prod * xb, axis=0, keepdims=True)
        part_ref[0, rows, :] = prod + dot3s(
            [((base[0][rows, :], base[1][rows, :]), g)], 1, 0
        )
    curv_ref[...] += jnp.broadcast_to(total, (8, V))
    e = dot3s([(base, split(tmat[leaf]))], 1, 0)
    eh, el = split(e)
    eh_ref[0] = eh
    el_ref[0] = el


def near_local(near, xh, xl, basis, call, trans, coup):
    def leafwise(*shape):
        return pl.BlockSpec((1,) + shape, lambda i: (i, 0, 0))

    def whole(*shape):
        return pl.BlockSpec(shape, lambda i: (0,) * len(shape))

    return pl.pallas_call(
        near_local_kernel,
        grid=(NL,),
        out_shape=(
            jax.ShapeDtypeStruct((NL, LEAF, V), F32),
            jax.ShapeDtypeStruct((NL, LEAF, R), BF16),
            jax.ShapeDtypeStruct((NL, LEAF, R), BF16),
            jax.ShapeDtypeStruct((8, V), F32),
        ),
        in_specs=[
            leafwise(LEAF, LEAF),
            leafwise(LEAF, V),
            leafwise(LEAF, V),
            leafwise(LEAF, R),
            whole(14, R, V),
            whole(2 * NL - 1, R, R),
            whole(NL - 1, R, R),
        ],
        out_specs=(leafwise(LEAF, V), leafwise(LEAF, R), leafwise(LEAF, R), whole(8, V)),
        scratch_shapes=[
            pltpu.VMEM((NL, R, V), F32),
            pltpu.VMEM((NL, R, R), F32),
            pltpu.VMEM((LEAF, LEAF), BF16),
            pltpu.VMEM((LEAF, LEAF), BF16),
        ],
        compiler_params=pltpu.CompilerParams(vmem_limit_bytes=40 * MIB),
        cost_estimate=pl.CostEstimate(flops=9 * 10**9, bytes_accessed=28 * 10**6, transcendentals=0),
        name="near_local",
    )(near, xh, xl, basis, call, trans, coup)


def chains_kernel(me, trans_ref, upper_ref, pair_ref, a1_ref, a2_ref, m0_ref, m1_ref, m3_ref):
    dev = me[0]

    def side(level):
        b = pair_ref[level]
        return jnp.where((dev >> level) % 2 == 0, b, b.T)

    m0_ref[0:R] = side(0).T
    m0_ref[R : 2 * R] = trans_ref[0].T
    w1 = upper_ref[0]
    w12 = dot3(w1, upper_ref[1])
    a1_ref[:, 0:R] = w1
    a1_ref[:, R : 2 * R] = w12
    m1_ref[0:R] = side(1).T
    m1_ref[R : 2 * R] = dot3(w1, side(2)).T
    m1_ref[2 * R : 3 * R] = w12.T
    w3 = upper_ref[2]
    w34 = dot3(w3, upper_ref[3])
    w345 = dot3(w34, upper_ref[4])
    a2_ref[:, 0:R] = w3
    a2_ref[:, R : 2 * R] = w34
    a2_ref[:, 2 * R : 3 * R] = w345
    m3_ref[0:R] = side(3).T
    m3_ref[R : 2 * R] = dot3(w3, side(4)).T
    m3_ref[2 * R : 3 * R] = dot3(w34, side(5)).T
    m3_ref[3 * R : 4 * R] = dot3(w345, side(6)).T


def after_core_kernel(me, pay_ref, got_ref, a1_ref, pair2_ref, lift3_ref):
    start = pl.multiple_of((me[0] % 2) * HALF, HALF)
    c1 = pay_ref[1, pl.ds(start, HALF), :] + got_ref[1, pl.ds(start, HALF), :]
    x = dot3(c1, a1_ref[...])
    pair2_ref[0] = c1
    pair2_ref[1] = x[:, 0:R]
    lift3_ref[...] = x[:, R : 2 * R]


def after_y_kernel(me, got_ref, a2_ref, send_ref, c3_ref):
    c3 = got_ref[0:QUART]
    for n in range(1, 4):
        c3 = c3 + got_ref[n * QUART : (n + 1) * QUART]
    c3_ref[...] = c3
    x = dot3(c3, a2_ref[...])
    parts = [c3, x[:, 0:R], x[:, R : 2 * R], x[:, 2 * R : 3 * R]]
    group = me[0] // 8
    for s in range(16):
        d = jnp.bitwise_xor(group, s)
        send_ref[s * QUART : (s + 1) * QUART] = jnp.where(
            d >= 8, parts[3], jnp.where(d >= 4, parts[2], jnp.where(d >= 2, parts[1], parts[0]))
        )


def after_top_kernel(me, got_ref, m3_ref, send_ref):
    group = me[0] // 8
    sums = [jnp.zeros((QUART, R), F32) for _ in range(4)]
    bounds = ((1, 2), (2, 4), (4, 8), (8, 16))
    for s in range(16):
        d = jnp.bitwise_xor(group, s)
        val = got_ref[s * QUART : (s + 1) * QUART]
        for j, (low, high) in enumerate(bounds):
            sums[j] += jnp.where(jnp.logical_and(d >= low, d < high), val, 0.0)
    inc3 = dot3(jnp.concatenate(sums, axis=1), m3_ref[...])
    for n in range(4):
        send_ref[n * QUART : (n + 1) * QUART] = inc3


def after_pair_kernel(pair2_ref, got_ref, c2_ref):
    c2_ref[...] = pair2_ref[1] + got_ref[1]


def to_core_kernel(got_ref, pair_got_ref, quad_got_ref, m1_ref, inc1_ref):
    sums = jnp.concatenate([pair_got_ref[0], quad_got_ref[...], got_ref[...]], axis=1)
    inc1_ref[...] = dot3(sums, m1_ref[...])


def curvature_kernel(
    me, pay_ref, got_ref, pair2_ref, pair_got_ref, c2_ref, quad_got_ref, c3_ref, inc3_ref,
    m0_ref, m1_ref, pair_ref, local_ref, send_ref, z,
):
    dev = me[0]
    z[...] = pay_ref[0] * dot3(got_ref[0], m0_ref[0:R])
    start = pl.multiple_of((dev % 2) * HALF, HALF)
    b2 = pair_ref[2]
    side2 = jnp.where((dev >> 2) % 2 == 0, b2, b2.T)
    field1 = dot3(pair_got_ref[0], m1_ref[0:R])
    field2 = dot3(quad_got_ref[...], side2, 1, 1)
    z[pl.ds(start, HALF), :] += pair2_ref[0] * field1 + 0.5 * (c2_ref[...] * field2)
    at = pl.multiple_of(start + ((dev // 2) % 4) * QUART, QUART)
    z[pl.ds(at, QUART), :] += c3_ref[...] * inc3_ref[0:QUART]
    zh, zl = split(z[...])
    ones = jnp.ones((8, R), BF16)
    total = lax.dot_general(
        jnp.concatenate([ones, ones], axis=1), jnp.concatenate([zh, zl], axis=1),
        (((1,), (1,)), ((), ())), preferred_element_type=F32,
    )
    total = total + local_ref[...]
    for n in range(16):
        send_ref[8 * n : 8 * n + 8] = total


def fold_kernel(count, repeat, scale, got_ref, send_ref):
    total = got_ref[0:8]
    for n in range(1, count):
        total = total + got_ref[8 * n : 8 * n + 8]
    total = total * scale
    for n in range(repeat):
        send_ref[8 * n : 8 * n + 8] = total


def small(body, outs, name, flops, scratch=()):
    vmem = pl.BlockSpec(memory_space=pltpu.VMEM)
    smem = pl.BlockSpec(memory_space=pltpu.SMEM)

    def call(*args):
        return pl.pallas_call(
            body,
            out_shape=tuple(jax.ShapeDtypeStruct(o, F32) for o in outs),
            in_specs=[smem if a.dtype == jnp.int32 else vmem for a in args],
            out_specs=tuple(vmem for _ in outs),
            scratch_shapes=list(scratch),
            compiler_params=pltpu.CompilerParams(vmem_limit_bytes=16 * MIB),
            cost_estimate=pl.CostEstimate(flops=flops, bytes_accessed=10**6, transcendentals=0),
            name=name,
        )(*args)

    return call


def rows_down_kernel(
    me, slot_hbm, sizes_hbm, part_hbm, eh_ref, el_ref, own_ref, other_ref, got_ref, m0_ref, out_hbm,
    slot, sizes, part, ot, pt, res, inct, sem, psem, osem,
):
    copies = [
        pltpu.make_async_copy(slot_hbm, slot, sem.at[0]),
        pltpu.make_async_copy(sizes_hbm, sizes, sem.at[1]),
    ]
    for c in copies:
        c.start()
    loads = [
        pltpu.make_async_copy(part_hbm.at[leaf], part.at[leaf], psem.at[leaf]) for leaf in range(NL)
    ]
    for c in loads:
        c.start()
    half = me[0] % 2
    inct[pl.ds(pl.multiple_of(half * HALF, HALF), HALF), :] = own_ref[...]
    inct[pl.ds(pl.multiple_of((1 - half) * HALF, HALF), HALF), :] = other_ref[...]
    root = dot3(jnp.concatenate([got_ref[0], inct[...]], axis=1), m0_ref[...])
    rh, rl = split(root.T)
    for c in copies:
        c.wait()
    zero = jnp.zeros((S, 128), F32)
    for leaf in range(NL):
        size = sizes[0, leaf]
        loads[leaf].wait()
        for blk in range(4):
            rows = slice(128 * blk, 128 * blk + 128)
            val = part[leaf, rows, :] + dot3s(
                [((eh_ref[leaf, rows, :], el_ref[leaf, rows, :]), (rh, rl))], 1, 0
            )
            row = lax.broadcasted_iota(jnp.int32, (128, V), 0) + 128 * blk
            val = jnp.where(row < size, val, 0.0)
            for b in range(16):
                for k in range(3):
                    ot[pl.ds((128 * blk + 8 * b) * S + k, 8, stride=S), :] = val[
                        8 * b : 8 * b + 8, 128 * k : 128 * k + 128
                    ]
        steps = (size + UN - 1) // UN

        def place(i, _, leaf=leaf):
            base = pl.multiple_of(i * UN, UN)
            rows = [ot[tile_rows(base + r, 1), :] for r in range(UN)]
            for r in range(UN):
                pt[tile_rows(slot[leaf * LEAF + base + r], 1), :] = rows[r]
            return 0

        lax.fori_loop(0, steps, place, 0)

        def blank(i, _, leaf=leaf):
            base = pl.multiple_of(i * UN, UN)
            for r in range(UN):
                pt[tile_rows(slot[leaf * LEAF + base + r], 1), :] = zero
            return 0

        lax.fori_loop(steps, LEAF // UN, blank, 0)
    stores = []
    for c in range(NL):

        def flat(i, _, c=c):
            for u in range(4):
                base = pl.multiple_of(c * LEAF + i * 32 + u * 8, 8)
                for k in range(3):
                    res[pl.ds(base, 8), 128 * k : 128 * k + 128] = pt[
                        pl.ds(pl.multiple_of(base * S, 8) + k, 8, stride=S), :
                    ]
            return 0

        lax.fori_loop(0, LEAF // 32, flat, 0)
        cp = pltpu.make_async_copy(
            res.at[pl.ds(c * LEAF, LEAF)], out_hbm.at[pl.ds(c * LEAF, LEAF)], osem.at[c]
        )
        cp.start()
        stores.append(cp)
    for cp in stores:
        cp.wait()


def rows_down(me, slot, sizes, part, eh, el, own, other, got, m0):
    hbm = pl.BlockSpec(memory_space=pl.ANY)
    vmem = pl.BlockSpec(memory_space=pltpu.VMEM)
    smem = pl.BlockSpec(memory_space=pltpu.SMEM)
    return pl.pallas_call(
        rows_down_kernel,
        out_shape=jax.ShapeDtypeStruct((ROWS, V), F32),
        in_specs=[smem, hbm, hbm, hbm] + [vmem] * 6,
        out_specs=hbm,
        scratch_shapes=[
            pltpu.SMEM((ROWS,), jnp.int32),
            pltpu.SMEM((1, NL), jnp.int32),
            pltpu.VMEM((NL, LEAF, V), F32),
            pltpu.VMEM((LEAF * S, 128), F32),
            pltpu.VMEM((ROWS * S, 128), F32),
            pltpu.VMEM((ROWS, V), F32),
            pltpu.VMEM((V, R), F32),
            pltpu.SemaphoreType.DMA((2,)),
            pltpu.SemaphoreType.DMA((NL,)),
            pltpu.SemaphoreType.DMA((NL,)),
        ],
        compiler_params=pltpu.CompilerParams(vmem_limit_bytes=48 * MIB),
        cost_estimate=pl.CostEstimate(flops=2 * 10**9, bytes_accessed=16 * 10**6, transcendentals=0),
        name="rows_down",
    )(me, slot, sizes, part, eh, el, own, other, got, m0)


def groups_of(bits, count):
    masks = [sum(1 << b for i, b in enumerate(bits) if k >> i & 1) for k in range(1 << len(bits))]
    full = masks[-1]
    return [[base | m for m in masks] for base in range(count) if base & full == 0]


def shards(
    vectors, slot_frame, leaf_sizes, near_field, leaf_basis,
    local_transfer, local_coupling, upper_transfer, pair_coupling,
):
    count = lax.axis_size("leaf")
    me = lax.axis_index("leaf").astype(jnp.int32).reshape(1)

    def swap(value, level):
        return lax.ppermute(value, "leaf", [(s, s ^ (1 << level)) for s in range(count)])

    def exchange(value, bits):
        return lax.all_to_all(
            value, "leaf", 0, 0, axis_index_groups=groups_of(bits, count), tiled=True
        )

    trans, coup, upper, pairs = (
        local_transfer[0], local_coupling[0], upper_transfer[0], pair_coupling[0],
    )
    a1, a2, m0, m1, m3 = small(
        chains_kernel, [(R, 2 * R), (R, 3 * R), (2 * R, R), (3 * R, R), (4 * R, R)], "chains", 10**8
    )(me, trans[2 * NL - 2 :], upper, pairs)
    xh, xl, call, pay = rows_up(slot_frame, leaf_sizes, vectors, leaf_basis, trans)
    core_got = swap(pay, 0)
    pair2, lift3 = small(after_core_kernel, [(2, HALF, R), (HALF, R)], "after_core", 10**8)(
        me, pay, core_got, a1
    )
    y_got = exchange(lift3, (1, 2))
    pair_got = swap(pair2, 1)
    top_send, c3 = small(after_y_kernel, [(16 * QUART, R), (QUART, R)], "after_y", 10**8)(
        me, y_got, a2
    )
    top_got = exchange(top_send, (3, 4, 5, 6))
    (c2,) = small(after_pair_kernel, [(HALF, R)], "after_pair", 10**6)(pair2, pair_got)
    quad_got = swap(c2, 2)
    part, eh, el, local = near_local(near_field, xh, xl, leaf_basis, call, trans, coup)
    (inc3,) = small(after_top_kernel, [(HALF, R)], "after_top", 10**8)(me, top_got, m3)
    inc3_got = exchange(inc3, (1, 2))
    (curv,) = small(curvature_kernel, [(128, V)], "curvature", 10**8, [pltpu.VMEM((V, R), F32)])(
        me, pay, core_got, pair2, pair_got, c2, quad_got, c3, inc3, m0, m1, pairs, local
    )
    curv = exchange(curv, (3, 4, 5, 6))
    (curv,) = small(functools.partial(fold_kernel, 16, 8, 1.0), [(64, V)], "fold_top", 10**5)(curv)
    curv = exchange(curv, (0, 1, 2))
    (curv,) = small(
        functools.partial(fold_kernel, 8, 1, 1.0 / (2.0 * LEAF)), [(8, V)], "fold_low", 10**5
    )(curv)
    (inc1,) = small(to_core_kernel, [(HALF, R)], "to_core", 10**8)(inc3_got, pair_got, quad_got, m1)
    inc1_got = swap(inc1, 0)
    products = rows_down(
        me, slot_frame, leaf_sizes, part, eh, el, inc1, inc1_got, core_got, m0
    )
    return products, curv[0]


def solution(mesh):
    return jax.shard_map(
        shards,
        mesh=mesh,
        in_specs=(
            P("leaf", None),
            P("leaf"),
            P("leaf", None),
            P("leaf", None, None),
            P("leaf", None, None),
            P("leaf", None, None, None),
            P("leaf", None, None, None),
            P("leaf", None, None, None),
            P("leaf", None, None, None),
        ),
        out_specs=(P("leaf", None), P()),
        check_vma=False,
    )
```

```python
import functools

import jax
import jax.numpy as jnp
from jax import lax
from jax.experimental import pallas as pl
from jax.experimental.pallas import tpu as pltpu
from jax.sharding import PartitionSpec as P

LEAF = 512
NL = 8
R = 128
V = 384
HALF = V // 2
QUART = HALF // 4
ROWS = NL * LEAF
S = 4
UN = 32
F32 = jnp.float32
BF16 = jnp.bfloat16
MIB = 1 << 20


def split(a):
    hi = a.astype(BF16)
    return hi, (a - hi.astype(F32)).astype(BF16)


def dot3s(terms, ca, cb):
    lhs, rhs = [], []
    for (ah, al), (bh, bl) in terms:
        lhs += [ah, ah, al]
        rhs += [bh, bl, bh]
    return lax.dot_general(
        jnp.concatenate(lhs, axis=ca),
        jnp.concatenate(rhs, axis=cb),
        (((ca,), (cb,)), ((), ())),
        preferred_element_type=F32,
    )


def dot3(a, b, ca=1, cb=0):
    return dot3s([(split(a), split(b))], ca, cb)


def tile_rows(start, count):
    return pl.ds(pl.multiple_of(start * S, S), count * S)


def far(x):
    return pltpu.with_memory_space_constraint(x, pltpu.HBM)


def lane_rows(p):
    parts = [p[0:1, 128 * k : 128 * k + 128] for k in range(3)]
    return jnp.concatenate(parts + [jnp.zeros((5, 128), F32)], axis=0)


def row_sums(z):
    zh, zl = split(z)
    ones = jnp.ones((8, 2 * R), BF16)
    return lax.dot_general(
        ones, jnp.concatenate([zh, zl], axis=1), (((1,), (1,)), ((), ())),
        preferred_element_type=F32,
    )


def rows_up_kernel(
    slot_hbm, sizes_hbm, v_hbm, basis_hbm, trans_hbm,
    xh_hbm, xl_hbm, call_hbm, pay_ref,
    slot, sizes, vbuf, vt, xt, basis, trans, xh, xl, call_ref, sem, vsem, osem,
):
    copies = [
        pltpu.make_async_copy(slot_hbm, slot, sem.at[0]),
        pltpu.make_async_copy(sizes_hbm, sizes, sem.at[1]),
        pltpu.make_async_copy(basis_hbm, basis, sem.at[2]),
        pltpu.make_async_copy(trans_hbm, trans, sem.at[3]),
    ]
    chunks = [
        pltpu.make_async_copy(
            v_hbm.at[pl.ds(c * LEAF, LEAF)], vbuf.at[pl.ds(c * LEAF, LEAF)], vsem.at[c]
        )
        for c in range(NL)
    ]
    copies[0].start()
    copies[1].start()
    for c in range(NL):
        chunks[c].start()
    copies[2].start()
    copies[3].start()
    for c in range(NL):
        chunks[c].wait()

        def spread(i, _, c=c):
            for u in range(4):
                base = pl.multiple_of(c * LEAF + i * 32 + u * 8, 8)
                for k in range(3):
                    vt[pl.ds(pl.multiple_of(base * S, 8) + k, 8, stride=S), :] = vbuf[
                        pl.ds(base, 8), 128 * k : 128 * k + 128
                    ]
            return 0

        lax.fori_loop(0, LEAF // 32, spread, 0)
    for c in copies:
        c.wait()
    outs = []
    coeffs = []
    for leaf in range(NL):
        size = sizes[0, leaf]

        def pick(i, _, leaf=leaf):
            base = pl.multiple_of(i * UN, UN)
            rows = [vt[tile_rows(slot[leaf * LEAF + base + r], 1), :] for r in range(UN)]
            for r in range(UN):
                xt[tile_rows(base + r, 1), :] = rows[r]
            return 0

        lax.fori_loop(0, (size + UN - 1) // UN, pick, 0)

        def pack(i, _, leaf=leaf, size=size):
            for u in range(8):
                base = pl.multiple_of(i * 128 + u * 16, 16)
                row = lax.broadcasted_iota(jnp.int32, (8, 128), 0) + base
                for k in range(3):
                    part = []
                    for half in range(2):
                        at = pl.multiple_of((base + 8 * half) * S, 8) + k
                        val = xt[pl.ds(at, 8, stride=S), :]
                        part.append(jnp.where(row + 8 * half < size, val, 0.0))
                    hi, lo = split(jnp.concatenate(part, axis=0))
                    xh[leaf, pl.ds(base, 16), 128 * k : 128 * k + 128] = hi
                    xl[leaf, pl.ds(base, 16), 128 * k : 128 * k + 128] = lo
            return 0

        lax.fori_loop(0, LEAF // 128, pack, 0)
        for n, (src, dst) in enumerate(((xh, xh_hbm), (xl, xl_hbm))):
            cp = pltpu.make_async_copy(src.at[leaf], dst.at[leaf], osem.at[2 * leaf + n])
            cp.start()
            outs.append(cp)
        c = dot3s([(split(basis[leaf]), (xh[leaf], xl[leaf]))], 0, 0)
        call_ref[leaf] = c
        coeffs.append(split(c))
    offset, at = 0, NL
    while len(coeffs) > 1:
        parents = []
        for m in range(len(coeffs) // 2):
            terms = [(split(trans[offset + 2 * m + t]), coeffs[2 * m + t]) for t in range(2)]
            c = dot3s(terms, 0, 0)
            parents.append(c)
            if len(coeffs) > 2:
                call_ref[at] = c
                at += 1
        offset += len(coeffs)
        coeffs = [split(c) for c in parents]
    cp = pltpu.make_async_copy(call_ref, call_hbm, osem.at[2 * NL])
    cp.start()
    outs.append(cp)
    pay_ref[0] = parents[0].T
    pay_ref[1] = dot3s([(coeffs[0], split(trans[2 * NL - 2]))], 0, 0)
    for cp in outs:
        cp.wait()


def rows_up(slot, sizes, vectors, basis, trans):
    hbm = pl.BlockSpec(memory_space=pltpu.HBM)
    vmem = pl.BlockSpec(memory_space=pltpu.VMEM)
    return pl.pallas_call(
        rows_up_kernel,
        out_shape=(
            pltpu.HBM((NL, LEAF, V), BF16),
            pltpu.HBM((NL, LEAF, V), BF16),
            pltpu.HBM((14, R, V), F32),
            jax.ShapeDtypeStruct((2, V, R), F32),
        ),
        in_specs=[hbm] * 5,
        out_specs=(hbm, hbm, hbm, vmem),
        scratch_shapes=[
            pltpu.SMEM((ROWS,), jnp.int32),
            pltpu.SMEM((1, NL), jnp.int32),
            pltpu.VMEM((ROWS, V), F32),
            pltpu.VMEM((ROWS * S, 128), F32),
            pltpu.VMEM((LEAF * S, 128), F32),
            pltpu.VMEM((NL, LEAF, R), F32),
            pltpu.VMEM((2 * NL - 1, R, R), F32),
            pltpu.VMEM((NL, LEAF, V), BF16),
            pltpu.VMEM((NL, LEAF, V), BF16),
            pltpu.VMEM((14, R, V), F32),
            pltpu.SemaphoreType.DMA((4,)),
            pltpu.SemaphoreType.DMA((NL,)),
            pltpu.SemaphoreType.DMA((2 * NL + 1,)),
        ],
        compiler_params=pltpu.CompilerParams(vmem_limit_bytes=32 * MIB),
        cost_estimate=pl.CostEstimate(flops=2 * 10**9, bytes_accessed=18 * 10**6, transcendentals=0),
        name="rows_up",
    )(far(slot), far(sizes), far(vectors), far(basis), far(trans))


def near_local_kernel(
    me, near_ref, xh_ref, xl_ref, call_hbm, trans_hbm, coup_hbm,
    pay_ref, got_ref, pair2_ref, pair_got_ref, c2_ref, m0_ref, m1_ref,
    part_ref, inc_ref, tmat_ref, curv_ref, near_h, near_l, call_ref, trans_ref, coup_ref, z, sem,
):
    leaf = pl.program_id(0)

    @pl.when(leaf == 0)
    def _():
        copies = [
            pltpu.make_async_copy(trans_hbm, trans_ref, sem.at[0]),
            pltpu.make_async_copy(coup_hbm, coup_ref, sem.at[1]),
            pltpu.make_async_copy(call_hbm, call_ref, sem.at[2]),
        ]
        for c in copies:
            c.start()
        z[...] = pay_ref[0] * dot3(got_ref[0], m0_ref[0:R])
        start = pl.multiple_of((me[0] % 2) * HALF, HALF)
        z[pl.ds(start, HALF), :] += pair2_ref[0] * dot3(pair_got_ref[0], m1_ref[0:R])
        for c in copies:
            c.wait()
        total = jnp.zeros((1, V), F32)
        starts = (0, 8, 12)
        fields = [None] * 14
        pair = 0
        for height in range(3):
            for m in range(4 >> height):
                a = starts[height] + 2 * m
                bm = split(coup_ref[pair])
                ca, cb = call_ref[a], call_ref[a + 1]
                fields[a] = dot3s([(bm, split(cb))], 1, 0)
                fields[a + 1] = dot3s([(bm, split(ca))], 0, 0)
                total += 2.0 * jnp.sum(ca * fields[a], axis=0, keepdims=True)
                pair += 1
        curv_ref[...] = row_sums(z[...]) + jnp.broadcast_to(total, (8, V))
        top = [split(fields[12 + m]) for m in range(2)]
        tops = [split(trans_ref[12 + m]) for m in range(2)]
        for m in range(4):
            w = split(trans_ref[8 + m])
            mid = split(fields[8 + m] + dot3s([(w, top[m // 2])], 1, 0))
            tmid = split(dot3s([(w, tops[m // 2])], 1, 0))
            for n in (2 * m, 2 * m + 1):
                wl = split(trans_ref[n])
                inc_ref[n] = fields[n] + dot3s([(wl, mid)], 1, 0)
                tmat_ref[n] = dot3s([(wl, tmid)], 1, 0)

    nh, nlo = split(near_ref[0])
    near_h[...] = nh
    near_l[...] = nlo
    xh, xl = xh_ref[0], xl_ref[0]
    total = jnp.zeros((1, V), F32)
    for blk in range(4):
        rows = slice(128 * blk, 128 * blk + 128)
        prod = dot3s([((near_h[rows, :], near_l[rows, :]), (xh, xl))], 1, 0)
        xb = xh[rows, :].astype(F32) + xl[rows, :].astype(F32)
        total += jnp.sum(prod * xb, axis=0, keepdims=True)
        part_ref[0, rows, :] = prod
    curv_ref[...] += jnp.broadcast_to(total, (8, V))


def near_local(me, near, xh, xl, call, trans, coup, *rest):
    def leafwise(width):
        return pl.BlockSpec((1, LEAF, width), lambda i: (i, 0, 0))

    vmem = pl.BlockSpec(memory_space=pltpu.VMEM)
    hbm = pl.BlockSpec(memory_space=pltpu.HBM)
    smem = pl.BlockSpec(memory_space=pltpu.SMEM)
    return pl.pallas_call(
        near_local_kernel,
        grid=(NL,),
        out_shape=(
            pltpu.HBM((NL, LEAF, V), F32),
            pltpu.HBM((NL, R, V), F32),
            pltpu.HBM((NL, R, R), F32),
            jax.ShapeDtypeStruct((8, V), F32),
        ),
        in_specs=[smem, leafwise(LEAF), leafwise(V), leafwise(V), hbm, hbm, hbm]
        + [vmem] * len(rest),
        out_specs=(leafwise(V), vmem, vmem, vmem),
        scratch_shapes=[
            pltpu.VMEM((LEAF, LEAF), BF16),
            pltpu.VMEM((LEAF, LEAF), BF16),
            pltpu.VMEM((14, R, V), F32),
            pltpu.VMEM((2 * NL - 1, R, R), F32),
            pltpu.VMEM((NL - 1, R, R), F32),
            pltpu.VMEM((V, R), F32),
            pltpu.SemaphoreType.DMA((3,)),
        ],
        compiler_params=pltpu.CompilerParams(vmem_limit_bytes=32 * MIB),
        cost_estimate=pl.CostEstimate(flops=7 * 10**9, bytes_accessed=10 * 10**6, transcendentals=0),
        name="near_local",
    )(me, far(near), far(xh), far(xl), far(call), far(trans), far(coup), *rest)


def chains_kernel(
    me, trans_hbm, upper_hbm, pair_hbm, a1_ref, a2_ref, m0_ref, m1_ref, m3_ref, side2_ref,
    trans_ref, upper_ref, pair_ref, sem,
):
    dev = me[0]
    copies = [
        pltpu.make_async_copy(trans_hbm.at[pl.ds(2 * NL - 2, 1)], trans_ref, sem.at[0]),
        pltpu.make_async_copy(upper_hbm, upper_ref, sem.at[1]),
        pltpu.make_async_copy(pair_hbm, pair_ref, sem.at[2]),
    ]
    for c in copies:
        c.start()
    for c in copies:
        c.wait()

    def side(level):
        b = pair_ref[level]
        return jnp.where((dev >> level) % 2 == 0, b, b.T)

    m0_ref[0:R] = side(0).T
    m0_ref[R : 2 * R] = trans_ref[0].T
    w1 = upper_ref[0]
    w12 = dot3(w1, upper_ref[1])
    a1_ref[:, 0:R] = w1
    a1_ref[:, R : 2 * R] = w12
    m1_ref[0:R] = side(1).T
    m1_ref[R : 2 * R] = dot3(w1, side(2)).T
    m1_ref[2 * R : 3 * R] = w12.T
    w3 = upper_ref[2]
    w34 = dot3(w3, upper_ref[3])
    w345 = dot3(w34, upper_ref[4])
    a2_ref[:, 0:R] = w3
    a2_ref[:, R : 2 * R] = w34
    a2_ref[:, 2 * R : 3 * R] = w345
    m3_ref[0:R] = side(3).T
    m3_ref[R : 2 * R] = dot3(w3, side(4)).T
    m3_ref[2 * R : 3 * R] = dot3(w34, side(5)).T
    m3_ref[3 * R : 4 * R] = dot3(w345, side(6)).T
    side2_ref[...] = side(2).T


def after_core_kernel(me, pay_ref, got_ref, a1_ref, pair2_ref, lift3_ref):
    start = pl.multiple_of((me[0] % 2) * HALF, HALF)
    c1 = pay_ref[1, pl.ds(start, HALF), :] + got_ref[1, pl.ds(start, HALF), :]
    x = dot3(c1, a1_ref[...])
    pair2_ref[0] = c1
    pair2_ref[1] = x[:, 0:R]
    lift3_ref[...] = x[:, R : 2 * R]


def after_y_kernel(me, got_ref, a2_ref, send_ref, c3_ref):
    c3 = got_ref[0:QUART]
    for n in range(1, 4):
        c3 = c3 + got_ref[n * QUART : (n + 1) * QUART]
    c3_ref[...] = c3
    x = dot3(c3, a2_ref[...])
    parts = [c3, x[:, 0:R], x[:, R : 2 * R], x[:, 2 * R : 3 * R]]
    group = me[0] // 8
    for s in range(16):
        d = jnp.bitwise_xor(group, s)
        send_ref[s * QUART : (s + 1) * QUART] = jnp.where(
            d >= 8, parts[3], jnp.where(d >= 4, parts[2], jnp.where(d >= 2, parts[1], parts[0]))
        )


def after_top_kernel(
    me, got_ref, m3_ref, side2_ref, c2_ref, quad_got_ref, c3_ref, local_ref, send_ref, z
):
    dev = me[0]
    group = dev // 8
    sums = [jnp.zeros((QUART, R), F32) for _ in range(4)]
    bounds = ((1, 2), (2, 4), (4, 8), (8, 16))
    for s in range(16):
        d = jnp.bitwise_xor(group, s)
        val = got_ref[s * QUART : (s + 1) * QUART]
        for j, (low, high) in enumerate(bounds):
            sums[j] += jnp.where(jnp.logical_and(d >= low, d < high), val, 0.0)
    inc3 = dot3(jnp.concatenate(sums, axis=1), m3_ref[...])
    z[...] = jnp.zeros((V, R), F32)
    start = pl.multiple_of((dev % 2) * HALF, HALF)
    z[pl.ds(start, HALF), :] = 0.5 * (c2_ref[...] * dot3(quad_got_ref[...], side2_ref[...]))
    at = pl.multiple_of(start + ((dev // 2) % 4) * QUART, QUART)
    z[pl.ds(at, QUART), :] += c3_ref[...] * inc3
    share = lane_rows(local_ref[...] + row_sums(z[...]))
    for n in range(4):
        send_ref[n, 0:QUART] = inc3
        send_ref[n, QUART : QUART + 8] = share


def after_pair_kernel(pair2_ref, got_ref, c2_ref):
    c2_ref[...] = pair2_ref[1] + got_ref[1]


def to_core_kernel(got_ref, pair_got_ref, quad_got_ref, m1_ref, out_ref):
    inc3 = jnp.concatenate([got_ref[n, 0:QUART] for n in range(4)], axis=0)
    sums = jnp.concatenate([pair_got_ref[0], quad_got_ref[...], inc3], axis=1)
    out_ref[0:HALF] = dot3(sums, m1_ref[...])
    share = got_ref[0, QUART : QUART + 8]
    for n in range(1, 4):
        share = share + got_ref[n, QUART : QUART + 8]
    out_ref[HALF : HALF + 8] = share


def core_share_kernel(own_ref, other_ref, send_ref):
    total = own_ref[HALF : HALF + 8] + other_ref[HALF : HALF + 8]
    for n in range(16):
        send_ref[n] = total


def all_share_kernel(got_ref, out_ref):
    total = got_ref[0]
    for n in range(1, 16):
        total = total + got_ref[n]
    out_ref[...] = total * (1.0 / (2.0 * LEAF))


def small(body, outs, name, flops, scratch=(), hbm_args=()):
    vmem = pl.BlockSpec(memory_space=pltpu.VMEM)
    smem = pl.BlockSpec(memory_space=pltpu.SMEM)
    hbm = pl.BlockSpec(memory_space=pltpu.HBM)

    def call(*args):
        return pl.pallas_call(
            body,
            out_shape=tuple(jax.ShapeDtypeStruct(o, F32) for o in outs),
            in_specs=[
                smem if a.dtype == jnp.int32 else (hbm if n in hbm_args else vmem)
                for n, a in enumerate(args)
            ],
            out_specs=tuple(vmem for _ in outs),
            scratch_shapes=list(scratch),
            compiler_params=pltpu.CompilerParams(vmem_limit_bytes=16 * MIB),
            cost_estimate=pl.CostEstimate(flops=flops, bytes_accessed=10**6, transcendentals=0),
            name=name,
        )(*args)

    return call


def rows_down_kernel(
    me, slot_hbm, sizes_hbm, basis_hbm, part_hbm, local_hbm, tmat_hbm,
    own_ref, other_ref, got_ref, m0_ref, out_hbm,
    slot, sizes, basis, part, local_ref, tmat_ref, ot, pt, res, inct, sem, psem, osem,
):
    copies = [
        pltpu.make_async_copy(slot_hbm, slot, sem.at[0]),
        pltpu.make_async_copy(sizes_hbm, sizes, sem.at[1]),
        pltpu.make_async_copy(tmat_hbm, tmat_ref, sem.at[2]),
        pltpu.make_async_copy(local_hbm, local_ref, sem.at[3]),
        pltpu.make_async_copy(basis_hbm, basis, sem.at[4]),
    ]
    for c in copies:
        c.start()
    loads = [
        pltpu.make_async_copy(part_hbm.at[leaf], part.at[leaf], psem.at[leaf]) for leaf in range(NL)
    ]
    for c in loads:
        c.start()
    half = me[0] % 2
    inct[pl.ds(pl.multiple_of(half * HALF, HALF), HALF), :] = own_ref[0:HALF]
    inct[pl.ds(pl.multiple_of((1 - half) * HALF, HALF), HALF), :] = other_ref[0:HALF]
    root = dot3(jnp.concatenate([got_ref[0], inct[...]], axis=1), m0_ref[...])
    rsplit = split(root.T)
    for c in copies:
        c.wait()
    zero = jnp.zeros((S, 128), F32)
    for leaf in range(NL):
        size = sizes[0, leaf]
        loads[leaf].wait()
        inc = split(local_ref[leaf] + dot3s([(split(tmat_ref[leaf]), rsplit)], 1, 0))
        for blk in range(4):
            rows = slice(128 * blk, 128 * blk + 128)
            val = part[leaf, rows, :] + dot3s([(split(basis[leaf, rows, :]), inc)], 1, 0)
            row = lax.broadcasted_iota(jnp.int32, (128, V), 0) + 128 * blk
            val = jnp.where(row < size, val, 0.0)
            for b in range(16):
                for k in range(3):
                    ot[pl.ds((128 * blk + 8 * b) * S + k, 8, stride=S), :] = val[
                        8 * b : 8 * b + 8, 128 * k : 128 * k + 128
                    ]
        steps = (size + UN - 1) // UN

        def place(i, _, leaf=leaf):
            base = pl.multiple_of(i * UN, UN)
            rows = [ot[tile_rows(base + r, 1), :] for r in range(UN)]
            for r in range(UN):
                pt[tile_rows(slot[leaf * LEAF + base + r], 1), :] = rows[r]
            return 0

        lax.fori_loop(0, steps, place, 0)

        def blank(i, _, leaf=leaf):
            base = pl.multiple_of(i * UN, UN)
            for r in range(UN):
                pt[tile_rows(slot[leaf * LEAF + base + r], 1), :] = zero
            return 0

        lax.fori_loop(steps, LEAF // UN, blank, 0)
    stores = []
    for c in range(NL):

        def flat(i, _, c=c):
            for u in range(4):
                base = pl.multiple_of(c * LEAF + i * 32 + u * 8, 8)
                for k in range(3):
                    res[pl.ds(base, 8), 128 * k : 128 * k + 128] = pt[
                        pl.ds(pl.multiple_of(base * S, 8) + k, 8, stride=S), :
                    ]
            return 0

        lax.fori_loop(0, LEAF // 32, flat, 0)
        cp = pltpu.make_async_copy(
            res.at[pl.ds(c * LEAF, LEAF)], out_hbm.at[pl.ds(c * LEAF, LEAF)], osem.at[c]
        )
        cp.start()
        stores.append(cp)
    for cp in stores:
        cp.wait()


def rows_down(me, slot, sizes, basis, part, local, tmat, *rest):
    hbm = pl.BlockSpec(memory_space=pltpu.HBM)
    vmem = pl.BlockSpec(memory_space=pltpu.VMEM)
    smem = pl.BlockSpec(memory_space=pltpu.SMEM)
    return pl.pallas_call(
        rows_down_kernel,
        out_shape=pltpu.HBM((ROWS, V), F32),
        in_specs=[smem] + [hbm] * 6 + [vmem] * len(rest),
        out_specs=hbm,
        scratch_shapes=[
            pltpu.SMEM((ROWS,), jnp.int32),
            pltpu.SMEM((1, NL), jnp.int32),
            pltpu.VMEM((NL, LEAF, R), F32),
            pltpu.VMEM((NL, LEAF, V), F32),
            pltpu.VMEM((NL, R, V), F32),
            pltpu.VMEM((NL, R, R), F32),
            pltpu.VMEM((LEAF * S, 128), F32),
            pltpu.VMEM((ROWS * S, 128), F32),
            pltpu.VMEM((ROWS, V), F32),
            pltpu.VMEM((V, R), F32),
            pltpu.SemaphoreType.DMA((5,)),
            pltpu.SemaphoreType.DMA((NL,)),
            pltpu.SemaphoreType.DMA((NL,)),
        ],
        compiler_params=pltpu.CompilerParams(vmem_limit_bytes=36 * MIB),
        cost_estimate=pl.CostEstimate(flops=2 * 10**9, bytes_accessed=16 * 10**6, transcendentals=0),
        name="rows_down",
    )(me, far(slot), far(sizes), far(basis), far(part), far(local), far(tmat), *rest)


def groups_of(bits, count):
    masks = [sum(1 << b for i, b in enumerate(bits) if k >> i & 1) for k in range(1 << len(bits))]
    full = masks[-1]
    return [[base | m for m in masks] for base in range(count) if base & full == 0]


def shards(
    vectors, slot_frame, leaf_sizes, near_field, leaf_basis,
    local_transfer, local_coupling, upper_transfer, pair_coupling,
):
    count = lax.axis_size("leaf")
    me = lax.axis_index("leaf").astype(jnp.int32).reshape(1)

    def swap(value, level):
        return lax.ppermute(value, "leaf", [(s, s ^ (1 << level)) for s in range(count)])

    def exchange(value, bits):
        return lax.all_to_all(
            value, "leaf", 0, 0, axis_index_groups=groups_of(bits, count), tiled=True
        )

    trans, coup, upper, pairs = (
        local_transfer[0], local_coupling[0], upper_transfer[0], pair_coupling[0],
    )
    a1, a2, m0, m1, m3, side2 = small(
        chains_kernel,
        [(R, 2 * R), (R, 3 * R), (2 * R, R), (3 * R, R), (4 * R, R), (R, R)],
        "chains",
        10**8,
        [
            pltpu.VMEM((1, R, R), F32),
            pltpu.VMEM((5, R, R), F32),
            pltpu.VMEM((7, R, R), F32),
            pltpu.SemaphoreType.DMA((3,)),
        ],
        (1, 2, 3),
    )(me, far(trans), far(upper), far(pairs))
    xh, xl, call, pay = rows_up(slot_frame, leaf_sizes, vectors, leaf_basis, trans)
    core_got = swap(pay, 0)
    pair2, lift3 = small(after_core_kernel, [(2, HALF, R), (HALF, R)], "after_core", 10**8)(
        me, pay, core_got, a1
    )
    y_got = exchange(lift3, (1, 2))
    pair_got = swap(pair2, 1)
    top_send, c3 = small(after_y_kernel, [(16 * QUART, R), (QUART, R)], "after_y", 10**8)(
        me, y_got, a2
    )
    top_got = exchange(top_send, (3, 4, 5, 6))
    (c2,) = small(after_pair_kernel, [(HALF, R)], "after_pair", 10**6)(pair2, pair_got)
    quad_got = swap(c2, 2)
    part, local, tmat, curv = near_local(
        me, near_field, xh, xl, call, trans, coup, pay, core_got, pair2, pair_got, c2, m0, m1
    )
    (inc3,) = small(
        after_top_kernel, [(4, QUART + 8, R)], "after_top", 10**8, [pltpu.VMEM((V, R), F32)]
    )(me, top_got, m3, side2, c2, quad_got, c3, curv)
    inc3_got = exchange(inc3, (1, 2))
    (inc1,) = small(to_core_kernel, [(HALF + 8, R)], "to_core", 10**8)(
        inc3_got, pair_got, quad_got, m1
    )
    inc1_got = swap(inc1, 0)
    (share,) = small(core_share_kernel, [(16, 8, R)], "core_share", 10**5)(inc1, inc1_got)
    share = exchange(share, (3, 4, 5, 6))
    products = rows_down(
        me, slot_frame, leaf_sizes, leaf_basis, part, local, tmat, inc1, inc1_got, core_got, m0
    )
    (curvature,) = small(all_share_kernel, [(8, R)], "all_share", 10**5)(share)
    return products, curvature[0:3].reshape(V)


def solution(mesh):
    return jax.shard_map(
        shards,
        mesh=mesh,
        in_specs=(
            P("leaf", None),
            P("leaf"),
            P("leaf", None),
            P("leaf", None, None),
            P("leaf", None, None),
            P("leaf", None, None, None),
            P("leaf", None, None, None),
            P("leaf", None, None, None),
            P("leaf", None, None, None),
        ),
        out_specs=(P("leaf", None), P()),
        check_vma=False,
    )
```

```python
import functools

import jax
import jax.numpy as jnp
from jax import lax
from jax.experimental import pallas as pl
from jax.experimental.pallas import tpu as pltpu
from jax.sharding import PartitionSpec as P

LEAF = 512
NL = 8
R = 128
V = 384
HALF = V // 2
QUART = HALF // 4
SHARE = 64
ROWS = NL * LEAF
S = 4
MB = 256
UN = 32
F32 = jnp.float32
BF16 = jnp.bfloat16
MIB = 1 << 20


def split(a):
    hi = a.astype(BF16)
    return hi, (a - hi.astype(F32)).astype(BF16)


def dot3s(terms, ca, cb):
    lhs, rhs = [], []
    for (ah, al), (bh, bl) in terms:
        lhs += [ah, ah, al]
        rhs += [bh, bl, bh]
    return lax.dot_general(
        jnp.concatenate(lhs, axis=ca),
        jnp.concatenate(rhs, axis=cb),
        (((ca,), (cb,)), ((), ())),
        preferred_element_type=F32,
    )


def dot3(a, b, ca=1, cb=0):
    return dot3s([(split(a), split(b))], ca, cb)


def tile_rows(start, count):
    return pl.ds(pl.multiple_of(start * S, S), count * S)


def far(x):
    return pltpu.with_memory_space_constraint(x, pltpu.HBM)


def lane_rows(p):
    parts = [p[0:1, 128 * k : 128 * k + 128] for k in range(3)]
    return jnp.concatenate(parts + [jnp.zeros((5, 128), F32)], axis=0)


def row_sums(z):
    zh, zl = split(z)
    ones = jnp.ones((8, 2 * R), BF16)
    return lax.dot_general(
        ones, jnp.concatenate([zh, zl], axis=1), (((1,), (1,)), ((), ())),
        preferred_element_type=F32,
    )


def rows_up_kernel(
    slot_hbm, sizes_hbm, v_hbm, basis_hbm, trans_hbm, near_hbm,
    part_hbm, call_hbm, pay_ref, curv_ref,
    slot, sizes, vbuf, vt, xt, basis, trans, near, xh, xl, call_ref,
    sem, vsem, nsem, osem,
):
    copies = [
        pltpu.make_async_copy(slot_hbm, slot, sem.at[0]),
        pltpu.make_async_copy(sizes_hbm, sizes, sem.at[1]),
        pltpu.make_async_copy(basis_hbm, basis, sem.at[2]),
        pltpu.make_async_copy(trans_hbm, trans, sem.at[3]),
    ]
    chunks = [
        pltpu.make_async_copy(
            v_hbm.at[pl.ds(c * LEAF, LEAF)], vbuf.at[pl.ds(c * LEAF, LEAF)], vsem.at[c]
        )
        for c in range(NL)
    ]
    copies[0].start()
    copies[1].start()
    for c in range(NL):
        chunks[c].start()
    nears = [
        pltpu.make_async_copy(near_hbm.at[leaf], near.at[leaf], nsem.at[leaf]) for leaf in range(NL)
    ]
    for c in range(NL):
        chunks[c].wait()
        if c == NL - 2:
            copies[2].start()
            for n in nears:
                n.start()
            copies[3].start()

        def spread(i, _, c=c):
            for u in range(8):
                base = pl.multiple_of(c * LEAF + i * 64 + u * 8, 8)
                for k in range(3):
                    vt[pl.ds(pl.multiple_of(base * S, 8) + k, 8, stride=S), :] = vbuf[
                        pl.ds(base, 8), 128 * k : 128 * k + 128
                    ]
            return 0

        lax.fori_loop(0, LEAF // 64, spread, 0)
    copies[0].wait()
    copies[1].wait()
    for leaf in range(NL):

        def pick(i, _, leaf=leaf):
            base = pl.multiple_of(leaf * LEAF + i * UN, UN)
            rows = [vt[tile_rows(slot[base + r], 1), :] for r in range(UN)]
            for r in range(UN):
                xt[tile_rows(base + r, 1), :] = rows[r]
            return 0

        lax.fori_loop(0, (sizes[0, leaf] + UN - 1) // UN, pick, 0)
    copies[2].wait()
    for c in nears[0:4]:
        c.wait()
    lane_row = lax.broadcasted_iota(jnp.int32, (8, 128), 0)

    def pack(leaf, first=0, last=LEAF):
        size = sizes[0, leaf]
        for base in range(first, last, 16):
            for k in range(3):
                pieces = []
                for half in (0, 8):
                    val = xt[pl.ds((leaf * LEAF + base + half) * S + k, 8, stride=S), :]
                    pieces.append(jnp.where(lane_row < size - (base + half), val, 0.0))
                hi, lo = split(jnp.concatenate(pieces, axis=0))
                xh[leaf, base : base + 16, 128 * k : 128 * k + 128] = hi
                xl[leaf, base : base + 16, 128 * k : 128 * k + 128] = lo

    outs = []
    coeffs = []
    total = jnp.zeros((1, V), F32)
    pack(0)
    for leaf in range(NL):
        x = (xh[leaf], xl[leaf])
        c = dot3s([(split(basis[leaf]), x)], 0, 0)
        call_ref[leaf] = c
        coeffs.append(split(c))
        for blk in range(LEAF // MB):
            rows = slice(MB * blk, MB * blk + MB)
            prod = dot3s([(split(near[leaf, rows, :]), x)], 1, 0)
            xb = xh[leaf, rows, :].astype(F32) + xl[leaf, rows, :].astype(F32)
            total += jnp.sum(prod * xb, axis=0, keepdims=True)
            vbuf[leaf * LEAF + MB * blk : leaf * LEAF + MB * blk + MB, :] = prod
            if leaf + 1 < NL:
                pack(leaf + 1, MB * blk, MB * blk + MB)
        if leaf % 4 == 3:
            for n in range(leaf - 3, leaf + 1):
                cp = pltpu.make_async_copy(
                    vbuf.at[pl.ds(n * LEAF, LEAF)], part_hbm.at[n], osem.at[n]
                )
                cp.start()
                outs.append(cp)
        if leaf == 3:
            for cp in nears[4:]:
                cp.wait()
    copies[3].wait()
    offset, at = 0, NL
    while len(coeffs) > 1:
        parents = []
        for m in range(len(coeffs) // 2):
            terms = [(split(trans[offset + 2 * m + t]), coeffs[2 * m + t]) for t in range(2)]
            c = dot3s(terms, 0, 0)
            parents.append(c)
            if len(coeffs) > 2:
                call_ref[at] = c
                at += 1
        offset += len(coeffs)
        coeffs = [split(c) for c in parents]
    cp = pltpu.make_async_copy(call_ref, call_hbm, osem.at[NL])
    cp.start()
    outs.append(cp)
    curv_ref[...] = jnp.broadcast_to(total, (8, V))
    pay_ref[0] = parents[0].T
    pay_ref[1] = dot3s([(coeffs[0], split(trans[2 * NL - 2]))], 0, 0)
    for cp in outs:
        cp.wait()


def rows_up(slot, sizes, vectors, basis, trans, near):
    hbm = pl.BlockSpec(memory_space=pltpu.HBM)
    vmem = pl.BlockSpec(memory_space=pltpu.VMEM)
    return pl.pallas_call(
        rows_up_kernel,
        out_shape=(
            pltpu.HBM((NL, LEAF, V), F32),
            pltpu.HBM((14, R, V), F32),
            jax.ShapeDtypeStruct((2, V, R), F32),
            jax.ShapeDtypeStruct((8, V), F32),
        ),
        in_specs=[hbm] * 6,
        out_specs=(hbm, hbm, vmem, vmem),
        scratch_shapes=[
            pltpu.SMEM((ROWS,), jnp.int32),
            pltpu.SMEM((1, NL), jnp.int32),
            pltpu.VMEM((ROWS, V), F32),
            pltpu.VMEM((ROWS * S, 128), F32),
            pltpu.VMEM((ROWS * S, 128), F32),
            pltpu.VMEM((NL, LEAF, R), F32),
            pltpu.VMEM((2 * NL - 1, R, R), F32),
            pltpu.VMEM((NL, LEAF, LEAF), F32),
            pltpu.VMEM((NL, LEAF, V), BF16),
            pltpu.VMEM((NL, LEAF, V), BF16),
            pltpu.VMEM((14, R, V), F32),
            pltpu.SemaphoreType.DMA((4,)),
            pltpu.SemaphoreType.DMA((NL,)),
            pltpu.SemaphoreType.DMA((NL,)),
            pltpu.SemaphoreType.DMA((NL + 1,)),
        ],
        compiler_params=pltpu.CompilerParams(vmem_limit_bytes=50 * MIB),
        cost_estimate=pl.CostEstimate(flops=7 * 10**9, bytes_accessed=28 * 10**6, transcendentals=0),
        name="rows_up",
    )(far(slot), far(sizes), far(vectors), far(basis), far(trans), far(near))


def fields_kernel(
    me, call_hbm, trans_hbm, coup_hbm,
    pay_ref, got_ref, pair2_ref, pair_got_ref, c2_ref, m0_ref, m1_ref, near_ref,
    inc_ref, tmat_ref, curv_ref, call_ref, trans_ref, coup_ref, z, sem,
):
    copies = [
        pltpu.make_async_copy(call_hbm, call_ref, sem.at[0]),
        pltpu.make_async_copy(trans_hbm, trans_ref, sem.at[1]),
        pltpu.make_async_copy(coup_hbm, coup_ref, sem.at[2]),
    ]
    for c in copies:
        c.start()
    z[...] = pay_ref[0] * dot3(got_ref[0], m0_ref[0:R])
    start = pl.multiple_of((me[0] % 2) * HALF, HALF)
    z[pl.ds(start, HALF), :] += pair2_ref[0] * dot3(pair_got_ref[0], m1_ref[0:R])
    for c in copies:
        c.wait()
    total = jnp.zeros((1, V), F32)
    starts = (0, 8, 12)
    fields = [None] * 14
    pair = 0
    for height in range(3):
        for m in range(4 >> height):
            a = starts[height] + 2 * m
            bm = split(coup_ref[pair])
            ca, cb = call_ref[a], call_ref[a + 1]
            fields[a] = dot3s([(bm, split(cb))], 1, 0)
            fields[a + 1] = dot3s([(bm, split(ca))], 0, 0)
            total += 2.0 * jnp.sum(ca * fields[a], axis=0, keepdims=True)
            pair += 1
    curv_ref[...] = near_ref[...] + row_sums(z[...]) + jnp.broadcast_to(total, (8, V))
    top = [split(fields[12 + m]) for m in range(2)]
    tops = [split(trans_ref[12 + m]) for m in range(2)]
    for m in range(4):
        w = split(trans_ref[8 + m])
        mid = split(fields[8 + m] + dot3s([(w, top[m // 2])], 1, 0))
        tmid = split(dot3s([(w, tops[m // 2])], 1, 0))
        for n in (2 * m, 2 * m + 1):
            wl = split(trans_ref[n])
            inc_ref[n] = fields[n] + dot3s([(wl, mid)], 1, 0)
            tmat_ref[n] = dot3s([(wl, tmid)], 1, 0)


def fields(me, call, trans, coup, *rest):
    vmem = pl.BlockSpec(memory_space=pltpu.VMEM)
    hbm = pl.BlockSpec(memory_space=pltpu.HBM)
    smem = pl.BlockSpec(memory_space=pltpu.SMEM)
    return pl.pallas_call(
        fields_kernel,
        out_shape=(
            pltpu.HBM((NL, R, V), F32),
            pltpu.HBM((NL, R, R), F32),
            jax.ShapeDtypeStruct((8, V), F32),
        ),
        in_specs=[smem, hbm, hbm, hbm] + [vmem] * len(rest),
        out_specs=(vmem, vmem, vmem),
        scratch_shapes=[
            pltpu.VMEM((14, R, V), F32),
            pltpu.VMEM((2 * NL - 1, R, R), F32),
            pltpu.VMEM((NL - 1, R, R), F32),
            pltpu.VMEM((V, R), F32),
            pltpu.SemaphoreType.DMA((3,)),
        ],
        compiler_params=pltpu.CompilerParams(vmem_limit_bytes=24 * MIB),
        cost_estimate=pl.CostEstimate(flops=2 * 10**9, bytes_accessed=8 * 10**6, transcendentals=0),
        name="fields",
    )(me, far(call), far(trans), far(coup), *rest)


def chains_kernel(
    me, trans_hbm, upper_hbm, pair_hbm, a1_ref, a2_ref, m0_ref, m1_ref, m3_ref, side2_ref,
    trans_ref, upper_ref, pair_ref, sem,
):
    dev = me[0]
    copies = [
        pltpu.make_async_copy(trans_hbm.at[pl.ds(2 * NL - 2, 1)], trans_ref, sem.at[0]),
        pltpu.make_async_copy(upper_hbm, upper_ref, sem.at[1]),
        pltpu.make_async_copy(pair_hbm, pair_ref, sem.at[2]),
    ]
    for c in copies:
        c.start()
    for c in copies:
        c.wait()

    def side(level):
        b = pair_ref[level]
        return jnp.where((dev >> level) % 2 == 0, b, b.T)

    m0_ref[0:R] = side(0).T
    m0_ref[R : 2 * R] = trans_ref[0].T
    w1 = upper_ref[0]
    w12 = dot3(w1, upper_ref[1])
    a1_ref[:, 0:R] = w1
    a1_ref[:, R : 2 * R] = w12
    m1_ref[0:R] = side(1).T
    m1_ref[R : 2 * R] = dot3(w1, side(2)).T
    m1_ref[2 * R : 3 * R] = w12.T
    w3 = upper_ref[2]
    w34 = dot3(w3, upper_ref[3])
    w345 = dot3(w34, upper_ref[4])
    a2_ref[:, 0:R] = w3
    a2_ref[:, R : 2 * R] = w34
    a2_ref[:, 2 * R : 3 * R] = w345
    m3_ref[0:R] = side(3).T
    m3_ref[R : 2 * R] = dot3(w3, side(4)).T
    m3_ref[2 * R : 3 * R] = dot3(w34, side(5)).T
    m3_ref[3 * R : 4 * R] = dot3(w345, side(6)).T
    side2_ref[...] = side(2).T


def after_core_kernel(me, pay_ref, got_ref, a1_ref, pair2_ref, lift3_ref):
    start = pl.multiple_of((me[0] % 2) * HALF, HALF)
    c1 = pay_ref[1, pl.ds(start, HALF), :] + got_ref[1, pl.ds(start, HALF), :]
    x = dot3(c1, a1_ref[...])
    pair2_ref[0] = c1
    pair2_ref[1] = x[:, 0:R]
    lift3_ref[...] = x[:, R : 2 * R]


def after_y_kernel(me, got_ref, a2_ref, send_ref, c3_ref):
    c3 = got_ref[0:QUART]
    for n in range(1, 4):
        c3 = c3 + got_ref[n * QUART : (n + 1) * QUART]
    c3_ref[...] = c3
    x = dot3(c3, a2_ref[...])
    parts = [c3, x[:, 0:R], x[:, R : 2 * R], x[:, 2 * R : 3 * R]]
    group = me[0] // 8
    for s in range(16):
        d = jnp.bitwise_xor(group, s)
        send_ref[s * QUART : (s + 1) * QUART] = jnp.where(
            d >= 8, parts[3], jnp.where(d >= 4, parts[2], jnp.where(d >= 2, parts[1], parts[0]))
        )


def after_top_kernel(
    me, got_ref, m3_ref, side2_ref, c2_ref, quad_got_ref, c3_ref, local_ref, send_ref, share_ref, z
):
    dev = me[0]
    group = dev // 8
    sums = [jnp.zeros((QUART, R), F32) for _ in range(4)]
    bounds = ((1, 2), (2, 4), (4, 8), (8, 16))
    for s in range(16):
        d = jnp.bitwise_xor(group, s)
        val = got_ref[s * QUART : (s + 1) * QUART]
        for j, (low, high) in enumerate(bounds):
            sums[j] += jnp.where(jnp.logical_and(d >= low, d < high), val, 0.0)
    inc3 = dot3(jnp.concatenate(sums, axis=1), m3_ref[...])
    z[...] = jnp.zeros((V, R), F32)
    start = pl.multiple_of((dev % 2) * HALF, HALF)
    z[pl.ds(start, HALF), :] = 0.5 * (c2_ref[...] * dot3(quad_got_ref[...], side2_ref[...]))
    at = pl.multiple_of(start + ((dev // 2) % 4) * QUART, QUART)
    z[pl.ds(at, QUART), :] += c3_ref[...] * inc3
    share = lane_rows(local_ref[...] + row_sums(z[...]))
    for n in range(4):
        send_ref[n * QUART : (n + 1) * QUART] = inc3
    for n in range(SHARE // 8):
        share_ref[8 * n : 8 * n + 8] = share


def after_pair_kernel(pair2_ref, got_ref, c2_ref):
    c2_ref[...] = pair2_ref[1] + got_ref[1]


def to_core_kernel(got_ref, pair_got_ref, quad_got_ref, m1_ref, out_ref):
    sums = jnp.concatenate([pair_got_ref[0], quad_got_ref[...], got_ref[...]], axis=1)
    out_ref[...] = dot3(sums, m1_ref[...])


def all_share_kernel(got_hbm, out_ref, got, sem):
    cp = pltpu.make_async_copy(got_hbm.at[:, pl.ds(0, 8)], got, sem)
    cp.start()
    cp.wait()
    out_ref[...] = jnp.sum(got[...], axis=0) * (1.0 / (2.0 * LEAF))


def small(body, outs, name, flops, scratch=(), hbm_args=()):
    vmem = pl.BlockSpec(memory_space=pltpu.VMEM)
    smem = pl.BlockSpec(memory_space=pltpu.SMEM)
    hbm = pl.BlockSpec(memory_space=pltpu.HBM)

    def call(*args):
        return pl.pallas_call(
            body,
            out_shape=tuple(jax.ShapeDtypeStruct(o, F32) for o in outs),
            in_specs=[
                smem if a.dtype == jnp.int32 else (hbm if n in hbm_args else vmem)
                for n, a in enumerate(args)
            ],
            out_specs=tuple(vmem for _ in outs),
            scratch_shapes=list(scratch),
            compiler_params=pltpu.CompilerParams(vmem_limit_bytes=16 * MIB),
            cost_estimate=pl.CostEstimate(flops=flops, bytes_accessed=10**6, transcendentals=0),
            name=name,
        )(*args)

    return call


def rows_down_kernel(
    me, slot_hbm, sizes_hbm, basis_hbm, part_hbm, local_hbm, tmat_hbm,
    own_ref, other_ref, got_ref, m0_ref, out_hbm,
    slot, sizes, basis, part, local_ref, tmat_ref, ot, pt, res, inct, sem, psem, osem,
):
    copies = [
        pltpu.make_async_copy(slot_hbm, slot, sem.at[0]),
        pltpu.make_async_copy(sizes_hbm, sizes, sem.at[1]),
        pltpu.make_async_copy(tmat_hbm, tmat_ref, sem.at[2]),
        pltpu.make_async_copy(local_hbm, local_ref, sem.at[3]),
        pltpu.make_async_copy(basis_hbm, basis, sem.at[4]),
    ]
    for c in copies:
        c.start()
    loads = [
        pltpu.make_async_copy(part_hbm.at[leaf], part.at[leaf], psem.at[leaf]) for leaf in range(NL)
    ]
    for c in loads:
        c.start()
    half = me[0] % 2
    inct[pl.ds(pl.multiple_of(half * HALF, HALF), HALF), :] = own_ref[...]
    inct[pl.ds(pl.multiple_of((1 - half) * HALF, HALF), HALF), :] = other_ref[...]
    root = dot3(jnp.concatenate([got_ref[0], inct[...]], axis=1), m0_ref[...])
    rsplit = split(root.T)
    for c in copies:
        c.wait()
    incs = [
        split(local_ref[leaf] + dot3s([(split(tmat_ref[leaf]), rsplit)], 1, 0)) for leaf in range(NL)
    ]
    for c in loads:
        c.wait()
    lane_row = lax.broadcasted_iota(jnp.int32, (8, 128), 0)
    for leaf in range(NL):
        size = sizes[0, leaf]
        for blk in range(LEAF // 128):
            rows = slice(128 * blk, 128 * blk + 128)
            val = part[leaf, rows, :] + dot3s([(split(basis[leaf, rows, :]), incs[leaf])], 1, 0)
            for b in range(16):
                keep = lane_row < size - (128 * blk + 8 * b)
                for k in range(3):
                    ot[pl.ds((leaf * LEAF + 128 * blk + 8 * b) * S + k, 8, stride=S), :] = jnp.where(
                        keep, val[8 * b : 8 * b + 8, 128 * k : 128 * k + 128], 0.0
                    )
    zero = jnp.zeros((S, 128), F32)
    for leaf in range(NL):
        steps = (sizes[0, leaf] + UN - 1) // UN

        def place(i, _, leaf=leaf):
            base = pl.multiple_of(leaf * LEAF + i * UN, UN)
            rows = [ot[tile_rows(base + r, 1), :] for r in range(UN)]
            for r in range(UN):
                pt[tile_rows(slot[base + r], 1), :] = rows[r]
            return 0

        lax.fori_loop(0, steps, place, 0)

        def blank(i, _, leaf=leaf):
            base = pl.multiple_of(leaf * LEAF + i * UN, UN)
            for r in range(UN):
                pt[tile_rows(slot[base + r], 1), :] = zero
            return 0

        lax.fori_loop(steps, LEAF // UN, blank, 0)
    stores = []
    for c in range(NL):

        def flat(i, _, c=c):
            for u in range(16):
                base = pl.multiple_of(c * LEAF + i * 128 + u * 8, 8)
                for k in range(3):
                    res[pl.ds(base, 8), 128 * k : 128 * k + 128] = pt[
                        pl.ds(pl.multiple_of(base * S, 8) + k, 8, stride=S), :
                    ]
            return 0

        lax.fori_loop(0, LEAF // 128, flat, 0)
        cp = pltpu.make_async_copy(
            res.at[pl.ds(c * LEAF, LEAF)], out_hbm.at[pl.ds(c * LEAF, LEAF)], osem.at[c]
        )
        cp.start()
        stores.append(cp)
    for cp in stores:
        cp.wait()


def rows_down(me, slot, sizes, basis, part, local, tmat, *rest):
    hbm = pl.BlockSpec(memory_space=pltpu.HBM)
    vmem = pl.BlockSpec(memory_space=pltpu.VMEM)
    smem = pl.BlockSpec(memory_space=pltpu.SMEM)
    return pl.pallas_call(
        rows_down_kernel,
        out_shape=pltpu.HBM((ROWS, V), F32),
        in_specs=[smem] + [hbm] * 6 + [vmem] * len(rest),
        out_specs=hbm,
        scratch_shapes=[
            pltpu.SMEM((ROWS,), jnp.int32),
            pltpu.SMEM((1, NL), jnp.int32),
            pltpu.VMEM((NL, LEAF, R), F32),
            pltpu.VMEM((NL, LEAF, V), F32),
            pltpu.VMEM((NL, R, V), F32),
            pltpu.VMEM((NL, R, R), F32),
            pltpu.VMEM((ROWS * S, 128), F32),
            pltpu.VMEM((ROWS * S, 128), F32),
            pltpu.VMEM((ROWS, V), F32),
            pltpu.VMEM((V, R), F32),
            pltpu.SemaphoreType.DMA((5,)),
            pltpu.SemaphoreType.DMA((NL,)),
            pltpu.SemaphoreType.DMA((NL,)),
        ],
        compiler_params=pltpu.CompilerParams(vmem_limit_bytes=44 * MIB),
        cost_estimate=pl.CostEstimate(flops=2 * 10**9, bytes_accessed=16 * 10**6, transcendentals=0),
        name="rows_down",
    )(me, far(slot), far(sizes), far(basis), far(part), far(local), far(tmat), *rest)


def groups_of(bits, count):
    masks = [sum(1 << b for i, b in enumerate(bits) if k >> i & 1) for k in range(1 << len(bits))]
    full = masks[-1]
    return [[base | m for m in masks] for base in range(count) if base & full == 0]


def shards(
    vectors, slot_frame, leaf_sizes, near_field, leaf_basis,
    local_transfer, local_coupling, upper_transfer, pair_coupling,
):
    count = lax.axis_size("leaf")
    me = lax.axis_index("leaf").astype(jnp.int32).reshape(1)

    def swap(value, level):
        return lax.ppermute(value, "leaf", [(s, s ^ (1 << level)) for s in range(count)])

    def exchange(value, bits):
        return lax.all_to_all(
            value, "leaf", 0, 0, axis_index_groups=groups_of(bits, count), tiled=True
        )

    trans, coup, upper, pairs = (
        local_transfer[0], local_coupling[0], upper_transfer[0], pair_coupling[0],
    )
    a1, a2, m0, m1, m3, side2 = small(
        chains_kernel,
        [(R, 2 * R), (R, 3 * R), (2 * R, R), (3 * R, R), (4 * R, R), (R, R)],
        "chains",
        10**8,
        [
            pltpu.VMEM((1, R, R), F32),
            pltpu.VMEM((5, R, R), F32),
            pltpu.VMEM((7, R, R), F32),
            pltpu.SemaphoreType.DMA((3,)),
        ],
        (1, 2, 3),
    )(me, far(trans), far(upper), far(pairs))
    part, call, pay, curv = rows_up(
        slot_frame, leaf_sizes, vectors, leaf_basis, trans, near_field
    )
    core_got = swap(pay, 0)
    pair2, lift3 = small(after_core_kernel, [(2, HALF, R), (HALF, R)], "after_core", 10**8)(
        me, pay, core_got, a1
    )
    y_got = exchange(lift3, (1, 2))
    pair_got = swap(pair2, 1)
    top_send, c3 = small(after_y_kernel, [(16 * QUART, R), (QUART, R)], "after_y", 10**8)(
        me, y_got, a2
    )
    top_got = exchange(top_send, (3, 4, 5, 6))
    (c2,) = small(after_pair_kernel, [(HALF, R)], "after_pair", 10**6)(pair2, pair_got)
    quad_got = swap(c2, 2)
    local, tmat, curv = fields(
        me, call, trans, coup, pay, core_got, pair2, pair_got, c2, m0, m1, curv
    )
    inc3, share = small(
        after_top_kernel, [(HALF, R), (SHARE, R)], "after_top", 10**8, [pltpu.VMEM((V, R), F32)]
    )(me, top_got, m3, side2, c2, quad_got, c3, curv)
    inc3_got = exchange(inc3, (1, 2))
    (inc1,) = small(to_core_kernel, [(HALF, R)], "to_core", 10**8)(
        inc3_got, pair_got, quad_got, m1
    )
    inc1_got = swap(inc1, 0)
    share = lax.all_gather(share, "leaf")
    products = rows_down(
        me, slot_frame, leaf_sizes, leaf_basis, part, local, tmat, inc1, inc1_got, core_got, m0
    )
    (curvature,) = small(
        all_share_kernel, [(8, R)], "all_share", 10**5,
        [pltpu.VMEM((count, 8, R), F32), pltpu.SemaphoreType.DMA], (0,),
    )(far(share))
    return products, curvature[0:3].reshape(V)


def solution(mesh):
    return jax.shard_map(
        shards,
        mesh=mesh,
        in_specs=(
            P("leaf", None),
            P("leaf"),
            P("leaf", None),
            P("leaf", None, None),
            P("leaf", None, None),
            P("leaf", None, None, None),
            P("leaf", None, None, None),
            P("leaf", None, None, None),
            P("leaf", None, None, None),
        ),
        out_specs=(P("leaf", None), P()),
        check_vma=False,
    )
```

```python
import functools

import jax
import jax.numpy as jnp
from jax import lax
from jax.experimental import pallas as pl
from jax.experimental.pallas import tpu as pltpu
from jax.sharding import PartitionSpec as P

LEAF = 512
NL = 8
R = 128
V = 384
HALF = V // 2
QUART = HALF // 4
ROWS = NL * LEAF
S = 4
MB = 256
UN = 32
F32 = jnp.float32
BF16 = jnp.bfloat16
MIB = 1 << 20


def split(a):
    hi = a.astype(BF16)
    return hi, (a - hi.astype(F32)).astype(BF16)


def dot3s(terms, ca, cb):
    lhs, rhs = [], []
    for (ah, al), (bh, bl) in terms:
        lhs += [ah, ah, al]
        rhs += [bh, bl, bh]
    return lax.dot_general(
        jnp.concatenate(lhs, axis=ca),
        jnp.concatenate(rhs, axis=cb),
        (((ca,), (cb,)), ((), ())),
        preferred_element_type=F32,
    )


def dot3(a, b, ca=1, cb=0):
    return dot3s([(split(a), split(b))], ca, cb)


def tile_rows(start, count):
    return pl.ds(pl.multiple_of(start * S, S), count * S)


def far(x):
    return pltpu.with_memory_space_constraint(x, pltpu.HBM)


def lane_rows(p):
    parts = [p[0:1, 128 * k : 128 * k + 128] for k in range(3)]
    return jnp.concatenate(parts + [jnp.zeros((5, 128), F32)], axis=0)


def row_sums(z):
    zh, zl = split(z)
    ones = jnp.ones((8, 2 * R), BF16)
    return lax.dot_general(
        ones, jnp.concatenate([zh, zl], axis=1), (((1,), (1,)), ((), ())),
        preferred_element_type=F32,
    )


def rows_up_kernel(
    slot_hbm, sizes_hbm, v_hbm, basis_hbm, trans_hbm, near_hbm,
    part_hbm, call_hbm, pay_ref, curv_ref,
    slot, sizes, vbuf, vt, xt, basis, trans, near, xh, xl, call_ref,
    sem, vsem, nsem, osem,
):
    copies = [
        pltpu.make_async_copy(slot_hbm, slot, sem.at[0]),
        pltpu.make_async_copy(sizes_hbm, sizes, sem.at[1]),
        pltpu.make_async_copy(basis_hbm, basis, sem.at[2]),
        pltpu.make_async_copy(trans_hbm, trans, sem.at[3]),
    ]
    chunks = [
        pltpu.make_async_copy(
            v_hbm.at[pl.ds(c * LEAF, LEAF)], vbuf.at[pl.ds(c * LEAF, LEAF)], vsem.at[c]
        )
        for c in range(NL)
    ]
    copies[0].start()
    copies[1].start()
    for c in range(NL):
        chunks[c].start()
    nears = [
        pltpu.make_async_copy(near_hbm.at[leaf], near.at[leaf], nsem.at[leaf]) for leaf in range(NL)
    ]
    for c in range(NL):
        chunks[c].wait()
        if c == NL - 2:
            copies[2].start()
            for n in nears:
                n.start()
            copies[3].start()

        def spread(i, _, c=c):
            for u in range(8):
                base = pl.multiple_of(c * LEAF + i * 64 + u * 8, 8)
                for k in range(3):
                    vt[pl.ds(pl.multiple_of(base * S, 8) + k, 8, stride=S), :] = vbuf[
                        pl.ds(base, 8), 128 * k : 128 * k + 128
                    ]
            return 0

        lax.fori_loop(0, LEAF // 64, spread, 0)
    copies[0].wait()
    copies[1].wait()
    for leaf in range(NL):

        def pick(i, _, leaf=leaf):
            base = pl.multiple_of(leaf * LEAF + i * UN, UN)
            rows = [vt[tile_rows(slot[base + r], 1), :] for r in range(UN)]
            for r in range(UN):
                xt[tile_rows(base + r, 1), :] = rows[r]
            return 0

        lax.fori_loop(0, (sizes[0, leaf] + UN - 1) // UN, pick, 0)
    copies[2].wait()
    for c in nears[0:4]:
        c.wait()
    lane_row = lax.broadcasted_iota(jnp.int32, (8, 128), 0)

    def pack(leaf, first=0, last=LEAF):
        size = sizes[0, leaf]
        for base in range(first, last, 16):
            for k in range(3):
                pieces = []
                for half in (0, 8):
                    val = xt[pl.ds((leaf * LEAF + base + half) * S + k, 8, stride=S), :]
                    pieces.append(jnp.where(lane_row < size - (base + half), val, 0.0))
                hi, lo = split(jnp.concatenate(pieces, axis=0))
                xh[leaf, base : base + 16, 128 * k : 128 * k + 128] = hi
                xl[leaf, base : base + 16, 128 * k : 128 * k + 128] = lo

    outs = []
    coeffs = []
    total = jnp.zeros((1, V), F32)
    pack(0)
    for leaf in range(NL):
        x = (xh[leaf], xl[leaf])
        c = dot3s([(split(basis[leaf]), x)], 0, 0)
        call_ref[leaf] = c
        coeffs.append(split(c))
        for blk in range(LEAF // MB):
            rows = slice(MB * blk, MB * blk + MB)
            prod = dot3s([(split(near[leaf, rows, :]), x)], 1, 0)
            xb = xh[leaf, rows, :].astype(F32) + xl[leaf, rows, :].astype(F32)
            total += jnp.sum(prod * xb, axis=0, keepdims=True)
            vbuf[leaf * LEAF + MB * blk : leaf * LEAF + MB * blk + MB, :] = prod
            if leaf + 1 < NL:
                pack(leaf + 1, MB * blk, MB * blk + MB)
        if leaf % 4 == 3:
            for n in range(leaf - 3, leaf + 1):
                cp = pltpu.make_async_copy(
                    vbuf.at[pl.ds(n * LEAF, LEAF)], part_hbm.at[n], osem.at[n]
                )
                cp.start()
                outs.append(cp)
        if leaf == 3:
            for cp in nears[4:]:
                cp.wait()
    copies[3].wait()
    offset, at = 0, NL
    while len(coeffs) > 1:
        parents = []
        for m in range(len(coeffs) // 2):
            terms = [(split(trans[offset + 2 * m + t]), coeffs[2 * m + t]) for t in range(2)]
            c = dot3s(terms, 0, 0)
            parents.append(c)
            if len(coeffs) > 2:
                call_ref[at] = c
                at += 1
        offset += len(coeffs)
        coeffs = [split(c) for c in parents]
    cp = pltpu.make_async_copy(call_ref, call_hbm, osem.at[NL])
    cp.start()
    outs.append(cp)
    curv_ref[...] = jnp.broadcast_to(total, (8, V))
    pay_ref[0] = parents[0].T
    pay_ref[1] = dot3s([(coeffs[0], split(trans[2 * NL - 2]))], 0, 0)
    for cp in outs:
        cp.wait()


def rows_up(slot, sizes, vectors, basis, trans, near):
    hbm = pl.BlockSpec(memory_space=pltpu.HBM)
    vmem = pl.BlockSpec(memory_space=pltpu.VMEM)
    return pl.pallas_call(
        rows_up_kernel,
        out_shape=(
            pltpu.HBM((NL, LEAF, V), F32),
            pltpu.HBM((14, R, V), F32),
            jax.ShapeDtypeStruct((2, V, R), F32),
            jax.ShapeDtypeStruct((8, V), F32),
        ),
        in_specs=[hbm] * 6,
        out_specs=(hbm, hbm, vmem, vmem),
        scratch_shapes=[
            pltpu.SMEM((ROWS,), jnp.int32),
            pltpu.SMEM((1, NL), jnp.int32),
            pltpu.VMEM((ROWS, V), F32),
            pltpu.VMEM((ROWS * S, 128), F32),
            pltpu.VMEM((ROWS * S, 128), F32),
            pltpu.VMEM((NL, LEAF, R), F32),
            pltpu.VMEM((2 * NL - 1, R, R), F32),
            pltpu.VMEM((NL, LEAF, LEAF), F32),
            pltpu.VMEM((NL, LEAF, V), BF16),
            pltpu.VMEM((NL, LEAF, V), BF16),
            pltpu.VMEM((14, R, V), F32),
            pltpu.SemaphoreType.DMA((4,)),
            pltpu.SemaphoreType.DMA((NL,)),
            pltpu.SemaphoreType.DMA((NL,)),
            pltpu.SemaphoreType.DMA((NL + 1,)),
        ],
        compiler_params=pltpu.CompilerParams(vmem_limit_bytes=50 * MIB),
        cost_estimate=pl.CostEstimate(flops=7 * 10**9, bytes_accessed=28 * 10**6, transcendentals=0),
        name="rows_up",
    )(far(slot), far(sizes), far(vectors), far(basis), far(trans), far(near))


def fields_kernel(
    me, call_hbm, trans_hbm, coup_hbm,
    pay_ref, got_ref, pair2_ref, pair_got_ref, c2_ref, m0_ref, m1_ref, near_ref,
    inc_ref, tmat_ref, curv_ref, call_ref, trans_ref, coup_ref, z, sem,
):
    copies = [
        pltpu.make_async_copy(call_hbm, call_ref, sem.at[0]),
        pltpu.make_async_copy(trans_hbm, trans_ref, sem.at[1]),
        pltpu.make_async_copy(coup_hbm, coup_ref, sem.at[2]),
    ]
    for c in copies:
        c.start()
    z[...] = pay_ref[0] * dot3(got_ref[0], m0_ref[0:R])
    start = pl.multiple_of((me[0] % 2) * HALF, HALF)
    z[pl.ds(start, HALF), :] += pair2_ref[0] * dot3(pair_got_ref[0], m1_ref[0:R])
    for c in copies:
        c.wait()
    total = jnp.zeros((1, V), F32)
    starts = (0, 8, 12)
    fields = [None] * 14
    pair = 0
    for height in range(3):
        for m in range(4 >> height):
            a = starts[height] + 2 * m
            bm = split(coup_ref[pair])
            ca, cb = call_ref[a], call_ref[a + 1]
            fields[a] = dot3s([(bm, split(cb))], 1, 0)
            fields[a + 1] = dot3s([(bm, split(ca))], 0, 0)
            total += 2.0 * jnp.sum(ca * fields[a], axis=0, keepdims=True)
            pair += 1
    curv_ref[...] = near_ref[...] + row_sums(z[...]) + jnp.broadcast_to(total, (8, V))
    top = [split(fields[12 + m]) for m in range(2)]
    tops = [split(trans_ref[12 + m]) for m in range(2)]
    for m in range(4):
        w = split(trans_ref[8 + m])
        mid = split(fields[8 + m] + dot3s([(w, top[m // 2])], 1, 0))
        tmid = split(dot3s([(w, tops[m // 2])], 1, 0))
        for n in (2 * m, 2 * m + 1):
            wl = split(trans_ref[n])
            inc_ref[n] = fields[n] + dot3s([(wl, mid)], 1, 0)
            tmat_ref[n] = dot3s([(wl, tmid)], 1, 0)


def fields(me, call, trans, coup, *rest):
    vmem = pl.BlockSpec(memory_space=pltpu.VMEM)
    hbm = pl.BlockSpec(memory_space=pltpu.HBM)
    smem = pl.BlockSpec(memory_space=pltpu.SMEM)
    return pl.pallas_call(
        fields_kernel,
        out_shape=(
            pltpu.HBM((NL, R, V), F32),
            pltpu.HBM((NL, R, R), F32),
            jax.ShapeDtypeStruct((8, V), F32),
        ),
        in_specs=[smem, hbm, hbm, hbm] + [vmem] * len(rest),
        out_specs=(vmem, vmem, vmem),
        scratch_shapes=[
            pltpu.VMEM((14, R, V), F32),
            pltpu.VMEM((2 * NL - 1, R, R), F32),
            pltpu.VMEM((NL - 1, R, R), F32),
            pltpu.VMEM((V, R), F32),
            pltpu.SemaphoreType.DMA((3,)),
        ],
        compiler_params=pltpu.CompilerParams(vmem_limit_bytes=24 * MIB),
        cost_estimate=pl.CostEstimate(flops=2 * 10**9, bytes_accessed=8 * 10**6, transcendentals=0),
        name="fields",
    )(me, far(call), far(trans), far(coup), *rest)


def chains_kernel(
    me, trans_hbm, upper_hbm, pair_hbm, a1_ref, a2_ref, m0_ref, m1_ref, m3_ref, side2_ref,
    trans_ref, upper_ref, pair_ref, sem,
):
    dev = me[0]
    copies = [
        pltpu.make_async_copy(trans_hbm.at[pl.ds(2 * NL - 2, 1)], trans_ref, sem.at[0]),
        pltpu.make_async_copy(upper_hbm, upper_ref, sem.at[1]),
        pltpu.make_async_copy(pair_hbm, pair_ref, sem.at[2]),
    ]
    for c in copies:
        c.start()
    for c in copies:
        c.wait()

    def side(level):
        b = pair_ref[level]
        return jnp.where((dev >> level) % 2 == 0, b, b.T)

    m0_ref[0:R] = side(0).T
    m0_ref[R : 2 * R] = trans_ref[0].T
    w1 = upper_ref[0]
    w12 = dot3(w1, upper_ref[1])
    a1_ref[:, 0:R] = w1
    a1_ref[:, R : 2 * R] = w12
    m1_ref[0:R] = side(1).T
    m1_ref[R : 2 * R] = dot3(w1, side(2)).T
    m1_ref[2 * R : 3 * R] = w12.T
    w3 = upper_ref[2]
    w34 = dot3(w3, upper_ref[3])
    w345 = dot3(w34, upper_ref[4])
    a2_ref[:, 0:R] = w3
    a2_ref[:, R : 2 * R] = w34
    a2_ref[:, 2 * R : 3 * R] = w345
    m3_ref[0:R] = side(3).T
    m3_ref[R : 2 * R] = dot3(w3, side(4)).T
    m3_ref[2 * R : 3 * R] = dot3(w34, side(5)).T
    m3_ref[3 * R : 4 * R] = dot3(w345, side(6)).T
    side2_ref[...] = side(2).T


def after_core_kernel(me, pay_ref, got_ref, a1_ref, pair2_ref, lift3_ref):
    start = pl.multiple_of((me[0] % 2) * HALF, HALF)
    c1 = pay_ref[1, pl.ds(start, HALF), :] + got_ref[1, pl.ds(start, HALF), :]
    x = dot3(c1, a1_ref[...])
    pair2_ref[0] = c1
    pair2_ref[1] = x[:, 0:R]
    lift3_ref[...] = x[:, R : 2 * R]


def after_y_kernel(me, got_ref, a2_ref, send_ref, c3_ref):
    c3 = got_ref[0:QUART]
    for n in range(1, 4):
        c3 = c3 + got_ref[n * QUART : (n + 1) * QUART]
    c3_ref[...] = c3
    x = dot3(c3, a2_ref[...])
    parts = [c3, x[:, 0:R], x[:, R : 2 * R], x[:, 2 * R : 3 * R]]
    group = me[0] // 8
    for s in range(16):
        d = jnp.bitwise_xor(group, s)
        send_ref[s * QUART : (s + 1) * QUART] = jnp.where(
            d >= 8, parts[3], jnp.where(d >= 4, parts[2], jnp.where(d >= 2, parts[1], parts[0]))
        )


def after_top_kernel(
    me, got_ref, m3_ref, side2_ref, c2_ref, quad_got_ref, c3_ref, local_ref, send_ref, z
):
    dev = me[0]
    group = dev // 8
    sums = [jnp.zeros((QUART, R), F32) for _ in range(4)]
    bounds = ((1, 2), (2, 4), (4, 8), (8, 16))
    for s in range(16):
        d = jnp.bitwise_xor(group, s)
        val = got_ref[s * QUART : (s + 1) * QUART]
        for j, (low, high) in enumerate(bounds):
            sums[j] += jnp.where(jnp.logical_and(d >= low, d < high), val, 0.0)
    inc3 = dot3(jnp.concatenate(sums, axis=1), m3_ref[...])
    z[...] = jnp.zeros((V, R), F32)
    start = pl.multiple_of((dev % 2) * HALF, HALF)
    z[pl.ds(start, HALF), :] = 0.5 * (c2_ref[...] * dot3(quad_got_ref[...], side2_ref[...]))
    at = pl.multiple_of(start + ((dev // 2) % 4) * QUART, QUART)
    z[pl.ds(at, QUART), :] += c3_ref[...] * inc3
    share = lane_rows(local_ref[...] + row_sums(z[...]))
    for n in range(4):
        send_ref[n, 0:QUART] = inc3
        send_ref[n, QUART : QUART + 8] = share


def after_pair_kernel(pair2_ref, got_ref, c2_ref):
    c2_ref[...] = pair2_ref[1] + got_ref[1]


def to_core_kernel(got_ref, pair_got_ref, quad_got_ref, m1_ref, out_ref):
    inc3 = jnp.concatenate([got_ref[n, 0:QUART] for n in range(4)], axis=0)
    sums = jnp.concatenate([pair_got_ref[0], quad_got_ref[...], inc3], axis=1)
    out_ref[0:HALF] = dot3(sums, m1_ref[...])
    share = got_ref[0, QUART : QUART + 8]
    for n in range(1, 4):
        share = share + got_ref[n, QUART : QUART + 8]
    out_ref[HALF : HALF + 8] = share


def core_share_kernel(own_ref, other_ref, send_ref):
    total = own_ref[HALF : HALF + 8] + other_ref[HALF : HALF + 8]
    for n in range(16):
        send_ref[n] = total


def all_share_kernel(got_ref, out_ref):
    total = got_ref[0]
    for n in range(1, 16):
        total = total + got_ref[n]
    out_ref[...] = total * (1.0 / (2.0 * LEAF))


def small(body, outs, name, flops, scratch=(), hbm_args=()):
    vmem = pl.BlockSpec(memory_space=pltpu.VMEM)
    smem = pl.BlockSpec(memory_space=pltpu.SMEM)
    hbm = pl.BlockSpec(memory_space=pltpu.HBM)

    def call(*args):
        return pl.pallas_call(
            body,
            out_shape=tuple(jax.ShapeDtypeStruct(o, F32) for o in outs),
            in_specs=[
                smem if a.dtype == jnp.int32 else (hbm if n in hbm_args else vmem)
                for n, a in enumerate(args)
            ],
            out_specs=tuple(vmem for _ in outs),
            scratch_shapes=list(scratch),
            compiler_params=pltpu.CompilerParams(vmem_limit_bytes=16 * MIB),
            cost_estimate=pl.CostEstimate(flops=flops, bytes_accessed=10**6, transcendentals=0),
            name=name,
        )(*args)

    return call


def rows_down_kernel(
    me, slot_hbm, sizes_hbm, basis_hbm, part_hbm, local_hbm, tmat_hbm,
    own_ref, other_ref, got_ref, m0_ref, out_hbm,
    slot, sizes, basis, part, local_ref, tmat_ref, ot, pt, res, inct, sem, psem, osem,
):
    copies = [
        pltpu.make_async_copy(slot_hbm, slot, sem.at[0]),
        pltpu.make_async_copy(sizes_hbm, sizes, sem.at[1]),
        pltpu.make_async_copy(tmat_hbm, tmat_ref, sem.at[2]),
        pltpu.make_async_copy(local_hbm, local_ref, sem.at[3]),
        pltpu.make_async_copy(basis_hbm, basis, sem.at[4]),
    ]
    for c in copies:
        c.start()
    loads = [
        pltpu.make_async_copy(part_hbm.at[leaf], part.at[leaf], psem.at[leaf]) for leaf in range(NL)
    ]
    for c in loads:
        c.start()
    half = me[0] % 2
    inct[pl.ds(pl.multiple_of(half * HALF, HALF), HALF), :] = own_ref[0:HALF]
    inct[pl.ds(pl.multiple_of((1 - half) * HALF, HALF), HALF), :] = other_ref[0:HALF]
    root = dot3(jnp.concatenate([got_ref[0], inct[...]], axis=1), m0_ref[...])
    rsplit = split(root.T)
    for c in copies:
        c.wait()
    incs = [
        split(local_ref[leaf] + dot3s([(split(tmat_ref[leaf]), rsplit)], 1, 0)) for leaf in range(NL)
    ]
    for c in loads:
        c.wait()
    lane_row = lax.broadcasted_iota(jnp.int32, (8, 128), 0)
    for leaf in range(NL):
        size = sizes[0, leaf]
        for blk in range(LEAF // 128):
            rows = slice(128 * blk, 128 * blk + 128)
            val = part[leaf, rows, :] + dot3s([(split(basis[leaf, rows, :]), incs[leaf])], 1, 0)
            for b in range(16):
                keep = lane_row < size - (128 * blk + 8 * b)
                for k in range(3):
                    ot[pl.ds((leaf * LEAF + 128 * blk + 8 * b) * S + k, 8, stride=S), :] = jnp.where(
                        keep, val[8 * b : 8 * b + 8, 128 * k : 128 * k + 128], 0.0
                    )
    zero = jnp.zeros((S, 128), F32)
    for leaf in range(NL):
        steps = (sizes[0, leaf] + UN - 1) // UN

        def place(i, _, leaf=leaf):
            base = pl.multiple_of(leaf * LEAF + i * UN, UN)
            rows = [ot[tile_rows(base + r, 1), :] for r in range(UN)]
            for r in range(UN):
                pt[tile_rows(slot[base + r], 1), :] = rows[r]
            return 0

        lax.fori_loop(0, steps, place, 0)

        def blank(i, _, leaf=leaf):
            base = pl.multiple_of(leaf * LEAF + i * UN, UN)
            for r in range(UN):
                pt[tile_rows(slot[base + r], 1), :] = zero
            return 0

        lax.fori_loop(steps, LEAF // UN, blank, 0)
    stores = []
    for c in range(NL):

        def flat(i, _, c=c):
            for u in range(16):
                base = pl.multiple_of(c * LEAF + i * 128 + u * 8, 8)
                for k in range(3):
                    res[pl.ds(base, 8), 128 * k : 128 * k + 128] = pt[
                        pl.ds(pl.multiple_of(base * S, 8) + k, 8, stride=S), :
                    ]
            return 0

        lax.fori_loop(0, LEAF // 128, flat, 0)
        cp = pltpu.make_async_copy(
            res.at[pl.ds(c * LEAF, LEAF)], out_hbm.at[pl.ds(c * LEAF, LEAF)], osem.at[c]
        )
        cp.start()
        stores.append(cp)
    for cp in stores:
        cp.wait()


def rows_down(me, slot, sizes, basis, part, local, tmat, *rest):
    hbm = pl.BlockSpec(memory_space=pltpu.HBM)
    vmem = pl.BlockSpec(memory_space=pltpu.VMEM)
    smem = pl.BlockSpec(memory_space=pltpu.SMEM)
    return pl.pallas_call(
        rows_down_kernel,
        out_shape=pltpu.HBM((ROWS, V), F32),
        in_specs=[smem] + [hbm] * 6 + [vmem] * len(rest),
        out_specs=hbm,
        scratch_shapes=[
            pltpu.SMEM((ROWS,), jnp.int32),
            pltpu.SMEM((1, NL), jnp.int32),
            pltpu.VMEM((NL, LEAF, R), F32),
            pltpu.VMEM((NL, LEAF, V), F32),
            pltpu.VMEM((NL, R, V), F32),
            pltpu.VMEM((NL, R, R), F32),
            pltpu.VMEM((ROWS * S, 128), F32),
            pltpu.VMEM((ROWS * S, 128), F32),
            pltpu.VMEM((ROWS, V), F32),
            pltpu.VMEM((V, R), F32),
            pltpu.SemaphoreType.DMA((5,)),
            pltpu.SemaphoreType.DMA((NL,)),
            pltpu.SemaphoreType.DMA((NL,)),
        ],
        compiler_params=pltpu.CompilerParams(vmem_limit_bytes=44 * MIB),
        cost_estimate=pl.CostEstimate(flops=2 * 10**9, bytes_accessed=16 * 10**6, transcendentals=0),
        name="rows_down",
    )(me, far(slot), far(sizes), far(basis), far(part), far(local), far(tmat), *rest)


def groups_of(bits, count):
    masks = [sum(1 << b for i, b in enumerate(bits) if k >> i & 1) for k in range(1 << len(bits))]
    full = masks[-1]
    return [[base | m for m in masks] for base in range(count) if base & full == 0]


def shards(
    vectors, slot_frame, leaf_sizes, near_field, leaf_basis,
    local_transfer, local_coupling, upper_transfer, pair_coupling,
):
    count = lax.axis_size("leaf")
    me = lax.axis_index("leaf").astype(jnp.int32).reshape(1)

    def swap(value, level):
        return lax.ppermute(value, "leaf", [(s, s ^ (1 << level)) for s in range(count)])

    def exchange(value, bits):
        return lax.all_to_all(
            value, "leaf", 0, 0, axis_index_groups=groups_of(bits, count), tiled=True
        )

    trans, coup, upper, pairs = (
        local_transfer[0], local_coupling[0], upper_transfer[0], pair_coupling[0],
    )
    a1, a2, m0, m1, m3, side2 = small(
        chains_kernel,
        [(R, 2 * R), (R, 3 * R), (2 * R, R), (3 * R, R), (4 * R, R), (R, R)],
        "chains",
        10**8,
        [
            pltpu.VMEM((1, R, R), F32),
            pltpu.VMEM((5, R, R), F32),
            pltpu.VMEM((7, R, R), F32),
            pltpu.SemaphoreType.DMA((3,)),
        ],
        (1, 2, 3),
    )(me, far(trans), far(upper), far(pairs))
    part, call, pay, curv = rows_up(
        slot_frame, leaf_sizes, vectors, leaf_basis, trans, near_field
    )
    core_got = swap(pay, 0)
    pair2, lift3 = small(after_core_kernel, [(2, HALF, R), (HALF, R)], "after_core", 10**8)(
        me, pay, core_got, a1
    )
    y_got = exchange(lift3, (1, 2))
    pair_got = swap(pair2, 1)
    top_send, c3 = small(after_y_kernel, [(16 * QUART, R), (QUART, R)], "after_y", 10**8)(
        me, y_got, a2
    )
    top_got = exchange(top_send, (3, 4, 5, 6))
    (c2,) = small(after_pair_kernel, [(HALF, R)], "after_pair", 10**6)(pair2, pair_got)
    quad_got = swap(c2, 2)
    local, tmat, curv = fields(
        me, call, trans, coup, pay, core_got, pair2, pair_got, c2, m0, m1, curv
    )
    (inc3,) = small(
        after_top_kernel, [(4, QUART + 8, R)], "after_top", 10**8, [pltpu.VMEM((V, R), F32)]
    )(me, top_got, m3, side2, c2, quad_got, c3, curv)
    inc3_got = exchange(inc3, (1, 2))
    (inc1,) = small(to_core_kernel, [(HALF + 8, R)], "to_core", 10**8)(
        inc3_got, pair_got, quad_got, m1
    )
    inc1_got = swap(inc1, 0)
    (share,) = small(core_share_kernel, [(16, 8, R)], "core_share", 10**5)(inc1, inc1_got)
    share = exchange(share, (3, 4, 5, 6))
    products = rows_down(
        me, slot_frame, leaf_sizes, leaf_basis, part, local, tmat, inc1, inc1_got, core_got, m0
    )
    (curvature,) = small(all_share_kernel, [(8, R)], "all_share", 10**5)(share)
    return products, curvature[0:3].reshape(V)


def solution(mesh):
    return jax.shard_map(
        shards,
        mesh=mesh,
        in_specs=(
            P("leaf", None),
            P("leaf"),
            P("leaf", None),
            P("leaf", None, None),
            P("leaf", None, None),
            P("leaf", None, None, None),
            P("leaf", None, None, None),
            P("leaf", None, None, None),
            P("leaf", None, None, None),
        ),
        out_specs=(P("leaf", None), P()),
        check_vma=False,
    )
```

```python
import functools

import jax
import jax.numpy as jnp
from jax import lax
from jax.experimental import pallas as pl
from jax.experimental.pallas import tpu as pltpu
from jax.sharding import PartitionSpec as P

LEAF = 512
NL = 8
R = 128
V = 384
HALF = V // 2
QUART = HALF // 4
ROWS = NL * LEAF
S = 4
MB = 128
BT = 16
UN = 32
F32 = jnp.float32
BF16 = jnp.bfloat16
MIB = 1 << 20


def split(a):
    hi = a.astype(BF16)
    return hi, (a - hi.astype(F32)).astype(BF16)


def dot3s(terms, ca, cb):
    lhs, rhs = [], []
    for (ah, al), (bh, bl) in terms:
        lhs += [ah, ah, al]
        rhs += [bh, bl, bh]
    return lax.dot_general(
        jnp.concatenate(lhs, axis=ca),
        jnp.concatenate(rhs, axis=cb),
        (((ca,), (cb,)), ((), ())),
        preferred_element_type=F32,
    )


def dot3(a, b, ca=1, cb=0):
    return dot3s([(split(a), split(b))], ca, cb)


def tile_rows(start, count):
    return pl.ds(pl.multiple_of(start * S, S), count * S)


def far(x):
    return pltpu.with_memory_space_constraint(x, pltpu.HBM)


def lane_rows(p):
    parts = [p[0:1, 128 * k : 128 * k + 128] for k in range(3)]
    return jnp.concatenate(parts + [jnp.zeros((5, 128), F32)], axis=0)


def row_sums(z):
    zh, zl = split(z)
    ones = jnp.ones((8, 2 * R), BF16)
    return lax.dot_general(
        ones, jnp.concatenate([zh, zl], axis=1), (((1,), (1,)), ((), ())),
        preferred_element_type=F32,
    )


def rows_up_kernel(
    slot_hbm, sizes_hbm, v_hbm, basis_hbm, trans_hbm, near_hbm, upper_hbm,
    part_hbm, call_hbm, pay_ref, curv_ref, lift_ref,
    slot, sizes, vbuf, vt, xt, basis, trans, near, xh, xl, call_ref, upper,
    sem, vsem, nsem, osem,
):
    copies = [
        pltpu.make_async_copy(slot_hbm, slot, sem.at[0]),
        pltpu.make_async_copy(sizes_hbm, sizes, sem.at[1]),
        pltpu.make_async_copy(basis_hbm, basis, sem.at[2]),
        pltpu.make_async_copy(trans_hbm, trans, sem.at[3]),
        pltpu.make_async_copy(upper_hbm.at[pl.ds(0, 2)], upper, sem.at[4]),
    ]
    chunks = [
        pltpu.make_async_copy(
            v_hbm.at[pl.ds(c * LEAF, LEAF)], vbuf.at[pl.ds(c * LEAF, LEAF)], vsem.at[c]
        )
        for c in range(NL)
    ]
    copies[0].start()
    copies[1].start()
    for c in range(NL):
        chunks[c].start()
    nears = [
        pltpu.make_async_copy(near_hbm.at[leaf], near.at[leaf], nsem.at[leaf]) for leaf in range(NL)
    ]
    for c in range(NL):
        chunks[c].wait()
        if c == NL - 2:
            copies[2].start()
            for n in nears:
                n.start()
            copies[3].start()
            copies[4].start()

        def spread(i, _, c=c):
            for u in range(8):
                base = pl.multiple_of(c * LEAF + i * 64 + u * 8, 8)
                for k in range(3):
                    vt[pl.ds(pl.multiple_of(base * S, 8) + k, 8, stride=S), :] = vbuf[
                        pl.ds(base, 8), 128 * k : 128 * k + 128
                    ]
            return 0

        lax.fori_loop(0, LEAF // 64, spread, 0)
    copies[0].wait()
    copies[1].wait()
    for leaf in range(NL):

        def pick(i, _, leaf=leaf):
            base = pl.multiple_of(leaf * LEAF + i * UN, UN)
            rows = [vt[tile_rows(slot[base + r], 1), :] for r in range(UN)]
            for r in range(UN):
                xt[tile_rows(base + r, 1), :] = rows[r]
            return 0

        lax.fori_loop(0, (sizes[0, leaf] + UN - 1) // UN, pick, 0)
    copies[2].wait()
    for c in nears[0:4]:
        c.wait()
    lane_row = lax.broadcasted_iota(jnp.int32, (8, 128), 0)

    def pack(leaf, first=0, last=LEAF):
        size = sizes[0, leaf]
        for base in range(first, last, 16):
            for k in range(3):
                pieces = []
                for half in (0, 8):
                    val = xt[pl.ds((leaf * LEAF + base + half) * S + k, 8, stride=S), :]
                    pieces.append(jnp.where(lane_row < size - (base + half), val, 0.0))
                hi, lo = split(jnp.concatenate(pieces, axis=0))
                xh[leaf, base : base + 16, 128 * k : 128 * k + 128] = hi
                xl[leaf, base : base + 16, 128 * k : 128 * k + 128] = lo

    outs = []
    coeffs = []
    total = jnp.zeros((1, V), F32)
    pack(0)
    for leaf in range(NL):
        x = (xh[leaf], xl[leaf])
        c = dot3s([(split(basis[leaf]), x)], 0, 0)
        call_ref[leaf] = c
        coeffs.append(split(c))
        for blk in range(LEAF // MB):
            rows = slice(MB * blk, MB * blk + MB)
            prod = dot3s([(split(near[leaf, rows, :]), x)], 1, 0)
            xb = xh[leaf, rows, :].astype(F32) + xl[leaf, rows, :].astype(F32)
            total += jnp.sum(prod * xb, axis=0, keepdims=True)
            vbuf[leaf * LEAF + MB * blk : leaf * LEAF + MB * blk + MB, :] = prod
            if leaf + 1 < NL:
                pack(leaf + 1, MB * blk, MB * blk + MB)
        if leaf % 2 == 1:
            for n in range(leaf - 1, leaf + 1):
                cp = pltpu.make_async_copy(
                    vbuf.at[pl.ds(n * LEAF, LEAF)], part_hbm.at[n], osem.at[n]
                )
                cp.start()
                outs.append(cp)
        if leaf == 3:
            for cp in nears[4:]:
                cp.wait()
    copies[3].wait()
    copies[4].wait()
    offset, at = 0, NL
    while len(coeffs) > 1:
        parents = []
        for m in range(len(coeffs) // 2):
            terms = [(split(trans[offset + 2 * m + t]), coeffs[2 * m + t]) for t in range(2)]
            c = dot3s(terms, 0, 0)
            parents.append(c)
            if len(coeffs) > 2:
                call_ref[at] = c
                at += 1
        offset += len(coeffs)
        coeffs = [split(c) for c in parents]
    cp = pltpu.make_async_copy(call_ref, call_hbm, osem.at[NL])
    cp.start()
    outs.append(cp)
    curv_ref[...] = jnp.broadcast_to(total, (8, V))
    pay_ref[0] = parents[0].T
    lift = dot3s([(coeffs[0], split(trans[2 * NL - 2]))], 0, 0)
    pay_ref[1] = lift
    lift_ref[...] = dot3(dot3(lift, upper[0]), upper[1])
    for cp in outs:
        cp.wait()


def rows_up(slot, sizes, vectors, basis, trans, near, upper):
    hbm = pl.BlockSpec(memory_space=pltpu.HBM)
    vmem = pl.BlockSpec(memory_space=pltpu.VMEM)
    return pl.pallas_call(
        rows_up_kernel,
        out_shape=(
            pltpu.HBM((NL, LEAF, V), F32),
            pltpu.HBM((14, R, V), F32),
            jax.ShapeDtypeStruct((2, V, R), F32),
            jax.ShapeDtypeStruct((8, V), F32),
            jax.ShapeDtypeStruct((V, R), F32),
        ),
        in_specs=[hbm] * 7,
        out_specs=(hbm, hbm, vmem, vmem, vmem),
        scratch_shapes=[
            pltpu.SMEM((ROWS,), jnp.int32),
            pltpu.SMEM((1, NL), jnp.int32),
            pltpu.VMEM((ROWS, V), F32),
            pltpu.VMEM((ROWS * S, 128), F32),
            pltpu.VMEM((ROWS * S, 128), F32),
            pltpu.VMEM((NL, LEAF, R), F32),
            pltpu.VMEM((2 * NL - 1, R, R), F32),
            pltpu.VMEM((NL, LEAF, LEAF), F32),
            pltpu.VMEM((NL, LEAF, V), BF16),
            pltpu.VMEM((NL, LEAF, V), BF16),
            pltpu.VMEM((14, R, V), F32),
            pltpu.VMEM((2, R, R), F32),
            pltpu.SemaphoreType.DMA((5,)),
            pltpu.SemaphoreType.DMA((NL,)),
            pltpu.SemaphoreType.DMA((NL,)),
            pltpu.SemaphoreType.DMA((NL + 1,)),
        ],
        compiler_params=pltpu.CompilerParams(vmem_limit_bytes=50 * MIB),
        cost_estimate=pl.CostEstimate(flops=7 * 10**9, bytes_accessed=28 * 10**6, transcendentals=0),
        name="rows_up",
    )(far(slot), far(sizes), far(vectors), far(basis), far(trans), far(near), far(upper))


def fields_kernel(
    me, call_hbm, trans_hbm, coup_hbm,
    pay_ref, got_ref, pair2_ref, pair_got_ref, c2_ref, m0_ref, m1_ref, near_ref,
    inc_ref, tmat_ref, curv_ref, call_ref, trans_ref, coup_ref, z, sem,
):
    copies = [
        pltpu.make_async_copy(call_hbm, call_ref, sem.at[0]),
        pltpu.make_async_copy(trans_hbm, trans_ref, sem.at[1]),
        pltpu.make_async_copy(coup_hbm, coup_ref, sem.at[2]),
    ]
    for c in copies:
        c.start()
    z[...] = pay_ref[0] * dot3(got_ref[0], m0_ref[0:R])
    start = pl.multiple_of((me[0] % 2) * HALF, HALF)
    z[pl.ds(start, HALF), :] += pair2_ref[0] * dot3(pair_got_ref[0], m1_ref[0:R])
    for c in copies:
        c.wait()
    total = jnp.zeros((1, V), F32)
    starts = (0, 8, 12)
    fields = [None] * 14
    pair = 0
    for height in range(3):
        for m in range(4 >> height):
            a = starts[height] + 2 * m
            bm = split(coup_ref[pair])
            ca, cb = call_ref[a], call_ref[a + 1]
            fields[a] = dot3s([(bm, split(cb))], 1, 0)
            fields[a + 1] = dot3s([(bm, split(ca))], 0, 0)
            total += 2.0 * jnp.sum(ca * fields[a], axis=0, keepdims=True)
            pair += 1
    curv_ref[...] = near_ref[...] + row_sums(z[...]) + jnp.broadcast_to(total, (8, V))
    top = [split(fields[12 + m]) for m in range(2)]
    tops = [split(trans_ref[12 + m]) for m in range(2)]
    for m in range(4):
        w = split(trans_ref[8 + m])
        mid = split(fields[8 + m] + dot3s([(w, top[m // 2])], 1, 0))
        tmid = split(dot3s([(w, tops[m // 2])], 1, 0))
        for n in (2 * m, 2 * m + 1):
            wl = split(trans_ref[n])
            inc_ref[n] = fields[n] + dot3s([(wl, mid)], 1, 0)
            tmat_ref[n] = dot3s([(wl, tmid)], 1, 0)


def fields(me, call, trans, coup, *rest):
    vmem = pl.BlockSpec(memory_space=pltpu.VMEM)
    hbm = pl.BlockSpec(memory_space=pltpu.HBM)
    smem = pl.BlockSpec(memory_space=pltpu.SMEM)
    return pl.pallas_call(
        fields_kernel,
        out_shape=(
            pltpu.HBM((NL, R, V), F32),
            pltpu.HBM((NL, R, R), F32),
            jax.ShapeDtypeStruct((8, V), F32),
        ),
        in_specs=[smem, hbm, hbm, hbm] + [vmem] * len(rest),
        out_specs=(vmem, vmem, vmem),
        scratch_shapes=[
            pltpu.VMEM((14, R, V), F32),
            pltpu.VMEM((2 * NL - 1, R, R), F32),
            pltpu.VMEM((NL - 1, R, R), F32),
            pltpu.VMEM((V, R), F32),
            pltpu.SemaphoreType.DMA((3,)),
        ],
        compiler_params=pltpu.CompilerParams(vmem_limit_bytes=24 * MIB),
        cost_estimate=pl.CostEstimate(flops=2 * 10**9, bytes_accessed=8 * 10**6, transcendentals=0),
        name="fields",
    )(me, far(call), far(trans), far(coup), *rest)


def chains_kernel(
    me, trans_hbm, upper_hbm, pair_hbm, a1_ref, a2_ref, m0_ref, m1_ref, m3_ref, side2_ref,
    trans_ref, upper_ref, pair_ref, sem,
):
    dev = me[0]
    copies = [
        pltpu.make_async_copy(trans_hbm.at[pl.ds(2 * NL - 2, 1)], trans_ref, sem.at[0]),
        pltpu.make_async_copy(upper_hbm, upper_ref, sem.at[1]),
        pltpu.make_async_copy(pair_hbm, pair_ref, sem.at[2]),
    ]
    for c in copies:
        c.start()
    for c in copies:
        c.wait()

    def side(level):
        b = pair_ref[level]
        return jnp.where((dev >> level) % 2 == 0, b, b.T)

    m0_ref[0:R] = side(0).T
    m0_ref[R : 2 * R] = trans_ref[0].T
    w1 = upper_ref[0]
    w12 = dot3(w1, upper_ref[1])
    a1_ref[...] = w1
    m1_ref[0:R] = side(1).T
    m1_ref[R : 2 * R] = dot3(w1, side(2)).T
    m1_ref[2 * R : 3 * R] = w12.T
    w3 = upper_ref[2]
    w34 = dot3(w3, upper_ref[3])
    w345 = dot3(w34, upper_ref[4])
    a2_ref[:, 0:R] = w3
    a2_ref[:, R : 2 * R] = w34
    a2_ref[:, 2 * R : 3 * R] = w345
    m3_ref[0:R] = side(3).T
    m3_ref[R : 2 * R] = dot3(w3, side(4)).T
    m3_ref[2 * R : 3 * R] = dot3(w34, side(5)).T
    m3_ref[3 * R : 4 * R] = dot3(w345, side(6)).T
    side2_ref[...] = side(2).T


def after_core_kernel(me, pay_ref, got_ref, a1_ref, pair2_ref):
    start = pl.multiple_of((me[0] % 2) * HALF, HALF)
    c1 = pay_ref[1, pl.ds(start, HALF), :] + got_ref[1, pl.ds(start, HALF), :]
    pair2_ref[0] = c1
    pair2_ref[1] = dot3(c1, a1_ref[...])


def after_y_kernel(me, got_ref, a2_ref, send_ref, c3_ref):
    c3 = got_ref[0:QUART]
    for n in range(1, 8):
        c3 = c3 + got_ref[n * QUART : (n + 1) * QUART]
    c3_ref[...] = c3
    x = dot3(c3, a2_ref[...])
    parts = [c3, x[:, 0:R], x[:, R : 2 * R], x[:, 2 * R : 3 * R]]
    group = me[0] // 8
    for s in range(16):
        d = jnp.bitwise_xor(group, s)
        send_ref[s * QUART : (s + 1) * QUART] = jnp.where(
            d >= 8, parts[3], jnp.where(d >= 4, parts[2], jnp.where(d >= 2, parts[1], parts[0]))
        )


def after_top_kernel(
    me, got_ref, m3_ref, side2_ref, c2_ref, quad_got_ref, c3_ref, local_ref, send_ref, z
):
    dev = me[0]
    group = dev // 8
    sums = [jnp.zeros((QUART, R), F32) for _ in range(4)]
    bounds = ((1, 2), (2, 4), (4, 8), (8, 16))
    for s in range(16):
        d = jnp.bitwise_xor(group, s)
        val = got_ref[s * QUART : (s + 1) * QUART]
        for j, (low, high) in enumerate(bounds):
            sums[j] += jnp.where(jnp.logical_and(d >= low, d < high), val, 0.0)
    inc3 = dot3(jnp.concatenate(sums, axis=1), m3_ref[...])
    z[...] = jnp.zeros((V, R), F32)
    start = pl.multiple_of((dev % 2) * HALF, HALF)
    z[pl.ds(start, HALF), :] = 0.5 * (c2_ref[...] * dot3(quad_got_ref[...], side2_ref[...]))
    at = pl.multiple_of((dev % 8) * QUART, QUART)
    z[pl.ds(at, QUART), :] += c3_ref[...] * inc3
    share = lane_rows(local_ref[...] + row_sums(z[...]))
    for n in range(8):
        send_ref[n, 0:QUART] = inc3
        send_ref[n, QUART : QUART + 8] = share


def after_pair_kernel(pair2_ref, got_ref, c2_ref):
    c2_ref[...] = pair2_ref[1] + got_ref[1]


def pair_field_kernel(pair_got_ref, quad_got_ref, m1_ref, out_ref):
    sums = jnp.concatenate([pair_got_ref[0], quad_got_ref[...]], axis=1)
    out_ref[...] = dot3(sums, m1_ref[0 : 2 * R])


def part_share_kernel(got_ref, send_ref):
    share = got_ref[0, QUART : QUART + 8]
    for n in range(1, 8):
        share = share + got_ref[n, QUART : QUART + 8]
    for n in range(16):
        send_ref[n] = share


def all_share_kernel(got_ref, out_ref):
    total = got_ref[0]
    for n in range(1, 16):
        total = total + got_ref[n]
    total = total * (1.0 / (2.0 * LEAF))
    for k in range(3):
        out_ref[128 * k : 128 * k + 128] = total[k]


def small(body, outs, name, flops, scratch=(), hbm_args=()):
    vmem = pl.BlockSpec(memory_space=pltpu.VMEM)
    smem = pl.BlockSpec(memory_space=pltpu.SMEM)
    hbm = pl.BlockSpec(memory_space=pltpu.HBM)

    def call(*args):
        return pl.pallas_call(
            body,
            out_shape=tuple(jax.ShapeDtypeStruct(o, F32) for o in outs),
            in_specs=[
                smem if a.dtype == jnp.int32 else (hbm if n in hbm_args else vmem)
                for n, a in enumerate(args)
            ],
            out_specs=tuple(vmem for _ in outs),
            scratch_shapes=list(scratch),
            compiler_params=pltpu.CompilerParams(vmem_limit_bytes=16 * MIB),
            cost_estimate=pl.CostEstimate(flops=flops, bytes_accessed=10**6, transcendentals=0),
            name=name,
        )(*args)

    return call


def rows_down_kernel(
    me, slot_hbm, sizes_hbm, basis_hbm, part_hbm, local_hbm, tmat_hbm,
    own_ref, other_ref, inc3_ref, got_ref, m0_ref, m1_ref, out_hbm,
    slot, sizes, basis, part, local_ref, tmat_ref, ot, pt, res, inct, sem, psem, osem,
):
    copies = [
        pltpu.make_async_copy(slot_hbm, slot, sem.at[0]),
        pltpu.make_async_copy(sizes_hbm, sizes, sem.at[1]),
        pltpu.make_async_copy(tmat_hbm, tmat_ref, sem.at[2]),
        pltpu.make_async_copy(local_hbm, local_ref, sem.at[3]),
        pltpu.make_async_copy(basis_hbm, basis, sem.at[4]),
    ]
    for c in copies:
        c.start()
    loads = [
        pltpu.make_async_copy(part_hbm.at[leaf], part.at[leaf], psem.at[leaf]) for leaf in range(NL)
    ]
    for c in loads:
        c.start()
    half = me[0] % 2
    inct[pl.ds(pl.multiple_of(half * HALF, HALF), HALF), :] = own_ref[...]
    inct[pl.ds(pl.multiple_of((1 - half) * HALF, HALF), HALF), :] = other_ref[...]
    inc3 = jnp.concatenate([inc3_ref[n, 0:QUART] for n in range(8)], axis=0)
    inc1 = inct[...] + dot3(inc3, m1_ref[2 * R : 3 * R])
    root = dot3(jnp.concatenate([got_ref[0], inc1], axis=1), m0_ref[...])
    rsplit = split(root.T)
    for c in copies:
        c.wait()
    incs = [
        split(local_ref[leaf] + dot3s([(split(tmat_ref[leaf]), rsplit)], 1, 0)) for leaf in range(NL)
    ]
    for c in loads:
        c.wait()
    lane_row = lax.broadcasted_iota(jnp.int32, (8, 128), 0)

    def place(leaf, first, last):
        for base in range(leaf * LEAF + first, leaf * LEAF + last, BT):
            rows = [ot[at * S : at * S + S, :] for at in range(base, base + BT)]
            for r in range(BT):
                pt[tile_rows(slot[base + r], 1), :] = rows[r]

    for leaf in range(NL):
        size = sizes[0, leaf]
        for blk in range(LEAF // 128):
            rows = slice(128 * blk, 128 * blk + 128)
            val = part[leaf, rows, :] + dot3s([(split(basis[leaf, rows, :]), incs[leaf])], 1, 0)
            for b in range(16):
                keep = lane_row < size - (128 * blk + 8 * b)
                for k in range(3):
                    ot[pl.ds((leaf * LEAF + 128 * blk + 8 * b) * S + k, 8, stride=S), :] = jnp.where(
                        keep, val[8 * b : 8 * b + 8, 128 * k : 128 * k + 128], 0.0
                    )
            if leaf > 0:
                place(leaf - 1, 128 * blk, 128 * blk + 128)
    place(NL - 1, 0, LEAF)
    stores = []
    for c in range(NL):

        def flat(i, _, c=c):
            for u in range(16):
                base = pl.multiple_of(c * LEAF + i * 128 + u * 8, 8)
                for k in range(3):
                    res[pl.ds(base, 8), 128 * k : 128 * k + 128] = pt[
                        pl.ds(pl.multiple_of(base * S, 8) + k, 8, stride=S), :
                    ]
            return 0

        lax.fori_loop(0, LEAF // 128, flat, 0)
        cp = pltpu.make_async_copy(
            res.at[pl.ds(c * LEAF, LEAF)], out_hbm.at[pl.ds(c * LEAF, LEAF)], osem.at[c]
        )
        cp.start()
        stores.append(cp)
    for cp in stores:
        cp.wait()


def rows_down(me, slot, sizes, basis, part, local, tmat, *rest):
    hbm = pl.BlockSpec(memory_space=pltpu.HBM)
    vmem = pl.BlockSpec(memory_space=pltpu.VMEM)
    smem = pl.BlockSpec(memory_space=pltpu.SMEM)
    return pl.pallas_call(
        rows_down_kernel,
        out_shape=pltpu.HBM((ROWS, V), F32),
        in_specs=[smem] + [hbm] * 6 + [vmem] * len(rest),
        out_specs=hbm,
        scratch_shapes=[
            pltpu.SMEM((ROWS,), jnp.int32),
            pltpu.SMEM((1, NL), jnp.int32),
            pltpu.VMEM((NL, LEAF, R), F32),
            pltpu.VMEM((NL, LEAF, V), F32),
            pltpu.VMEM((NL, R, V), F32),
            pltpu.VMEM((NL, R, R), F32),
            pltpu.VMEM((ROWS * S, 128), F32),
            pltpu.VMEM((ROWS * S, 128), F32),
            pltpu.VMEM((ROWS, V), F32),
            pltpu.VMEM((V, R), F32),
            pltpu.SemaphoreType.DMA((5,)),
            pltpu.SemaphoreType.DMA((NL,)),
            pltpu.SemaphoreType.DMA((NL,)),
        ],
        compiler_params=pltpu.CompilerParams(vmem_limit_bytes=44 * MIB),
        cost_estimate=pl.CostEstimate(flops=2 * 10**9, bytes_accessed=16 * 10**6, transcendentals=0),
        name="rows_down",
    )(me, far(slot), far(sizes), far(basis), far(part), far(local), far(tmat), *rest)


def groups_of(bits, count):
    masks = [sum(1 << b for i, b in enumerate(bits) if k >> i & 1) for k in range(1 << len(bits))]
    full = masks[-1]
    return [[base | m for m in masks] for base in range(count) if base & full == 0]


def shards(
    vectors, slot_frame, leaf_sizes, near_field, leaf_basis,
    local_transfer, local_coupling, upper_transfer, pair_coupling,
):
    count = lax.axis_size("leaf")
    me = lax.axis_index("leaf").astype(jnp.int32).reshape(1)

    def swap(value, level):
        return lax.ppermute(value, "leaf", [(s, s ^ (1 << level)) for s in range(count)])

    def exchange(value, bits):
        return lax.all_to_all(
            value, "leaf", 0, 0, axis_index_groups=groups_of(bits, count), tiled=True
        )

    trans, coup, upper, pairs = (
        local_transfer[0], local_coupling[0], upper_transfer[0], pair_coupling[0],
    )
    a1, a2, m0, m1, m3, side2 = small(
        chains_kernel,
        [(R, R), (R, 3 * R), (2 * R, R), (3 * R, R), (4 * R, R), (R, R)],
        "chains",
        10**8,
        [
            pltpu.VMEM((1, R, R), F32),
            pltpu.VMEM((5, R, R), F32),
            pltpu.VMEM((7, R, R), F32),
            pltpu.SemaphoreType.DMA((3,)),
        ],
        (1, 2, 3),
    )(me, far(trans), far(upper), far(pairs))
    part, call, pay, curv, lift3 = rows_up(
        slot_frame, leaf_sizes, vectors, leaf_basis, trans, near_field, upper
    )
    core_got = swap(pay, 0)
    y_got = exchange(lift3, (0, 1, 2))
    (pair2,) = small(after_core_kernel, [(2, HALF, R)], "after_core", 10**8)(me, pay, core_got, a1)
    pair_got = swap(pair2, 1)
    top_send, c3 = small(after_y_kernel, [(16 * QUART, R), (QUART, R)], "after_y", 10**8)(
        me, y_got, a2
    )
    top_got = exchange(top_send, (3, 4, 5, 6))
    (c2,) = small(after_pair_kernel, [(HALF, R)], "after_pair", 10**6)(pair2, pair_got)
    quad_got = swap(c2, 2)
    local, tmat, curv = fields(
        me, call, trans, coup, pay, core_got, pair2, pair_got, c2, m0, m1, curv
    )
    (field1,) = small(pair_field_kernel, [(HALF, R)], "pair_field", 10**8)(pair_got, quad_got, m1)
    field1_got = swap(field1, 0)
    (inc3,) = small(
        after_top_kernel, [(8, QUART + 8, R)], "after_top", 10**8, [pltpu.VMEM((V, R), F32)]
    )(me, top_got, m3, side2, c2, quad_got, c3, curv)
    inc3_got = exchange(inc3, (0, 1, 2))
    (share,) = small(part_share_kernel, [(16, 8, R)], "part_share", 10**5)(inc3_got)
    share = exchange(share, (3, 4, 5, 6))
    products = rows_down(
        me, slot_frame, leaf_sizes, leaf_basis, part, local, tmat,
        field1, field1_got, inc3_got, core_got, m0, m1,
    )
    (curvature,) = small(all_share_kernel, [(V,)], "all_share", 10**5)(share)
    return products, curvature


def solution(mesh):
    return jax.shard_map(
        shards,
        mesh=mesh,
        in_specs=(
            P("leaf", None),
            P("leaf"),
            P("leaf", None),
            P("leaf", None, None),
            P("leaf", None, None),
            P("leaf", None, None, None),
            P("leaf", None, None, None),
            P("leaf", None, None, None),
            P("leaf", None, None, None),
        ),
        out_specs=(P("leaf", None), P()),
        check_vma=False,
    )
```

```python
import functools

import jax
import jax.numpy as jnp
from jax import lax
from jax.experimental import pallas as pl
from jax.experimental.pallas import tpu as pltpu
from jax.sharding import PartitionSpec as P

LEAF = 512
NL = 8
R = 128
V = 384
HALF = V // 2
QUART = HALF // 4
ROWS = NL * LEAF
S = 4
MB = 128
BT = 16
UN = 32
F32 = jnp.float32
BF16 = jnp.bfloat16
MIB = 1 << 20


def split(a):
    hi = a.astype(BF16)
    return hi, (a - hi.astype(F32)).astype(BF16)


def dot3s(terms, ca, cb):
    lhs, rhs = [], []
    for (ah, al), (bh, bl) in terms:
        lhs += [ah, ah, al]
        rhs += [bh, bl, bh]
    return lax.dot_general(
        jnp.concatenate(lhs, axis=ca),
        jnp.concatenate(rhs, axis=cb),
        (((ca,), (cb,)), ((), ())),
        preferred_element_type=F32,
    )


def dot3(a, b, ca=1, cb=0):
    return dot3s([(split(a), split(b))], ca, cb)


def tile_rows(start, count):
    return pl.ds(pl.multiple_of(start * S, S), count * S)


def far(x):
    return pltpu.with_memory_space_constraint(x, pltpu.HBM)


def lane_rows(p):
    parts = [p[0:1, 128 * k : 128 * k + 128] for k in range(3)]
    return jnp.concatenate(parts + [jnp.zeros((5, 128), F32)], axis=0)


def row_sums(z):
    zh, zl = split(z)
    ones = jnp.ones((8, 2 * R), BF16)
    return lax.dot_general(
        ones, jnp.concatenate([zh, zl], axis=1), (((1,), (1,)), ((), ())),
        preferred_element_type=F32,
    )


def rows_up_kernel(
    slot_hbm, sizes_hbm, v_hbm, basis_hbm, trans_hbm, near_hbm, upper_hbm,
    part_hbm, call_hbm, pay_ref, curv_ref, lift_ref,
    slot, sizes, vbuf, vt, xt, basis, trans, near, xh, xl, call_ref, upper,
    sem, vsem, nsem, osem,
):
    copies = [
        pltpu.make_async_copy(slot_hbm, slot, sem.at[0]),
        pltpu.make_async_copy(sizes_hbm, sizes, sem.at[1]),
        pltpu.make_async_copy(basis_hbm, basis, sem.at[2]),
        pltpu.make_async_copy(trans_hbm, trans, sem.at[3]),
        pltpu.make_async_copy(upper_hbm.at[pl.ds(0, 2)], upper, sem.at[4]),
    ]
    chunks = [
        pltpu.make_async_copy(
            v_hbm.at[pl.ds(c * LEAF, LEAF)], vbuf.at[pl.ds(c * LEAF, LEAF)], vsem.at[c]
        )
        for c in range(NL)
    ]
    copies[0].start()
    copies[1].start()
    for c in range(NL):
        chunks[c].start()
    nears = [
        pltpu.make_async_copy(near_hbm.at[leaf], near.at[leaf], nsem.at[leaf]) for leaf in range(NL)
    ]
    for c in range(NL):
        chunks[c].wait()
        if c == NL - 2:
            copies[2].start()
            for n in nears:
                n.start()
            copies[3].start()
            copies[4].start()

        def spread(i, _, c=c):
            for u in range(8):
                base = pl.multiple_of(c * LEAF + i * 64 + u * 8, 8)
                for k in range(3):
                    vt[pl.ds(pl.multiple_of(base * S, 8) + k, 8, stride=S), :] = vbuf[
                        pl.ds(base, 8), 128 * k : 128 * k + 128
                    ]
            return 0

        lax.fori_loop(0, LEAF // 64, spread, 0)
    copies[0].wait()
    copies[1].wait()
    for leaf in range(NL):

        def pick(i, _, leaf=leaf):
            base = pl.multiple_of(leaf * LEAF + i * UN, UN)
            rows = [vt[tile_rows(slot[base + r], 1), :] for r in range(UN)]
            for r in range(UN):
                xt[tile_rows(base + r, 1), :] = rows[r]
            return 0

        lax.fori_loop(0, (sizes[0, leaf] + UN - 1) // UN, pick, 0)
    copies[2].wait()
    for c in nears[0:4]:
        c.wait()
    lane_row = lax.broadcasted_iota(jnp.int32, (8, 128), 0)

    def pack(leaf, first=0, last=LEAF):
        size = sizes[0, leaf]
        for base in range(first, last, 16):
            for k in range(3):
                pieces = []
                for half in (0, 8):
                    val = xt[pl.ds((leaf * LEAF + base + half) * S + k, 8, stride=S), :]
                    pieces.append(jnp.where(lane_row < size - (base + half), val, 0.0))
                hi, lo = split(jnp.concatenate(pieces, axis=0))
                xh[leaf, base : base + 16, 128 * k : 128 * k + 128] = hi
                xl[leaf, base : base + 16, 128 * k : 128 * k + 128] = lo

    outs = []
    coeffs = []
    total = jnp.zeros((1, V), F32)
    pack(0)
    for leaf in range(NL):
        x = (xh[leaf], xl[leaf])
        c = dot3s([(split(basis[leaf]), x)], 0, 0)
        call_ref[leaf] = c
        coeffs.append(split(c))
        for blk in range(LEAF // MB):
            rows = slice(MB * blk, MB * blk + MB)
            prod = dot3s([(split(near[leaf, rows, :]), x)], 1, 0)
            xb = xh[leaf, rows, :].astype(F32) + xl[leaf, rows, :].astype(F32)
            total += jnp.sum(prod * xb, axis=0, keepdims=True)
            vbuf[leaf * LEAF + MB * blk : leaf * LEAF + MB * blk + MB, :] = prod
            if leaf + 1 < NL:
                pack(leaf + 1, MB * blk, MB * blk + MB)
        if leaf % 2 == 1:
            for n in range(leaf - 1, leaf + 1):
                cp = pltpu.make_async_copy(
                    vbuf.at[pl.ds(n * LEAF, LEAF)], part_hbm.at[n], osem.at[n]
                )
                cp.start()
                outs.append(cp)
        if leaf == 3:
            for cp in nears[4:]:
                cp.wait()
    copies[3].wait()
    copies[4].wait()
    offset, at = 0, NL
    while len(coeffs) > 1:
        parents = []
        for m in range(len(coeffs) // 2):
            terms = [(split(trans[offset + 2 * m + t]), coeffs[2 * m + t]) for t in range(2)]
            c = dot3s(terms, 0, 0)
            parents.append(c)
            if len(coeffs) > 2:
                call_ref[at] = c
                at += 1
        offset += len(coeffs)
        coeffs = [split(c) for c in parents]
    cp = pltpu.make_async_copy(call_ref, call_hbm, osem.at[NL])
    cp.start()
    outs.append(cp)
    curv_ref[...] = jnp.broadcast_to(total, (8, V))
    pay_ref[0] = parents[0].T
    lift = dot3s([(coeffs[0], split(trans[2 * NL - 2]))], 0, 0)
    pay_ref[1] = lift
    lift_ref[...] = dot3(dot3(lift, upper[0]), upper[1])
    for cp in outs:
        cp.wait()


def rows_up(slot, sizes, vectors, basis, trans, near, upper):
    hbm = pl.BlockSpec(memory_space=pltpu.HBM)
    vmem = pl.BlockSpec(memory_space=pltpu.VMEM)
    return pl.pallas_call(
        rows_up_kernel,
        out_shape=(
            pltpu.HBM((NL, LEAF, V), F32),
            pltpu.HBM((14, R, V), F32),
            jax.ShapeDtypeStruct((2, V, R), F32),
            jax.ShapeDtypeStruct((8, V), F32),
            jax.ShapeDtypeStruct((V, R), F32),
        ),
        in_specs=[hbm] * 7,
        out_specs=(hbm, hbm, vmem, vmem, vmem),
        scratch_shapes=[
            pltpu.SMEM((ROWS,), jnp.int32),
            pltpu.SMEM((1, NL), jnp.int32),
            pltpu.VMEM((ROWS, V), F32),
            pltpu.VMEM((ROWS * S, 128), F32),
            pltpu.VMEM((ROWS * S, 128), F32),
            pltpu.VMEM((NL, LEAF, R), F32),
            pltpu.VMEM((2 * NL - 1, R, R), F32),
            pltpu.VMEM((NL, LEAF, LEAF), F32),
            pltpu.VMEM((NL, LEAF, V), BF16),
            pltpu.VMEM((NL, LEAF, V), BF16),
            pltpu.VMEM((14, R, V), F32),
            pltpu.VMEM((2, R, R), F32),
            pltpu.SemaphoreType.DMA((5,)),
            pltpu.SemaphoreType.DMA((NL,)),
            pltpu.SemaphoreType.DMA((NL,)),
            pltpu.SemaphoreType.DMA((NL + 1,)),
        ],
        compiler_params=pltpu.CompilerParams(vmem_limit_bytes=50 * MIB),
        cost_estimate=pl.CostEstimate(flops=7 * 10**9, bytes_accessed=28 * 10**6, transcendentals=0),
        name="rows_up",
    )(far(slot), far(sizes), far(vectors), far(basis), far(trans), far(near), far(upper))


def fields_kernel(
    me, call_hbm, coup_hbm,
    pay_ref, got_ref, pair2_ref, pair_got_ref, c2_ref, m0_ref, m1_ref, near_ref,
    field_hbm, curv_ref, call_ref, coup_ref, field_ref, z, sem,
):
    copies = [
        pltpu.make_async_copy(call_hbm, call_ref, sem.at[0]),
        pltpu.make_async_copy(coup_hbm, coup_ref, sem.at[1]),
    ]
    for c in copies:
        c.start()
    z[...] = pay_ref[0] * dot3(got_ref[0], m0_ref[0:R])
    start = pl.multiple_of((me[0] % 2) * HALF, HALF)
    z[pl.ds(start, HALF), :] += pair2_ref[0] * dot3(pair_got_ref[0], m1_ref[0:R])
    for c in copies:
        c.wait()
    total = jnp.zeros((1, V), F32)
    starts = (0, 8, 12)
    pair = 0
    outs = []
    for height in range(3):
        for m in range(4 >> height):
            a = starts[height] + 2 * m
            bm = split(coup_ref[pair])
            ca, cb = call_ref[a], call_ref[a + 1]
            left = dot3s([(bm, split(cb))], 1, 0)
            field_ref[a] = left
            field_ref[a + 1] = dot3s([(bm, split(ca))], 0, 0)
            total += 2.0 * jnp.sum(ca * left, axis=0, keepdims=True)
            pair += 1
        if height != 1:
            cp = pltpu.make_async_copy(
                field_ref.at[pl.ds(0, 8) if height == 0 else pl.ds(8, 6)],
                field_hbm.at[pl.ds(0, 8) if height == 0 else pl.ds(8, 6)],
                sem.at[2 + height // 2],
            )
            cp.start()
            outs.append(cp)
    curv_ref[...] = near_ref[...] + row_sums(z[...]) + jnp.broadcast_to(total, (8, V))
    for cp in outs:
        cp.wait()


def fields(me, call, coup, *rest):
    vmem = pl.BlockSpec(memory_space=pltpu.VMEM)
    hbm = pl.BlockSpec(memory_space=pltpu.HBM)
    smem = pl.BlockSpec(memory_space=pltpu.SMEM)
    return pl.pallas_call(
        fields_kernel,
        out_shape=(pltpu.HBM((14, R, V), F32), jax.ShapeDtypeStruct((8, V), F32)),
        in_specs=[smem, hbm, hbm] + [vmem] * len(rest),
        out_specs=(hbm, vmem),
        scratch_shapes=[
            pltpu.VMEM((14, R, V), F32),
            pltpu.VMEM((NL - 1, R, R), F32),
            pltpu.VMEM((14, R, V), F32),
            pltpu.VMEM((V, R), F32),
            pltpu.SemaphoreType.DMA((4,)),
        ],
        compiler_params=pltpu.CompilerParams(vmem_limit_bytes=24 * MIB),
        cost_estimate=pl.CostEstimate(flops=2 * 10**9, bytes_accessed=16 * 10**6, transcendentals=0),
        name="fields",
    )(me, far(call), far(coup), *rest)


def paths_kernel(field_hbm, trans_hbm, after_ref, inc_hbm, tmat_hbm, field, trans, inc, tmat, sem):
    copies = [
        pltpu.make_async_copy(trans_hbm, trans, sem.at[0]),
        pltpu.make_async_copy(field_hbm, field, sem.at[1]),
    ]
    for c in copies:
        c.start()
    copies[0].wait()
    tops = [split(trans[12 + m]) for m in range(2)]
    for m in range(4):
        tmid = split(dot3s([(split(trans[8 + m]), tops[m // 2])], 1, 0))
        for n in (2 * m, 2 * m + 1):
            tmat[n] = dot3s([(split(trans[n]), tmid)], 1, 0)
    outs = [pltpu.make_async_copy(tmat, tmat_hbm, sem.at[2]), pltpu.make_async_copy(inc, inc_hbm, sem.at[3])]
    outs[0].start()
    copies[1].wait()
    top = [split(field[12 + m]) for m in range(2)]
    for m in range(4):
        mid = split(field[8 + m] + dot3s([(split(trans[8 + m]), top[m // 2])], 1, 0))
        for n in (2 * m, 2 * m + 1):
            inc[n] = field[n] + dot3s([(split(trans[n]), mid)], 1, 0)
    outs[1].start()
    for cp in outs:
        cp.wait()


def paths(field, trans, after):
    hbm = pl.BlockSpec(memory_space=pltpu.HBM)
    return pl.pallas_call(
        paths_kernel,
        out_shape=(pltpu.HBM((NL, R, V), F32), pltpu.HBM((NL, R, R), F32)),
        in_specs=[hbm, hbm, pl.BlockSpec(memory_space=pl.ANY)],
        out_specs=(hbm, hbm),
        scratch_shapes=[
            pltpu.VMEM((14, R, V), F32),
            pltpu.VMEM((2 * NL - 1, R, R), F32),
            pltpu.VMEM((NL, R, V), F32),
            pltpu.VMEM((NL, R, R), F32),
            pltpu.SemaphoreType.DMA((4,)),
        ],
        compiler_params=pltpu.CompilerParams(vmem_limit_bytes=24 * MIB),
        cost_estimate=pl.CostEstimate(flops=10**9, bytes_accessed=6 * 10**6, transcendentals=0),
        name="paths",
    )(far(field), far(trans), after)


def chains_kernel(
    me, trans_hbm, upper_hbm, pair_hbm, a1_ref, a2_ref, m0_ref, m1_ref, m3_ref, side2_ref,
    trans_ref, upper_ref, pair_ref, sem,
):
    dev = me[0]
    copies = [
        pltpu.make_async_copy(trans_hbm.at[pl.ds(2 * NL - 2, 1)], trans_ref, sem.at[0]),
        pltpu.make_async_copy(upper_hbm, upper_ref, sem.at[1]),
        pltpu.make_async_copy(pair_hbm, pair_ref, sem.at[2]),
    ]
    for c in copies:
        c.start()
    for c in copies:
        c.wait()

    def side(level):
        b = pair_ref[level]
        return jnp.where((dev >> level) % 2 == 0, b, b.T)

    m0_ref[0:R] = side(0).T
    m0_ref[R : 2 * R] = trans_ref[0].T
    w1 = upper_ref[0]
    w12 = dot3(w1, upper_ref[1])
    a1_ref[...] = w1
    m1_ref[0:R] = side(1).T
    m1_ref[R : 2 * R] = dot3(w1, side(2)).T
    m1_ref[2 * R : 3 * R] = w12.T
    w3 = upper_ref[2]
    w34 = dot3(w3, upper_ref[3])
    w345 = dot3(w34, upper_ref[4])
    a2_ref[:, 0:R] = w3
    a2_ref[:, R : 2 * R] = w34
    a2_ref[:, 2 * R : 3 * R] = w345
    m3_ref[0:R] = side(3).T
    m3_ref[R : 2 * R] = dot3(w3, side(4)).T
    m3_ref[2 * R : 3 * R] = dot3(w34, side(5)).T
    m3_ref[3 * R : 4 * R] = dot3(w345, side(6)).T
    side2_ref[...] = side(2).T


def after_core_kernel(me, pay_ref, got_ref, a1_ref, pair2_ref):
    start = pl.multiple_of((me[0] % 2) * HALF, HALF)
    c1 = pay_ref[1, pl.ds(start, HALF), :] + got_ref[1, pl.ds(start, HALF), :]
    pair2_ref[0] = c1
    pair2_ref[1] = dot3(c1, a1_ref[...])


def after_y_kernel(me, got_ref, a2_ref, pair2_ref, send_ref, c3_ref):
    c3 = got_ref[0:QUART]
    for n in range(1, 8):
        c3 = c3 + got_ref[n * QUART : (n + 1) * QUART]
    c3_ref[...] = c3
    x = dot3(c3, a2_ref[...])
    parts = [c3, x[:, 0:R], x[:, R : 2 * R], x[:, 2 * R : 3 * R]]
    group = me[0] // 8
    for s in range(16):
        d = jnp.bitwise_xor(group, s)
        send_ref[s * QUART : (s + 1) * QUART] = jnp.where(
            d >= 8, parts[3], jnp.where(d >= 4, parts[2], jnp.where(d >= 2, parts[1], parts[0]))
        )


def after_top_kernel(
    me, got_ref, m3_ref, side2_ref, c2_ref, quad_got_ref, c3_ref, local_ref, send_ref, z
):
    dev = me[0]
    group = dev // 8
    sums = [jnp.zeros((QUART, R), F32) for _ in range(4)]
    bounds = ((1, 2), (2, 4), (4, 8), (8, 16))
    for s in range(16):
        d = jnp.bitwise_xor(group, s)
        val = got_ref[s * QUART : (s + 1) * QUART]
        for j, (low, high) in enumerate(bounds):
            sums[j] += jnp.where(jnp.logical_and(d >= low, d < high), val, 0.0)
    inc3 = dot3(jnp.concatenate(sums, axis=1), m3_ref[...])
    z[...] = jnp.zeros((V, R), F32)
    start = pl.multiple_of((dev % 2) * HALF, HALF)
    z[pl.ds(start, HALF), :] = 0.5 * (c2_ref[...] * dot3(quad_got_ref[...], side2_ref[...]))
    at = pl.multiple_of((dev % 8) * QUART, QUART)
    z[pl.ds(at, QUART), :] += c3_ref[...] * inc3
    share = lane_rows(local_ref[...] + row_sums(z[...]))
    for n in range(8):
        send_ref[n, 0:QUART] = inc3
        send_ref[n, QUART : QUART + 8] = share


def after_pair_kernel(pair2_ref, got_ref, c2_ref):
    c2_ref[...] = pair2_ref[1] + got_ref[1]


def pair_field_kernel(pair_got_ref, quad_got_ref, m1_ref, out_ref):
    sums = jnp.concatenate([pair_got_ref[0], quad_got_ref[...]], axis=1)
    out_ref[...] = dot3(sums, m1_ref[0 : 2 * R])


def part_share_kernel(got_ref, send_ref):
    share = got_ref[0, QUART : QUART + 8]
    for n in range(1, 8):
        share = share + got_ref[n, QUART : QUART + 8]
    for n in range(16):
        send_ref[n] = share


def all_share_kernel(got_ref, out_ref):
    total = got_ref[0]
    for n in range(1, 16):
        total = total + got_ref[n]
    total = total * (1.0 / (2.0 * LEAF))
    for k in range(3):
        out_ref[128 * k : 128 * k + 128] = total[k]


def small(body, outs, name, flops, scratch=(), hbm_args=()):
    vmem = pl.BlockSpec(memory_space=pltpu.VMEM)
    smem = pl.BlockSpec(memory_space=pltpu.SMEM)
    hbm = pl.BlockSpec(memory_space=pltpu.HBM)

    def call(*args):
        return pl.pallas_call(
            body,
            out_shape=tuple(jax.ShapeDtypeStruct(o, F32) for o in outs),
            in_specs=[
                smem if a.dtype == jnp.int32 else (hbm if n in hbm_args else vmem)
                for n, a in enumerate(args)
            ],
            out_specs=tuple(vmem for _ in outs),
            scratch_shapes=list(scratch),
            compiler_params=pltpu.CompilerParams(vmem_limit_bytes=16 * MIB),
            cost_estimate=pl.CostEstimate(flops=flops, bytes_accessed=10**6, transcendentals=0),
            name=name,
        )(*args)

    return call


def rows_down_kernel(
    me, slot_hbm, sizes_hbm, basis_hbm, part_hbm, local_hbm, tmat_hbm,
    own_ref, other_ref, inc3_ref, got_ref, m0_ref, m1_ref, out_hbm,
    slot, sizes, basis, part, local_ref, tmat_ref, ot, pt, res, inct, sem, psem, osem,
):
    copies = [
        pltpu.make_async_copy(slot_hbm, slot, sem.at[0]),
        pltpu.make_async_copy(sizes_hbm, sizes, sem.at[1]),
        pltpu.make_async_copy(tmat_hbm, tmat_ref, sem.at[2]),
        pltpu.make_async_copy(local_hbm, local_ref, sem.at[3]),
        pltpu.make_async_copy(basis_hbm, basis, sem.at[4]),
    ]
    for c in copies:
        c.start()
    loads = [
        pltpu.make_async_copy(part_hbm.at[leaf], part.at[leaf], psem.at[leaf]) for leaf in range(NL)
    ]
    for c in loads:
        c.start()
    half = me[0] % 2
    inct[pl.ds(pl.multiple_of(half * HALF, HALF), HALF), :] = own_ref[...]
    inct[pl.ds(pl.multiple_of((1 - half) * HALF, HALF), HALF), :] = other_ref[...]
    inc3 = jnp.concatenate([inc3_ref[n, 0:QUART] for n in range(8)], axis=0)
    inc1 = inct[...] + dot3(inc3, m1_ref[2 * R : 3 * R])
    root = dot3(jnp.concatenate([got_ref[0], inc1], axis=1), m0_ref[...])
    rsplit = split(root.T)
    for c in copies:
        c.wait()
    incs = [
        split(local_ref[leaf] + dot3s([(split(tmat_ref[leaf]), rsplit)], 1, 0)) for leaf in range(NL)
    ]
    for c in loads:
        c.wait()
    lane_row = lax.broadcasted_iota(jnp.int32, (8, 128), 0)

    def place(leaf, first, last):
        for base in range(leaf * LEAF + first, leaf * LEAF + last, BT):
            rows = [ot[at * S : at * S + S, :] for at in range(base, base + BT)]
            for r in range(BT):
                pt[tile_rows(slot[base + r], 1), :] = rows[r]

    for leaf in range(NL):
        size = sizes[0, leaf]
        for blk in range(LEAF // 128):
            rows = slice(128 * blk, 128 * blk + 128)
            val = part[leaf, rows, :] + dot3s([(split(basis[leaf, rows, :]), incs[leaf])], 1, 0)
            for b in range(16):
                keep = lane_row < size - (128 * blk + 8 * b)
                for k in range(3):
                    ot[pl.ds((leaf * LEAF + 128 * blk + 8 * b) * S + k, 8, stride=S), :] = jnp.where(
                        keep, val[8 * b : 8 * b + 8, 128 * k : 128 * k + 128], 0.0
                    )
            if leaf > 0:
                place(leaf - 1, 128 * blk, 128 * blk + 128)
    place(NL - 1, 0, LEAF)
    stores = []
    for c in range(NL):

        def flat(i, _, c=c):
            for u in range(16):
                base = pl.multiple_of(c * LEAF + i * 128 + u * 8, 8)
                for k in range(3):
                    res[pl.ds(base, 8), 128 * k : 128 * k + 128] = pt[
                        pl.ds(pl.multiple_of(base * S, 8) + k, 8, stride=S), :
                    ]
            return 0

        lax.fori_loop(0, LEAF // 128, flat, 0)
        cp = pltpu.make_async_copy(
            res.at[pl.ds(c * LEAF, LEAF)], out_hbm.at[pl.ds(c * LEAF, LEAF)], osem.at[c]
        )
        cp.start()
        stores.append(cp)
    for cp in stores:
        cp.wait()


def rows_down(me, slot, sizes, basis, part, local, tmat, *rest):
    hbm = pl.BlockSpec(memory_space=pltpu.HBM)
    vmem = pl.BlockSpec(memory_space=pltpu.VMEM)
    smem = pl.BlockSpec(memory_space=pltpu.SMEM)
    return pl.pallas_call(
        rows_down_kernel,
        out_shape=pltpu.HBM((ROWS, V), F32),
        in_specs=[smem] + [hbm] * 6 + [vmem] * len(rest),
        out_specs=hbm,
        scratch_shapes=[
            pltpu.SMEM((ROWS,), jnp.int32),
            pltpu.SMEM((1, NL), jnp.int32),
            pltpu.VMEM((NL, LEAF, R), F32),
            pltpu.VMEM((NL, LEAF, V), F32),
            pltpu.VMEM((NL, R, V), F32),
            pltpu.VMEM((NL, R, R), F32),
            pltpu.VMEM((ROWS * S, 128), F32),
            pltpu.VMEM((ROWS * S, 128), F32),
            pltpu.VMEM((ROWS, V), F32),
            pltpu.VMEM((V, R), F32),
            pltpu.SemaphoreType.DMA((5,)),
            pltpu.SemaphoreType.DMA((NL,)),
            pltpu.SemaphoreType.DMA((NL,)),
        ],
        compiler_params=pltpu.CompilerParams(vmem_limit_bytes=44 * MIB),
        cost_estimate=pl.CostEstimate(flops=2 * 10**9, bytes_accessed=16 * 10**6, transcendentals=0),
        name="rows_down",
    )(me, far(slot), far(sizes), far(basis), far(part), far(local), far(tmat), *rest)


def groups_of(bits, count):
    masks = [sum(1 << b for i, b in enumerate(bits) if k >> i & 1) for k in range(1 << len(bits))]
    full = masks[-1]
    return [[base | m for m in masks] for base in range(count) if base & full == 0]


def shards(
    vectors, slot_frame, leaf_sizes, near_field, leaf_basis,
    local_transfer, local_coupling, upper_transfer, pair_coupling,
):
    count = lax.axis_size("leaf")
    me = lax.axis_index("leaf").astype(jnp.int32).reshape(1)

    def swap(value, level):
        return lax.ppermute(value, "leaf", [(s, s ^ (1 << level)) for s in range(count)])

    def exchange(value, bits):
        return lax.all_to_all(
            value, "leaf", 0, 0, axis_index_groups=groups_of(bits, count), tiled=True
        )

    trans, coup, upper, pairs = (
        local_transfer[0], local_coupling[0], upper_transfer[0], pair_coupling[0],
    )
    a1, a2, m0, m1, m3, side2 = small(
        chains_kernel,
        [(R, R), (R, 3 * R), (2 * R, R), (3 * R, R), (4 * R, R), (R, R)],
        "chains",
        10**8,
        [
            pltpu.VMEM((1, R, R), F32),
            pltpu.VMEM((5, R, R), F32),
            pltpu.VMEM((7, R, R), F32),
            pltpu.SemaphoreType.DMA((3,)),
        ],
        (1, 2, 3),
    )(me, far(trans), far(upper), far(pairs))
    part, call, pay, curv, lift3 = rows_up(
        slot_frame, leaf_sizes, vectors, leaf_basis, trans, near_field, upper
    )
    core_got = swap(pay, 0)
    y_got = exchange(lift3, (0, 1, 2))
    (pair2,) = small(after_core_kernel, [(2, HALF, R)], "after_core", 10**8)(me, pay, core_got, a1)
    pair_got = swap(pair2, 1)
    top_send, c3 = small(after_y_kernel, [(16 * QUART, R), (QUART, R)], "after_y", 10**8)(
        me, y_got, a2, pair2
    )
    top_got = exchange(top_send, (3, 4, 5, 6))
    (c2,) = small(after_pair_kernel, [(HALF, R)], "after_pair", 10**6)(pair2, pair_got)
    quad_got = swap(c2, 2)
    field, curv = fields(me, call, coup, pay, core_got, pair2, pair_got, c2, m0, m1, curv)
    (field1,) = small(pair_field_kernel, [(HALF, R)], "pair_field", 10**8)(pair_got, quad_got, m1)
    field1_got = swap(field1, 0)
    (inc3,) = small(
        after_top_kernel, [(8, QUART + 8, R)], "after_top", 10**8, [pltpu.VMEM((V, R), F32)]
    )(me, top_got, m3, side2, c2, quad_got, c3, curv)
    inc3_got = exchange(inc3, (0, 1, 2))
    local, tmat = paths(field, trans, field1)
    (share,) = small(part_share_kernel, [(16, 8, R)], "part_share", 10**5)(inc3_got)
    share = exchange(share, (3, 4, 5, 6))
    products = rows_down(
        me, slot_frame, leaf_sizes, leaf_basis, part, local, tmat,
        field1, field1_got, inc3_got, core_got, m0, m1,
    )
    (curvature,) = small(all_share_kernel, [(V,)], "all_share", 10**5)(share)
    return products, curvature


def solution(mesh):
    return jax.shard_map(
        shards,
        mesh=mesh,
        in_specs=(
            P("leaf", None),
            P("leaf"),
            P("leaf", None),
            P("leaf", None, None),
            P("leaf", None, None),
            P("leaf", None, None, None),
            P("leaf", None, None, None),
            P("leaf", None, None, None),
            P("leaf", None, None, None),
        ),
        out_specs=(P("leaf", None), P()),
        check_vma=False,
    )
```

```python
import functools

import jax
import jax.numpy as jnp
from jax import lax
from jax.experimental import pallas as pl
from jax.experimental.pallas import tpu as pltpu
from jax.sharding import PartitionSpec as P

LEAF = 512
NL = 8
R = 128
V = 384
HALF = V // 2
QUART = HALF // 4
ROWS = NL * LEAF
S = 4
MB = 128
BT = 16
UN = 64
F32 = jnp.float32
BF16 = jnp.bfloat16
MIB = 1 << 20


def split(a):
    hi = a.astype(BF16)
    return hi, (a - hi.astype(F32)).astype(BF16)


def dot3s(terms, ca, cb):
    lhs, rhs = [], []
    for (ah, al), (bh, bl) in terms:
        lhs += [ah, ah, al]
        rhs += [bh, bl, bh]
    return lax.dot_general(
        jnp.concatenate(lhs, axis=ca),
        jnp.concatenate(rhs, axis=cb),
        (((ca,), (cb,)), ((), ())),
        preferred_element_type=F32,
    )


def dot3(a, b, ca=1, cb=0):
    return dot3s([(split(a), split(b))], ca, cb)


def tile_rows(start, count):
    return pl.ds(pl.multiple_of(start * S, S), count * S)


def far(x):
    return pltpu.with_memory_space_constraint(x, pltpu.HBM)


def lane_rows(p):
    parts = [p[0:1, 128 * k : 128 * k + 128] for k in range(3)]
    return jnp.concatenate(parts + [jnp.zeros((5, 128), F32)], axis=0)


def row_sums(z):
    zh, zl = split(z)
    ones = jnp.ones((8, 2 * R), BF16)
    return lax.dot_general(
        ones, jnp.concatenate([zh, zl], axis=1), (((1,), (1,)), ((), ())),
        preferred_element_type=F32,
    )


def rows_up_kernel(
    slot_hbm, sizes_hbm, v_hbm, basis_hbm, trans_hbm, near_hbm, upper_hbm,
    part_hbm, call_hbm, pay_ref, curv_ref, lift_ref,
    slot, sizes, vbuf, vt, xt, basis, trans, near, xh, xl, call_ref, upper,
    sem, vsem, nsem, osem,
):
    copies = [
        pltpu.make_async_copy(slot_hbm, slot, sem.at[0]),
        pltpu.make_async_copy(sizes_hbm, sizes, sem.at[1]),
        pltpu.make_async_copy(basis_hbm, basis, sem.at[2]),
        pltpu.make_async_copy(trans_hbm, trans, sem.at[3]),
        pltpu.make_async_copy(upper_hbm.at[pl.ds(0, 2)], upper, sem.at[4]),
    ]
    chunks = [
        pltpu.make_async_copy(
            v_hbm.at[pl.ds(c * LEAF, LEAF)], vbuf.at[pl.ds(c * LEAF, LEAF)], vsem.at[c]
        )
        for c in range(NL)
    ]
    copies[0].start()
    copies[1].start()
    for c in range(NL):
        chunks[c].start()
    nears = [
        pltpu.make_async_copy(near_hbm.at[leaf], near.at[leaf], nsem.at[leaf]) for leaf in range(NL)
    ]
    for c in range(NL):
        chunks[c].wait()
        if c == NL - 2:
            copies[2].start()
            for n in nears:
                n.start()
            copies[3].start()
            copies[4].start()

        def spread(i, _, c=c):
            for u in range(8):
                base = pl.multiple_of(c * LEAF + i * 64 + u * 8, 8)
                for k in range(3):
                    vt[pl.ds(pl.multiple_of(base * S, 8) + k, 8, stride=S), :] = vbuf[
                        pl.ds(base, 8), 128 * k : 128 * k + 128
                    ]
            return 0

        lax.fori_loop(0, LEAF // 64, spread, 0)
    copies[0].wait()
    copies[1].wait()
    for leaf in range(NL):

        def pick(i, _, leaf=leaf):
            base = pl.multiple_of(leaf * LEAF + i * UN, UN)
            rows = [vt[tile_rows(slot[base + r], 1), :] for r in range(UN)]
            for r in range(UN):
                xt[tile_rows(base + r, 1), :] = rows[r]
            return 0

        lax.fori_loop(0, (sizes[0, leaf] + UN - 1) // UN, pick, 0)
    copies[2].wait()
    for c in nears[0:4]:
        c.wait()
    lane_row = lax.broadcasted_iota(jnp.int32, (8, 128), 0)

    def pack(leaf, first=0, last=LEAF):
        size = sizes[0, leaf]
        for base in range(first, last, 16):
            for k in range(3):
                pieces = []
                for half in (0, 8):
                    val = xt[pl.ds((leaf * LEAF + base + half) * S + k, 8, stride=S), :]
                    pieces.append(jnp.where(lane_row < size - (base + half), val, 0.0))
                hi, lo = split(jnp.concatenate(pieces, axis=0))
                xh[leaf, base : base + 16, 128 * k : 128 * k + 128] = hi
                xl[leaf, base : base + 16, 128 * k : 128 * k + 128] = lo

    outs = []
    coeffs = []
    total = jnp.zeros((1, V), F32)
    pack(0)
    for leaf in range(NL):
        x = (xh[leaf], xl[leaf])
        c = dot3s([(split(basis[leaf]), x)], 0, 0)
        call_ref[leaf] = c
        coeffs.append(split(c))
        for blk in range(LEAF // MB):
            rows = slice(MB * blk, MB * blk + MB)
            prod = dot3s([(split(near[leaf, rows, :]), x)], 1, 0)
            xb = xh[leaf, rows, :].astype(F32) + xl[leaf, rows, :].astype(F32)
            total += jnp.sum(prod * xb, axis=0, keepdims=True)
            vbuf[leaf * LEAF + MB * blk : leaf * LEAF + MB * blk + MB, :] = prod
            if leaf + 1 < NL:
                pack(leaf + 1, MB * blk, MB * blk + MB)
        if leaf % 2 == 1:
            for n in range(leaf - 1, leaf + 1):
                cp = pltpu.make_async_copy(
                    vbuf.at[pl.ds(n * LEAF, LEAF)], part_hbm.at[n], osem.at[n]
                )
                cp.start()
                outs.append(cp)
        if leaf == 3:
            for cp in nears[4:]:
                cp.wait()
    cp = pltpu.make_async_copy(call_ref.at[pl.ds(0, NL)], call_hbm.at[pl.ds(0, NL)], osem.at[NL + 1])
    cp.start()
    outs.append(cp)
    copies[3].wait()
    copies[4].wait()
    offset, at = 0, NL
    while len(coeffs) > 1:
        parents = []
        for m in range(len(coeffs) // 2):
            terms = [(split(trans[offset + 2 * m + t]), coeffs[2 * m + t]) for t in range(2)]
            c = dot3s(terms, 0, 0)
            parents.append(c)
            if len(coeffs) > 2:
                call_ref[at] = c
                at += 1
        offset += len(coeffs)
        coeffs = [split(c) for c in parents]
    cp = pltpu.make_async_copy(call_ref.at[pl.ds(NL, 6)], call_hbm.at[pl.ds(NL, 6)], osem.at[NL])
    cp.start()
    outs.append(cp)
    curv_ref[...] = jnp.broadcast_to(total, (8, V))
    pay_ref[0] = parents[0].T
    lift = dot3s([(coeffs[0], split(trans[2 * NL - 2]))], 0, 0)
    pay_ref[1] = lift
    lift_ref[...] = dot3(dot3(lift, upper[0]), upper[1])
    for cp in outs:
        cp.wait()


def rows_up(slot, sizes, vectors, basis, trans, near, upper):
    hbm = pl.BlockSpec(memory_space=pltpu.HBM)
    vmem = pl.BlockSpec(memory_space=pltpu.VMEM)
    return pl.pallas_call(
        rows_up_kernel,
        out_shape=(
            pltpu.HBM((NL, LEAF, V), F32),
            pltpu.HBM((14, R, V), F32),
            jax.ShapeDtypeStruct((2, V, R), F32),
            jax.ShapeDtypeStruct((8, V), F32),
            jax.ShapeDtypeStruct((V, R), F32),
        ),
        in_specs=[hbm] * 7,
        out_specs=(hbm, hbm, vmem, vmem, vmem),
        scratch_shapes=[
            pltpu.SMEM((ROWS,), jnp.int32),
            pltpu.SMEM((1, NL), jnp.int32),
            pltpu.VMEM((ROWS, V), F32),
            pltpu.VMEM((ROWS * S, 128), F32),
            pltpu.VMEM((ROWS * S, 128), F32),
            pltpu.VMEM((NL, LEAF, R), F32),
            pltpu.VMEM((2 * NL - 1, R, R), F32),
            pltpu.VMEM((NL, LEAF, LEAF), F32),
            pltpu.VMEM((NL, LEAF, V), BF16),
            pltpu.VMEM((NL, LEAF, V), BF16),
            pltpu.VMEM((14, R, V), F32),
            pltpu.VMEM((2, R, R), F32),
            pltpu.SemaphoreType.DMA((5,)),
            pltpu.SemaphoreType.DMA((NL,)),
            pltpu.SemaphoreType.DMA((NL,)),
            pltpu.SemaphoreType.DMA((NL + 2,)),
        ],
        compiler_params=pltpu.CompilerParams(vmem_limit_bytes=50 * MIB),
        cost_estimate=pl.CostEstimate(flops=7 * 10**9, bytes_accessed=28 * 10**6, transcendentals=0),
        name="rows_up",
    )(far(slot), far(sizes), far(vectors), far(basis), far(trans), far(near), far(upper))


def fields_kernel(
    me, call_hbm, coup_hbm,
    pay_ref, got_ref, pair2_ref, pair_got_ref, c2_ref, m0_ref, m1_ref, near_ref,
    field_hbm, curv_ref, call_ref, coup_ref, field_ref, z, sem,
):
    copies = [
        pltpu.make_async_copy(call_hbm, call_ref, sem.at[0]),
        pltpu.make_async_copy(coup_hbm, coup_ref, sem.at[1]),
    ]
    for c in copies:
        c.start()
    z[...] = pay_ref[0] * dot3(got_ref[0], m0_ref[0:R])
    start = pl.multiple_of((me[0] % 2) * HALF, HALF)
    z[pl.ds(start, HALF), :] += pair2_ref[0] * dot3(pair_got_ref[0], m1_ref[0:R])
    for c in copies:
        c.wait()
    total = jnp.zeros((1, V), F32)
    starts = (0, 8, 12)
    pair = 0
    outs = []
    for height in range(3):
        for m in range(4 >> height):
            a = starts[height] + 2 * m
            bm = split(coup_ref[pair])
            ca, cb = call_ref[a], call_ref[a + 1]
            left = dot3s([(bm, split(cb))], 1, 0)
            field_ref[a] = left
            field_ref[a + 1] = dot3s([(bm, split(ca))], 0, 0)
            total += 2.0 * jnp.sum(ca * left, axis=0, keepdims=True)
            pair += 1
        if height != 1:
            cp = pltpu.make_async_copy(
                field_ref.at[pl.ds(0, 8) if height == 0 else pl.ds(8, 6)],
                field_hbm.at[pl.ds(0, 8) if height == 0 else pl.ds(8, 6)],
                sem.at[2 + height // 2],
            )
            cp.start()
            outs.append(cp)
    curv_ref[...] = near_ref[...] + row_sums(z[...]) + jnp.broadcast_to(total, (8, V))
    for cp in outs:
        cp.wait()


def fields(me, call, coup, *rest):
    vmem = pl.BlockSpec(memory_space=pltpu.VMEM)
    hbm = pl.BlockSpec(memory_space=pltpu.HBM)
    smem = pl.BlockSpec(memory_space=pltpu.SMEM)
    return pl.pallas_call(
        fields_kernel,
        out_shape=(pltpu.HBM((14, R, V), F32), jax.ShapeDtypeStruct((8, V), F32)),
        in_specs=[smem, hbm, hbm] + [vmem] * len(rest),
        out_specs=(hbm, vmem),
        scratch_shapes=[
            pltpu.VMEM((14, R, V), F32),
            pltpu.VMEM((NL - 1, R, R), F32),
            pltpu.VMEM((14, R, V), F32),
            pltpu.VMEM((V, R), F32),
            pltpu.SemaphoreType.DMA((4,)),
        ],
        compiler_params=pltpu.CompilerParams(vmem_limit_bytes=24 * MIB),
        cost_estimate=pl.CostEstimate(flops=2 * 10**9, bytes_accessed=16 * 10**6, transcendentals=0),
        name="fields",
    )(me, far(call), far(coup), *rest)


def paths_kernel(field_hbm, trans_hbm, after_ref, inc_hbm, tmat_hbm, field, trans, inc, tmat, sem):
    copies = [
        pltpu.make_async_copy(trans_hbm, trans, sem.at[0]),
        pltpu.make_async_copy(field_hbm, field, sem.at[1]),
    ]
    for c in copies:
        c.start()
    copies[0].wait()
    tops = [split(trans[12 + m]) for m in range(2)]
    for m in range(4):
        tmid = split(dot3s([(split(trans[8 + m]), tops[m // 2])], 1, 0))
        for n in (2 * m, 2 * m + 1):
            tmat[n] = dot3s([(split(trans[n]), tmid)], 1, 0)
    outs = [pltpu.make_async_copy(tmat, tmat_hbm, sem.at[2]), pltpu.make_async_copy(inc, inc_hbm, sem.at[3])]
    outs[0].start()
    copies[1].wait()
    top = [split(field[12 + m]) for m in range(2)]
    for m in range(4):
        mid = split(field[8 + m] + dot3s([(split(trans[8 + m]), top[m // 2])], 1, 0))
        for n in (2 * m, 2 * m + 1):
            inc[n] = field[n] + dot3s([(split(trans[n]), mid)], 1, 0)
    outs[1].start()
    for cp in outs:
        cp.wait()


def paths(field, trans, after):
    hbm = pl.BlockSpec(memory_space=pltpu.HBM)
    return pl.pallas_call(
        paths_kernel,
        out_shape=(pltpu.HBM((NL, R, V), F32), pltpu.HBM((NL, R, R), F32)),
        in_specs=[hbm, hbm, pl.BlockSpec(memory_space=pl.ANY)],
        out_specs=(hbm, hbm),
        scratch_shapes=[
            pltpu.VMEM((14, R, V), F32),
            pltpu.VMEM((2 * NL - 1, R, R), F32),
            pltpu.VMEM((NL, R, V), F32),
            pltpu.VMEM((NL, R, R), F32),
            pltpu.SemaphoreType.DMA((4,)),
        ],
        compiler_params=pltpu.CompilerParams(vmem_limit_bytes=24 * MIB),
        cost_estimate=pl.CostEstimate(flops=10**9, bytes_accessed=6 * 10**6, transcendentals=0),
        name="paths",
    )(far(field), far(trans), after)


def chains_kernel(
    me, trans_hbm, upper_hbm, pair_hbm, a1_ref, a2_ref, m0_ref, m1_ref, m3_ref, side2_ref,
    trans_ref, upper_ref, pair_ref, sem,
):
    dev = me[0]
    copies = [
        pltpu.make_async_copy(trans_hbm.at[pl.ds(2 * NL - 2, 1)], trans_ref, sem.at[0]),
        pltpu.make_async_copy(upper_hbm, upper_ref, sem.at[1]),
        pltpu.make_async_copy(pair_hbm, pair_ref, sem.at[2]),
    ]
    for c in copies:
        c.start()
    for c in copies:
        c.wait()

    def side(level):
        b = pair_ref[level]
        return jnp.where((dev >> level) % 2 == 0, b, b.T)

    m0_ref[0:R] = side(0).T
    m0_ref[R : 2 * R] = trans_ref[0].T
    w1 = upper_ref[0]
    w12 = dot3(w1, upper_ref[1])
    a1_ref[...] = w1
    m1_ref[0:R] = side(1).T
    m1_ref[R : 2 * R] = dot3(w1, side(2)).T
    m1_ref[2 * R : 3 * R] = w12.T
    w3 = upper_ref[2]
    w34 = dot3(w3, upper_ref[3])
    w345 = dot3(w34, upper_ref[4])
    a2_ref[:, 0:R] = w3
    a2_ref[:, R : 2 * R] = w34
    a2_ref[:, 2 * R : 3 * R] = w345
    m3_ref[0:R] = side(3).T
    m3_ref[R : 2 * R] = dot3(w3, side(4)).T
    m3_ref[2 * R : 3 * R] = dot3(w34, side(5)).T
    m3_ref[3 * R : 4 * R] = dot3(w345, side(6)).T
    side2_ref[...] = side(2).T


def after_core_kernel(me, pay_ref, got_ref, a1_ref, pair2_ref):
    start = pl.multiple_of((me[0] % 2) * HALF, HALF)
    c1 = pay_ref[1, pl.ds(start, HALF), :] + got_ref[1, pl.ds(start, HALF), :]
    pair2_ref[0] = c1
    pair2_ref[1] = dot3(c1, a1_ref[...])


def after_y_kernel(me, got_ref, a2_ref, pair2_ref, send_ref, c3_ref):
    c3 = got_ref[0:QUART]
    for n in range(1, 8):
        c3 = c3 + got_ref[n * QUART : (n + 1) * QUART]
    c3_ref[...] = c3
    x = dot3(c3, a2_ref[...])
    parts = [c3, x[:, 0:R], x[:, R : 2 * R], x[:, 2 * R : 3 * R]]
    group = me[0] // 8
    for s in range(16):
        d = jnp.bitwise_xor(group, s)
        send_ref[s * QUART : (s + 1) * QUART] = jnp.where(
            d >= 8, parts[3], jnp.where(d >= 4, parts[2], jnp.where(d >= 2, parts[1], parts[0]))
        )


def after_top_kernel(
    me, got_ref, m3_ref, side2_ref, c2_ref, quad_got_ref, c3_ref, local_ref, send_ref, z
):
    dev = me[0]
    group = dev // 8
    sums = [jnp.zeros((QUART, R), F32) for _ in range(4)]
    bounds = ((1, 2), (2, 4), (4, 8), (8, 16))
    for s in range(16):
        d = jnp.bitwise_xor(group, s)
        val = got_ref[s * QUART : (s + 1) * QUART]
        for j, (low, high) in enumerate(bounds):
            sums[j] += jnp.where(jnp.logical_and(d >= low, d < high), val, 0.0)
    inc3 = dot3(jnp.concatenate(sums, axis=1), m3_ref[...])
    z[...] = jnp.zeros((V, R), F32)
    start = pl.multiple_of((dev % 2) * HALF, HALF)
    z[pl.ds(start, HALF), :] = 0.5 * (c2_ref[...] * dot3(quad_got_ref[...], side2_ref[...]))
    at = pl.multiple_of((dev % 8) * QUART, QUART)
    z[pl.ds(at, QUART), :] += c3_ref[...] * inc3
    share = lane_rows(local_ref[...] + row_sums(z[...]))
    for n in range(8):
        send_ref[n, 0:QUART] = inc3
        send_ref[n, QUART : QUART + 8] = share


def after_pair_kernel(pair2_ref, got_ref, c2_ref):
    c2_ref[...] = pair2_ref[1] + got_ref[1]


def pair_field_kernel(pair_got_ref, quad_got_ref, m1_ref, out_ref):
    sums = jnp.concatenate([pair_got_ref[0], quad_got_ref[...]], axis=1)
    out_ref[...] = dot3(sums, m1_ref[0 : 2 * R])


def part_share_kernel(got_ref, send_ref):
    share = got_ref[0, QUART : QUART + 8]
    for n in range(1, 8):
        share = share + got_ref[n, QUART : QUART + 8]
    for n in range(16):
        send_ref[n] = share


def all_share_kernel(got_ref, out_ref):
    total = got_ref[0]
    for n in range(1, 16):
        total = total + got_ref[n]
    total = total * (1.0 / (2.0 * LEAF))
    for k in range(3):
        out_ref[128 * k : 128 * k + 128] = total[k]


def small(body, outs, name, flops, scratch=(), hbm_args=()):
    vmem = pl.BlockSpec(memory_space=pltpu.VMEM)
    smem = pl.BlockSpec(memory_space=pltpu.SMEM)
    hbm = pl.BlockSpec(memory_space=pltpu.HBM)

    def call(*args):
        return pl.pallas_call(
            body,
            out_shape=tuple(jax.ShapeDtypeStruct(o, F32) for o in outs),
            in_specs=[
                smem if a.dtype == jnp.int32 else (hbm if n in hbm_args else vmem)
                for n, a in enumerate(args)
            ],
            out_specs=tuple(vmem for _ in outs),
            scratch_shapes=list(scratch),
            compiler_params=pltpu.CompilerParams(vmem_limit_bytes=16 * MIB),
            cost_estimate=pl.CostEstimate(flops=flops, bytes_accessed=10**6, transcendentals=0),
            name=name,
        )(*args)

    return call


def rows_down_kernel(
    me, slot_hbm, sizes_hbm, basis_hbm, part_hbm, local_hbm, tmat_hbm,
    own_ref, other_ref, inc3_ref, got_ref, m0_ref, m1_ref, out_hbm,
    slot, sizes, basis, part, local_ref, tmat_ref, ot, pt, res, inct, sem, psem, osem,
):
    copies = [
        pltpu.make_async_copy(slot_hbm, slot, sem.at[0]),
        pltpu.make_async_copy(sizes_hbm, sizes, sem.at[1]),
        pltpu.make_async_copy(tmat_hbm, tmat_ref, sem.at[2]),
        pltpu.make_async_copy(local_hbm, local_ref, sem.at[3]),
        pltpu.make_async_copy(basis_hbm, basis, sem.at[4]),
    ]
    for c in copies:
        c.start()
    loads = [
        pltpu.make_async_copy(part_hbm.at[leaf], part.at[leaf], psem.at[leaf]) for leaf in range(NL)
    ]
    for c in loads:
        c.start()
    half = me[0] % 2
    inct[pl.ds(pl.multiple_of(half * HALF, HALF), HALF), :] = own_ref[...]
    inct[pl.ds(pl.multiple_of((1 - half) * HALF, HALF), HALF), :] = other_ref[...]
    inc3 = jnp.concatenate([inc3_ref[n, 0:QUART] for n in range(8)], axis=0)
    inc1 = inct[...] + dot3(inc3, m1_ref[2 * R : 3 * R])
    root = dot3(jnp.concatenate([got_ref[0], inc1], axis=1), m0_ref[...])
    rsplit = split(root.T)
    for c in copies:
        c.wait()
    incs = [
        split(local_ref[leaf] + dot3s([(split(tmat_ref[leaf]), rsplit)], 1, 0)) for leaf in range(NL)
    ]
    for c in loads:
        c.wait()
    lane_row = lax.broadcasted_iota(jnp.int32, (8, 128), 0)

    def place(leaf, first, last):
        for base in range(leaf * LEAF + first, leaf * LEAF + last, BT):
            rows = [ot[at * S : at * S + S, :] for at in range(base, base + BT)]
            for r in range(BT):
                pt[tile_rows(slot[base + r], 1), :] = rows[r]

    for leaf in range(NL):
        size = sizes[0, leaf]
        for blk in range(LEAF // 128):
            rows = slice(128 * blk, 128 * blk + 128)
            val = part[leaf, rows, :] + dot3s([(split(basis[leaf, rows, :]), incs[leaf])], 1, 0)
            for b in range(16):
                keep = lane_row < size - (128 * blk + 8 * b)
                for k in range(3):
                    ot[pl.ds((leaf * LEAF + 128 * blk + 8 * b) * S + k, 8, stride=S), :] = jnp.where(
                        keep, val[8 * b : 8 * b + 8, 128 * k : 128 * k + 128], 0.0
                    )
            if leaf > 0:
                place(leaf - 1, 128 * blk, 128 * blk + 128)
    place(NL - 1, 0, LEAF)
    stores = []
    for c in range(NL):

        def flat(i, _, c=c):
            for u in range(16):
                base = pl.multiple_of(c * LEAF + i * 128 + u * 8, 8)
                for k in range(3):
                    res[pl.ds(base, 8), 128 * k : 128 * k + 128] = pt[
                        pl.ds(pl.multiple_of(base * S, 8) + k, 8, stride=S), :
                    ]
            return 0

        lax.fori_loop(0, LEAF // 128, flat, 0)
        cp = pltpu.make_async_copy(
            res.at[pl.ds(c * LEAF, LEAF)], out_hbm.at[pl.ds(c * LEAF, LEAF)], osem.at[c]
        )
        cp.start()
        stores.append(cp)
    for cp in stores:
        cp.wait()


def rows_down(me, slot, sizes, basis, part, local, tmat, *rest):
    hbm = pl.BlockSpec(memory_space=pltpu.HBM)
    vmem = pl.BlockSpec(memory_space=pltpu.VMEM)
    smem = pl.BlockSpec(memory_space=pltpu.SMEM)
    return pl.pallas_call(
        rows_down_kernel,
        out_shape=pltpu.HBM((ROWS, V), F32),
        in_specs=[smem] + [hbm] * 6 + [vmem] * len(rest),
        out_specs=hbm,
        scratch_shapes=[
            pltpu.SMEM((ROWS,), jnp.int32),
            pltpu.SMEM((1, NL), jnp.int32),
            pltpu.VMEM((NL, LEAF, R), F32),
            pltpu.VMEM((NL, LEAF, V), F32),
            pltpu.VMEM((NL, R, V), F32),
            pltpu.VMEM((NL, R, R), F32),
            pltpu.VMEM((ROWS * S, 128), F32),
            pltpu.VMEM((ROWS * S, 128), F32),
            pltpu.VMEM((ROWS, V), F32),
            pltpu.VMEM((V, R), F32),
            pltpu.SemaphoreType.DMA((5,)),
            pltpu.SemaphoreType.DMA((NL,)),
            pltpu.SemaphoreType.DMA((NL,)),
        ],
        compiler_params=pltpu.CompilerParams(vmem_limit_bytes=44 * MIB),
        cost_estimate=pl.CostEstimate(flops=2 * 10**9, bytes_accessed=16 * 10**6, transcendentals=0),
        name="rows_down",
    )(me, far(slot), far(sizes), far(basis), far(part), far(local), far(tmat), *rest)


def groups_of(bits, count):
    masks = [sum(1 << b for i, b in enumerate(bits) if k >> i & 1) for k in range(1 << len(bits))]
    full = masks[-1]
    return [[base | m for m in masks] for base in range(count) if base & full == 0]


def shards(
    vectors, slot_frame, leaf_sizes, near_field, leaf_basis,
    local_transfer, local_coupling, upper_transfer, pair_coupling,
):
    count = lax.axis_size("leaf")
    me = lax.axis_index("leaf").astype(jnp.int32).reshape(1)

    def swap(value, level):
        return lax.ppermute(value, "leaf", [(s, s ^ (1 << level)) for s in range(count)])

    def exchange(value, bits):
        return lax.all_to_all(
            value, "leaf", 0, 0, axis_index_groups=groups_of(bits, count), tiled=True
        )

    trans, coup, upper, pairs = (
        local_transfer[0], local_coupling[0], upper_transfer[0], pair_coupling[0],
    )
    a1, a2, m0, m1, m3, side2 = small(
        chains_kernel,
        [(R, R), (R, 3 * R), (2 * R, R), (3 * R, R), (4 * R, R), (R, R)],
        "chains",
        10**8,
        [
            pltpu.VMEM((1, R, R), F32),
            pltpu.VMEM((5, R, R), F32),
            pltpu.VMEM((7, R, R), F32),
            pltpu.SemaphoreType.DMA((3,)),
        ],
        (1, 2, 3),
    )(me, far(trans), far(upper), far(pairs))
    part, call, pay, curv, lift3 = rows_up(
        slot_frame, leaf_sizes, vectors, leaf_basis, trans, near_field, upper
    )
    core_got = swap(pay, 0)
    y_got = exchange(lift3, (0, 1, 2))
    (pair2,) = small(after_core_kernel, [(2, HALF, R)], "after_core", 10**8)(me, pay, core_got, a1)
    pair_got = swap(pair2, 1)
    top_send, c3 = small(after_y_kernel, [(16 * QUART, R), (QUART, R)], "after_y", 10**8)(
        me, y_got, a2, pair2
    )
    top_got = exchange(top_send, (3, 4, 5, 6))
    (c2,) = small(after_pair_kernel, [(HALF, R)], "after_pair", 10**6)(pair2, pair_got)
    quad_got = swap(c2, 2)
    field, curv = fields(me, call, coup, pay, core_got, pair2, pair_got, c2, m0, m1, curv)
    (field1,) = small(pair_field_kernel, [(HALF, R)], "pair_field", 10**8)(pair_got, quad_got, m1)
    field1_got = swap(field1, 0)
    (inc3,) = small(
        after_top_kernel, [(8, QUART + 8, R)], "after_top", 10**8, [pltpu.VMEM((V, R), F32)]
    )(me, top_got, m3, side2, c2, quad_got, c3, curv)
    inc3_got = exchange(inc3, (0, 1, 2))
    local, tmat = paths(field, trans, field1)
    (share,) = small(part_share_kernel, [(16, 8, R)], "part_share", 10**5)(inc3_got)
    share = exchange(share, (3, 4, 5, 6))
    products = rows_down(
        me, slot_frame, leaf_sizes, leaf_basis, part, local, tmat,
        field1, field1_got, inc3_got, core_got, m0, m1,
    )
    (curvature,) = small(all_share_kernel, [(V,)], "all_share", 10**5)(share)
    return products, curvature


def solution(mesh):
    return jax.shard_map(
        shards,
        mesh=mesh,
        in_specs=(
            P("leaf", None),
            P("leaf"),
            P("leaf", None),
            P("leaf", None, None),
            P("leaf", None, None),
            P("leaf", None, None, None),
            P("leaf", None, None, None),
            P("leaf", None, None, None),
            P("leaf", None, None, None),
        ),
        out_specs=(P("leaf", None), P()),
        check_vma=False,
    )
```
